128 devices in a mesh: face: 4 (over z_hi, core), tile: 32 (over x, y, z_lo).
Axes of the slice: x: 4, y: 4, z: 4 (z_hi: 2, z_lo: 2; z = z_hi * 2 + z_lo), core: 2. Of those that a mesh axis runs over, the one named last changes fastest.
Arguments:
- predicted_field: bfloat16 [16, 8192, 128], P(None, ('face', 'tile')), may hold values from -6 to 6
- parent_band_holder: int32 [8192, 2], P(('face', 'tile')), may hold values from 0 to 127, all different within a row; in each aligned block of 64 rows (0 to 63, 64 to 127, ...) at most 2 rows name the same one
- parent_band_slot: int32 [8192, 2], P(('face', 'tile')), may hold values from 0 to 63
- neighbour_positions: int32 [4, 8192, 128], P(None, ('face', 'tile')), may hold values from 0 to 255
- unscaled_neighbour_factor: float32 [4, 8192, 128], P(None, ('face', 'tile')), may hold values from 0.05 to 1
- truth_field: float32 [1024, 1024], P('tile', 'face'), may hold values from -6 to 6
Outputs:
- predicted_field_slope: float32 [16, 8192, 128], P(None, ('face', 'tile'))
The draws below stay inside these ranges and needn't reach their ends.
Inputs may be any that keep to these rules, and one draw needn't show every extreme that they name: `parent_band_holder`: the two entries of a row differ. Within the 64 rows of one device no device is named more than 2 times, and some device is named exactly 2 times.
All inputs are finite; a program needn't handle non-finite values.
Results may differ from the reference program's by a relative error of at most 0.0003.
Values may be sent and summed in bfloat16 or wider, within the bound.
No kernel may reach another device: no remote copies, remote signals or barrier semaphores. Data moves between devices by JAX's collectives and lax.ppermute only.
A program may use at most 128 MiB of HBM per device.

```python
import math
import jax
import jax.numpy as jnp
import numpy as np
from jax import lax

PARTICIPANT_NUM = 16
PIXELS_PER_BAND = 128
BLK_DEV = 64
RANGE = 8
J = 4
SLOT = 2
LAT_DEV = 32
BAND_COUNT_ALL = 8192
NLAT = 1024
NLON = 1024
N_FACE = 4
N_TILE = 32


def touch_ends(result, own_key, low, largest):
    longest = result.shape.index(max(result.shape))
    spots = []
    for shift in (0, 1):
        where = [jax.random.randint(jax.random.fold_in(own_key, axis), (), 0, length) for axis, length in enumerate(result.shape)]
        where[longest] = (where[longest] + shift) % result.shape[longest]
        spots.append(tuple(where))
    return result.at[spots[0]].set(low).at[spots[1]].set(largest)


def steps_of(stream_key, dims, pieces, low, top_value):
    def one(axis_at, blocks):
        steps = jax.random.uniform(jax.random.fold_in(jax.random.fold_in(stream_key, 6), axis_at), (blocks,), jnp.float32, low / len(pieces), top_value / len(pieces))
        return jnp.repeat(jnp.exp(steps), dims[axis_at] // blocks).reshape((-1,) + (1,) * (len(dims) - axis_at - 1))

    loudness = one(*pieces[0])
    for cut in pieces[1:]:
        loudness = loudness * one(*cut)
    return loudness


def assign_block(own_key, own, number, rows, number_of, top, limit, slope):
    order = jax.random.permutation(own_key, number_of)
    heavy_load, ordinary = shares(number_of, rows * top, limit, slope, True), shares(number_of, rows * top, limit, slope, False)
    places = jnp.arange(number_of)

    def named(sizes, rotation):
        used = int((sizes > 0).sum())
        fixed = max(1, used // 4)
        passed = fixed + (places - fixed + rotation * (used - fixed)) % max(1, number_of - fixed)
        return jnp.zeros((number_of,), jnp.int32).at[order[jnp.where(places < fixed, places, passed)]].set(jnp.asarray(sizes, jnp.int32))

    sizes = jnp.where(number % 4 == 0, named(heavy_load, number // 4), named(ordinary, number - number // 4 - 1))
    mixed = jax.random.permutation(jax.random.fold_in(own, 3), number_of)
    giver, taker = mixed[0:number_of // 2 * 2:2], mixed[1:number_of // 2 * 2:2]
    room = jnp.minimum(sizes[giver] - 1, limit - sizes[taker]) // 2
    room = jnp.where((giver == order[0]) | (taker == order[0]) | (sizes[taker] == 0), 0, jnp.maximum(room, 0))
    passed = jax.random.randint(jax.random.fold_in(own, 4), (number_of // 2,), 0, 1 << 20) % (room + 1)
    sizes = sizes.at[giver].add(-passed).at[taker].add(passed)
    members = jnp.searchsorted(jnp.cumsum(sizes), jnp.arange(rows * top), side="right").astype(jnp.int32)
    table = members.reshape(top, rows).T
    table = table[jax.random.permutation(jax.random.fold_in(own, 1), rows)]
    rotation = jax.random.randint(jax.random.fold_in(own, 2), (rows, 1), 0, top)
    return jnp.take_along_axis(table, (jnp.arange(top)[None, :] + rotation) % top, axis=1)


def shares(amount, total, limit, slope, full):
    portions = [(1 << 20) // math.isqrt(rank ** slope) + 1 for rank in range(1, amount + 1)]
    largest = limit if full else min(limit, max(-(-total // amount), total * portions[0] // sum(portions)))
    least = 1 if total - largest >= amount - 1 else 0
    counts, spare = [largest] + [least] * (amount - 1), total - largest - least * (amount - 1)
    while spare > 0:
        movable = [i for i in range(1, amount) if counts[i] < largest] or [i for i in range(1, amount) if counts[i] < limit]
        pool, budget = sum([portions[i] for i in movable]), spare
        for i in movable:
            extra = min(limit - counts[i], max(1, budget * portions[i] // pool), spare)
            counts[i] = counts[i] + extra
            spare = spare - extra
    return np.array(counts)


def normal_values(stream_key, extent, width, limit, split=(), held_as=jnp.bfloat16):
    values = width * jax.random.normal(stream_key, extent, jnp.float32)
    if split:
        values = values * steps_of(stream_key, extent, split, -0.22, 0.18)
    return jnp.clip(values, -limit, limit).astype(held_as)


def setup_inputs(seed: int = 0) -> dict:
    seeds = jax.random.split(jax.random.key(seed), 7)
    predicted_field = normal_values(seeds[0], (PARTICIPANT_NUM, BAND_COUNT_ALL, PIXELS_PER_BAND), 1.0, 6.0, ((1, 128),))
    parent_band_holder_keys = jax.random.split(jax.random.fold_in(seeds[1], 1), BAND_COUNT_ALL // BLK_DEV)
    parent_band_holder_turns = jax.random.permutation(jax.random.fold_in(seeds[1], 3), BAND_COUNT_ALL // BLK_DEV)
    parent_band_holder = jax.vmap(lambda own, number: assign_block(jax.random.fold_in(seeds[1], 2), own, number, BLK_DEV, N_FACE * N_TILE, 2, SLOT, 1))(parent_band_holder_keys, parent_band_holder_turns).reshape((BAND_COUNT_ALL, 2))
    parent_band_slot = touch_ends(jax.random.randint(seeds[2], (BAND_COUNT_ALL, 2), 0, BLK_DEV), jax.random.fold_in(seeds[2], 1), 0, BLK_DEV - 1).astype(jnp.int32)
    neighbour_positions = touch_ends(jax.random.randint(seeds[3], (J, BAND_COUNT_ALL, PIXELS_PER_BAND), 0, 2 * PIXELS_PER_BAND), jax.random.fold_in(seeds[3], 1), 0, (2 * PIXELS_PER_BAND) - 1).astype(jnp.int32)
    unscaled_neighbour_factor = jnp.clip(0.05 + 0.95 * jax.random.uniform(seeds[4], (J, BAND_COUNT_ALL, PIXELS_PER_BAND), jnp.float32) ** steps_of(seeds[4], (J, BAND_COUNT_ALL, PIXELS_PER_BAND), ((1, 128),), -0.2, 0.2), 0.05, 1.0)
    truth_field = normal_values(seeds[5], (NLAT, NLON), 1.0, 6.0, ((0, 32), (1, 4)), jnp.float32)
    return dict(predicted_field=predicted_field, parent_band_holder=parent_band_holder, parent_band_slot=parent_band_slot, neighbour_positions=neighbour_positions, unscaled_neighbour_factor=unscaled_neighbour_factor, truth_field=truth_field)


FLOOR = 0.01

def pair_push(first, second, weight, participant_count):
    diff = first[:participant_count] - second[:participant_count]
    square_sum = diff * diff + FLOOR
    inverse_power = square_sum ** (-0.75)
    spread = lax.optimization_barrier(jnp.mean(square_sum * inverse_power, axis=0))
    observed = first[participant_count] - second[participant_count]
    mismatch = (observed * observed + FLOOR) ** 0.25 - spread
    return weight / participant_count * mismatch * diff * inverse_power

def gather_weighted(values, neighbour_positions, norm_weight):
    participant_count = values.shape[0]
    band_ids = jnp.arange(values.shape[1], dtype=jnp.int32)[:, None]
    summed = jnp.zeros((participant_count,) + neighbour_positions.shape[1:], jnp.float32)
    for point in range(neighbour_positions.shape[0]):
        picked = values[:, band_ids, neighbour_positions[point]]
        summed = summed + picked.astype(jnp.float32) * norm_weight[point][None]
    return summed

def reference(predicted_field, parent_band_holder, parent_band_slot, neighbour_positions, unscaled_neighbour_factor, truth_field):
    participant_count = predicted_field.shape[0]
    parent_band = (parent_band_holder * BLK_DEV + parent_band_slot).reshape(-1).astype(jnp.int32)
    incoming_bands = jnp.take(predicted_field, parent_band, axis=1).reshape(participant_count, BAND_COUNT_ALL, 2 * PIXELS_PER_BAND)
    norm_weight = unscaled_neighbour_factor / lax.optimization_barrier(jnp.sum(unscaled_neighbour_factor, axis=0, keepdims=True))
    regridded = gather_weighted(incoming_bands, neighbour_positions, norm_weight)
    field = regridded.reshape(participant_count, N_FACE, N_TILE, LAT_DEV, 2 * PIXELS_PER_BAND)
    field = field.transpose(0, 2, 3, 1, 4).reshape(participant_count, NLAT, NLON)
    stacked = jnp.concatenate([field, truth_field[None]], axis=0)
    gradient = jnp.zeros((participant_count, NLAT, NLON), jnp.float32)
    for offset in range(1, RANGE + 1):
        pushed = pair_push(stacked[:, :-offset], stacked[:, offset:], 1.0 / offset, participant_count)
        zero_rows = jnp.zeros((participant_count, offset, NLON), jnp.float32)
        gradient = gradient - jnp.concatenate([pushed, zero_rows], axis=1)
        gradient = gradient + jnp.concatenate([zero_rows, pushed], axis=1)
    for offset in range(1, RANGE + 1):
        pushed = pair_push(stacked, jnp.roll(stacked, -offset, axis=2), 1.0 / offset, participant_count)
        gradient = gradient - pushed + jnp.roll(pushed, offset, axis=2)
    grad_blocks = gradient.reshape(participant_count, N_TILE, LAT_DEV, N_FACE, 2 * PIXELS_PER_BAND)
    grad_blocks = grad_blocks.transpose(0, 3, 1, 2, 4).reshape(participant_count, BAND_COUNT_ALL, PIXELS_PER_BAND)
    unused, pullback = jax.vjp(lambda values: gather_weighted(values, neighbour_positions, norm_weight), jnp.zeros((participant_count, BAND_COUNT_ALL, 2 * PIXELS_PER_BAND), jnp.float32))
    incoming_slope_parts = pullback(grad_blocks)[0].reshape(participant_count, 2 * BAND_COUNT_ALL, PIXELS_PER_BAND)
    predicted_field_slope = jnp.zeros((participant_count, BAND_COUNT_ALL, PIXELS_PER_BAND), jnp.float32).at[:, parent_band].add(incoming_slope_parts)
    return predicted_field_slope
```

```python
import jax
import jax.numpy as jnp
from jax import lax
from jax.experimental import pallas as pl
from jax.experimental.pallas import tpu as pltpu
from jax.sharding import PartitionSpec as P

RANGE = 8
FLOOR = 0.01
M = 16
BANDS = 64
LANES = 128
ROWS = 32
EXT = ROWS + 2 * RANGE
DEVICES = 128
POINTS = 4
F32 = jnp.float32
I32 = jnp.int32
BF16 = jnp.bfloat16
AXES = ("face", "tile")


def struct(shape, dtype=F32):
    return jax.ShapeDtypeStruct(shape, dtype)


def lane_ids(rows=8):
    return lax.broadcasted_iota(I32, (rows, LANES), 1)


def row_ids(rows=8):
    return lax.broadcasted_iota(I32, (rows, LANES), 0)


def request_kernel(holder_ref, slot_ref, wanted_ref, place_ref):
    owner = lane_ids(BANDS).astype(F32)
    band = row_ids(BANDS)
    big = float(1 << 20)
    hots, codes = [], []
    for k in range(2):
        holder = holder_ref[:, k : k + 1].astype(F32)
        slot = slot_ref[:, k : k + 1]
        hots.append(jnp.broadcast_to(holder, (BANDS, LANES)) == owner)
        codes.append(((band + k * BANDS) * BANDS + slot).astype(F32))
    low = [jnp.min(jnp.where(h, c, big), axis=0, keepdims=True) for h, c in zip(hots, codes)]
    high = [jnp.max(jnp.where(h, c, -1.0), axis=0, keepdims=True) for h, c in zip(hots, codes)]
    first = jnp.minimum(low[0], low[1])
    last = jnp.maximum(high[0], high[1])
    named, twice = last >= 0.0, last > first
    slots = [
        jnp.where(named, (first.astype(I32) & (BANDS - 1)).astype(F32), 0.0),
        jnp.where(twice, (last.astype(I32) & (BANDS - 1)).astype(F32), 0.0),
    ]
    rows = row_ids(LANES)
    table = jnp.where(rows == 0, slots[0], jnp.where(rows == 1, slots[1], 0.0))
    wanted_ref[...] = jnp.transpose(table).astype(I32)
    lanes = lane_ids(BANDS)
    columns = jnp.zeros((BANDS, LANES), F32)
    for k in range(2):
        spot = 2.0 * owner + jnp.where(codes[k] == first, 0.0, 1.0)
        spot = jnp.sum(jnp.where(hots[k], spot, 0.0), axis=1, keepdims=True)
        columns = jnp.where(lanes == k, spot, columns)
    columns = jnp.concatenate([columns, jnp.zeros((LANES - BANDS, LANES), F32)], axis=0)
    place_ref[...] = jnp.transpose(columns)[:8].astype(I32)


def request(holder, slot):
    return pl.pallas_call(
        request_kernel,
        out_shape=(struct((DEVICES, LANES), I32), struct((8, LANES), I32)),
        name="request",
    )(holder, slot)


def pack_kernel(asked_ref, bands_ref, out_ref, slots_ref, smem, sem):
    table = jnp.transpose(asked_ref[...].astype(F32))[:8].astype(I32)
    slots_ref[...] = table
    copy = pltpu.make_async_copy(slots_ref, smem, sem)
    copy.start()
    copy.wait()

    def step(i, carry):
        for r in range(2):
            out_ref[2 * i + r] = bands_ref[smem[r, i]]
        return carry

    lax.fori_loop(0, DEVICES, step, 0, unroll=8)


def pack(asked, bands):
    return pl.pallas_call(
        pack_kernel,
        out_shape=(struct((2 * DEVICES, M, LANES), BF16), struct((8, LANES), I32)),
        scratch_shapes=[pltpu.SMEM((8, LANES), I32), pltpu.SemaphoreType.DMA],
        name="pack",
    )(asked, bands)


def regrid_kernel(
    place_ref, recv_ref, pos_ref, factor_ref, truth_ref,
    field_ref, posn_ref, weight_ref, north_ref, south_ref, west_ref, east_ref,
    low_ref, high_ref,
):
    def spread(row, carry):
        for half in range(2):
            for k, tab in enumerate((low_ref, high_ref)):
                strip = recv_ref[place_ref[k, 2 * row + half]].astype(F32)
                tab[pl.ds(half * ROWS + row, M, stride=BANDS), :] = strip
        return carry

    lax.fori_loop(0, ROWS, spread, 0, unroll=4)

    for half in range(2):
        factors = [factor_ref[pl.ds(j * BANDS + half, ROWS, stride=2), :] for j in range(POINTS)]
        total = factors[0] + factors[1] + factors[2] + factors[3]
        for j in range(POINTS):
            spot = j * BANDS + half * ROWS
            posn_ref[pl.ds(spot, ROWS), :] = pos_ref[pl.ds(j * BANDS + half, ROWS, stride=2), :]
            weight_ref[pl.ds(spot, ROWS), :] = factors[j] / total

    def regrid(block, carry):
        row = pl.multiple_of(block * 8, 8)
        posn = [posn_ref[pl.ds(j * BANDS + row, 8), :] for j in range(POINTS)]
        weight = [weight_ref[pl.ds(j * BANDS + row, 8), :] for j in range(POINTS)]
        lane = [p & (LANES - 1) for p in posn]
        upper = [p >= LANES for p in posn]
        for m in range(M):
            low = low_ref[pl.ds(m * BANDS + row, 8), :]
            high = high_ref[pl.ds(m * BANDS + row, 8), :]
            out = jnp.zeros((8, LANES), F32)
            for j in range(POINTS):
                a = jnp.take_along_axis(low, lane[j], axis=1, mode="promise_in_bounds")
                b = jnp.take_along_axis(high, lane[j], axis=1, mode="promise_in_bounds")
                out = out + weight[j] * jnp.where(upper[j], b, a)
            field_ref[pl.ds(m * BANDS + row, 8), :] = out
        return carry

    lax.fori_loop(0, BANDS // 8, regrid, 0)

    for half in range(2):
        field_ref[pl.ds(M * BANDS + half * ROWS, ROWS), :] = truth_ref[:, half * LANES : (half + 1) * LANES]
    for m in range(M + 1):
        for half in range(2):
            spot = m * BANDS + half * ROWS
            north_ref[pl.ds((2 * m + half) * 8, 8), :] = field_ref[pl.ds(spot, 8), :]
            south_ref[pl.ds((2 * m + half) * 8, 8), :] = field_ref[pl.ds(spot + ROWS - 8, 8), :]
    lanes = lane_ids()
    for rb in range(ROWS // 8):
        west = jnp.zeros((8, LANES), F32)
        east = jnp.zeros((8, LANES), F32)
        for m in range(M):
            mine = (lanes >> 3) == m
            left = field_ref[pl.ds(m * BANDS + rb * 8, 8), :]
            right = field_ref[pl.ds(m * BANDS + ROWS + rb * 8, 8), :]
            west = jnp.where(mine, pltpu.roll(left, (8 * m) % LANES, 1), west)
            east = jnp.where(mine, pltpu.roll(right, (8 * m + 8) % LANES, 1), east)
        west_ref[pl.ds(rb * 8, 8), :] = west
        east_ref[pl.ds(rb * 8, 8), :] = east
    west_ref[pl.ds(ROWS, ROWS), :] = truth_ref[:, :LANES]
    east_ref[pl.ds(ROWS, ROWS), :] = truth_ref[:, LANES:]


VMEM = pl.BlockSpec(memory_space=pltpu.VMEM)
SMEM = pl.BlockSpec(memory_space=pltpu.SMEM)


def regrid(place, recv, pos, factor, truth):
    tall = struct(((M + 1) * 2 * RANGE, LANES))
    wide = struct((2 * ROWS, LANES))
    return pl.pallas_call(
        regrid_kernel,
        in_specs=[SMEM, VMEM, VMEM, VMEM, VMEM],
        out_shape=(
            struct(((M + 1) * BANDS, LANES)),
            struct((POINTS * BANDS, LANES), I32),
            struct((POINTS * BANDS, LANES)),
            tall, tall, wide, wide,
        ),
        scratch_shapes=[pltpu.VMEM((M * BANDS, LANES), F32)] * 2,
        name="regrid",
    )(place, recv, pos, factor, truth)


def fall(square_sum):
    root = lax.rsqrt(square_sum)
    return root * (root * lax.rsqrt(root))


def spread_of(diff):
    square_sum = diff * diff + FLOOR
    return square_sum * fall(square_sum)


def push_kernel(
    place_ref, tile_ref, field_ref, posn_ref, weight_ref, top_ref, bottom_ref, left_ref, right_ref,
    out_ref, ext, grad, ring,
):
    for mh in range(2 * (M + 1)):
        ext[pl.ds(mh * EXT, 8), :] = top_ref[pl.ds(mh * 8, 8), :]
        ext[pl.ds(mh * EXT + 8, ROWS), :] = field_ref[pl.ds(mh * ROWS, ROWS), :]
        ext[pl.ds(mh * EXT + 8 + ROWS, 8), :] = bottom_ref[pl.ds(mh * 8, 8), :]
    grad[...] = jnp.zeros_like(grad)
    first_row = tile_ref[0] * ROWS - RANGE

    def latitude(step, carry):
        half = step // 5
        block = step % 5
        base = pl.multiple_of(half * EXT + block * 8, 8)
        rows = row_ids() + (first_row + block * 8)
        firsts = [ext[pl.ds(base + m * 2 * EXT, 8), :] for m in range(M + 1)]
        for k in range(1, RANGE + 1):
            total = jnp.zeros((8, LANES), F32)
            slopes = []
            for m in range(M):
                diff = firsts[m] - ext[pl.ds(base + m * 2 * EXT + k, 8), :]
                square_sum = diff * diff + FLOOR
                power = fall(square_sum)
                total = total + square_sum * power
                slopes.append(diff * power)
            seen = spread_of(firsts[M] - ext[pl.ds(base + M * 2 * EXT + k, 8), :])
            inside = (rows >= 0) & (rows + k < ROWS * 32)
            push = jnp.where(inside, (1.0 / (k * M)) * (seen - total * (1.0 / M)), 0.0)
            for m in range(M):
                pushed = push * slopes[m]
                here = base + m * 2 * EXT
                grad[pl.ds(here, 8), :] -= pushed
                grad[pl.ds(here + k, 8), :] += pushed
        return carry

    lax.fori_loop(0, 10, latitude, 0)

    lanes = lane_ids()

    def longitude(rb, carry):
        row = pl.multiple_of(rb * 8, 8)
        left = left_ref[pl.ds(row, 8), :]
        right = right_ref[pl.ds(row, 8), :]
        for m in range(M + 1):
            spot = m * 2 * EXT + 8 + row
            ring[m * 3] = ext[pl.ds(spot, 8), :]
            ring[m * 3 + 1] = ext[pl.ds(spot + EXT, 8), :]
            if m < M:
                after = pltpu.roll(right, (LANES - 8 * m) % LANES, 1)
                before = pltpu.roll(left, (LANES - 8 - 8 * m) % LANES, 1)
            else:
                after = right_ref[pl.ds(ROWS + row, 8), :]
                before = left_ref[pl.ds(ROWS + row, 8), :]
            ring[m * 3 + 2] = jnp.where(lanes < RANGE, after, jnp.where(lanes >= LANES - RANGE, before, 0.0))

        for k in range(1, RANGE + 1):
            def pair_diff(m):
                here = [ring[m * 3 + v] for v in range(3)]
                moved = [pltpu.roll(x, LANES - k, 1) for x in here]
                return [
                    here[v] - jnp.where(lanes < LANES - k, moved[v], moved[(v + 1) % 3])
                    for v in range(3)
                ]

            totals = [jnp.zeros((8, LANES), F32)] * 3
            slopes = []
            for m in range(M):
                diffs = pair_diff(m)
                row_slopes = []
                for v in range(3):
                    square_sum = diffs[v] * diffs[v] + FLOOR
                    power = fall(square_sum)
                    totals[v] = totals[v] + square_sum * power
                    row_slopes.append(diffs[v] * power)
                slopes.append(row_slopes)
            seen = [spread_of(d) for d in pair_diff(M)]
            push = [(1.0 / (k * M)) * (seen[v] - totals[v] * (1.0 / M)) for v in range(3)]
            for m in range(M):
                pushed = [push[v] * slopes[m][v] for v in range(3)]
                moved = [pltpu.roll(x, k, 1) for x in pushed]
                for v in range(2):
                    spot = m * 2 * EXT + 8 + row + v * EXT
                    grad[pl.ds(spot, 8), :] += jnp.where(lanes >= k, moved[v], moved[(v + 2) % 3]) - pushed[v]
        return carry

    lax.fori_loop(0, ROWS // 8, longitude, 0)

    def clear(i, carry):
        out_ref[i] = jnp.zeros((M, LANES), F32)
        return carry

    lax.fori_loop(0, 2 * DEVICES, clear, 0, unroll=8)

    cells = row_ids(2 * LANES)

    def adjoint(row, carry):
        for half in range(2):
            tile = grad[pl.ds(half * EXT + 8 + row, M, stride=2 * EXT), :]
            parts, hots = [], []
            for j in range(POINTS):
                spot = j * BANDS + half * ROWS + row
                parts.append(tile * weight_ref[pl.ds(spot, 1), :])
                hots.append(jnp.where(cells == posn_ref[pl.ds(spot, 1), :], 1.0, 0.0).astype(BF16))
            part = jnp.concatenate(parts, axis=1)
            high = part.astype(BF16)
            low = (part - high.astype(F32)).astype(BF16)
            both = lax.dot_general(
                jnp.concatenate([high, low], axis=0),
                jnp.concatenate(hots, axis=1),
                (((1,), (1,)), ((), ())),
                preferred_element_type=F32,
            )
            both = both[:M] + both[M:]
            for k in range(2):
                out_ref[place_ref[k, 2 * row + half]] = both[:, k * LANES : (k + 1) * LANES]
        return carry

    lax.fori_loop(0, ROWS, adjoint, 0)


def push(place, tile, field, posn, weight, top, bottom, left, right):
    return pl.pallas_call(
        push_kernel,
        in_specs=[SMEM, SMEM] + [VMEM] * 7,
        out_shape=struct((2 * DEVICES, M, LANES)),
        scratch_shapes=[
            pltpu.VMEM((2 * (M + 1) * EXT, LANES), F32),
            pltpu.VMEM((2 * M * EXT, LANES), F32),
            pltpu.VMEM((3 * (M + 1), 8, LANES), F32),
        ],
        name="push",
    )(place, tile, field, posn, weight, top, bottom, left, right)


def collect_kernel(slots_ref, back_ref, out_ref):
    out_ref[...] = jnp.zeros_like(out_ref)

    def step(i, carry):
        for r in range(2):
            where = pl.ds(slots_ref[r, i], M, stride=BANDS)
            out_ref[where, :] += back_ref[2 * i + r]
        return carry

    lax.fori_loop(0, DEVICES, step, 0, unroll=4)


def collect(slots, back):
    return pl.pallas_call(
        collect_kernel,
        in_specs=[SMEM, VMEM],
        out_shape=struct((M * BANDS, LANES)),
        name="collect",
    )(slots, back)


def exchange(x):
    return lax.all_to_all(x, AXES, split_axis=0, concat_axis=0, tiled=True)


def local(predicted_field, parent_band_holder, parent_band_slot, neighbour_positions, unscaled_neighbour_factor, truth_field):
    tiles, faces = lax.axis_size("tile"), lax.axis_size("face")
    bands = jnp.transpose(predicted_field, (1, 0, 2))
    wanted, place = request(parent_band_holder, parent_band_slot)
    asked = exchange(wanted)
    outgoing, slots = pack(asked, bands)
    recv = exchange(outgoing.reshape(DEVICES, 2, M, LANES)).reshape(2 * DEVICES, M, LANES)
    field, posn, weight, north, south, west, east = regrid(
        place,
        recv,
        neighbour_positions.reshape(POINTS * BANDS, LANES),
        unscaled_neighbour_factor.reshape(POINTS * BANDS, LANES),
        truth_field,
    )
    up = [(i + 1, i) for i in range(tiles - 1)]
    down = [(i, i + 1) for i in range(tiles - 1)]
    bottom = lax.ppermute(north, "tile", up)
    top = lax.ppermute(south, "tile", down)
    right = lax.ppermute(west, "face", [((i + 1) % faces, i) for i in range(faces)])
    left = lax.ppermute(east, "face", [(i, (i + 1) % faces) for i in range(faces)])
    tile = lax.axis_index("tile").astype(I32).reshape(1)
    back = push(place, tile, field, posn, weight, top, bottom, left, right)
    back = exchange(back.reshape(DEVICES, 2, M, LANES)).reshape(2 * DEVICES, M, LANES)
    return collect(slots, back).reshape(M, BANDS, LANES)


def solution(mesh):
    in_specs = (
        P(None, AXES, None),
        P(AXES, None),
        P(AXES, None),
        P(None, AXES, None),
        P(None, AXES, None),
        P("tile", "face"),
    )
    return jax.shard_map(local, mesh=mesh, in_specs=in_specs, out_specs=P(None, AXES, None), check_vma=False)
```

```python
import jax
import jax.numpy as jnp
from jax import lax
from jax.experimental import pallas as pl
from jax.experimental.pallas import tpu as pltpu
from jax.sharding import PartitionSpec as P

RANGE = 8
FLOOR = 0.01
M = 16
BANDS = 64
LANES = 128
ROWS = 32
EXT = ROWS + 2 * RANGE
DEVICES = 128
POINTS = 4
QUADS = M // 4
TURN = 2 * LANES + 2 * RANGE
MESSAGE = M + 1
TOP = 32700.0
F32 = jnp.float32
I32 = jnp.int32
BF16 = jnp.bfloat16
AXES = ("face", "tile")


def struct(shape, dtype=F32):
    return jax.ShapeDtypeStruct(shape, dtype)


def lane_ids(rows=8):
    return lax.broadcasted_iota(I32, (rows, LANES), 1)


def row_ids(rows=8):
    return lax.broadcasted_iota(I32, (rows, LANES), 0)


def request_kernel(holder_ref, slot_ref, wanted_ref, place_ref):
    owner = lax.broadcasted_iota(I32, (DEVICES, BANDS), 0).astype(F32)
    band = lax.broadcasted_iota(I32, (1, BANDS), 1)
    big = float(1 << 20)
    hots, codes = [], []
    for k in range(2):
        holder = holder_ref[k : k + 1, :].astype(F32)
        code = (band + k * BANDS) * BANDS + slot_ref[k : k + 1, :]
        hots.append(holder == owner)
        codes.append(jnp.broadcast_to(code.astype(F32), (DEVICES, BANDS)))
    low = [jnp.min(jnp.where(h, c, big), axis=1, keepdims=True) for h, c in zip(hots, codes)]
    high = [jnp.max(jnp.where(h, c, -1.0), axis=1, keepdims=True) for h, c in zip(hots, codes)]
    first = jnp.minimum(low[0], low[1])
    last = jnp.maximum(high[0], high[1])
    slots = [
        jnp.where(last >= 0.0, first.astype(I32) & (BANDS - 1), 0),
        jnp.where(last > first, last.astype(I32) & (BANDS - 1), 0),
    ]
    lanes = lane_ids(DEVICES)
    wanted_ref[...] = jnp.where(lanes == 0, slots[0], jnp.where(lanes == 1, slots[1], 0))
    place_ref[...] = jnp.zeros((8, LANES), I32)
    for k in range(2):
        spot = 2.0 * owner + jnp.where(codes[k] == first, 0.0, 1.0)
        spot = jnp.sum(jnp.where(hots[k], spot, 0.0), axis=0, keepdims=True)
        place_ref[k : k + 1, :BANDS] = spot.astype(I32)


def request(holder, slot):
    return pl.pallas_call(
        request_kernel,
        out_shape=(struct((DEVICES, LANES), I32), struct((8, LANES), I32)),
        name="request",
    )(holder, slot)


def pack_kernel(asked_ref, bands_ref, out_ref, slots_ref, smem, sem):
    table = jnp.transpose(asked_ref[...].astype(F32))[:8].astype(I32)
    slots_ref[...] = table
    copy = pltpu.make_async_copy(slots_ref, smem, sem)
    copy.start()
    copy.wait()

    def step(i, carry):
        for r in range(2):
            out_ref[2 * i + r] = bands_ref[smem[r, i]]
        return carry

    lax.fori_loop(0, DEVICES, step, 0, unroll=8)


def pack(asked, bands):
    return pl.pallas_call(
        pack_kernel,
        out_shape=(struct((2 * DEVICES, M, LANES), BF16), struct((8, LANES), I32)),
        scratch_shapes=[pltpu.SMEM((8, LANES), I32), pltpu.SemaphoreType.DMA],
        name="pack",
    )(asked, bands)


def regrid_kernel(
    place_ref, recv_ref, pos_ref, factor_ref, truth_ref,
    field_ref, turned_ref, posn_ref, weight_ref, north_ref, south_ref, west_ref, east_ref,
    low_ref, high_ref,
):
    def spread(row, carry):
        for half in range(2):
            for k, tab in enumerate((low_ref, high_ref)):
                strip = recv_ref[place_ref[k, 2 * row + half]].astype(F32)
                tab[pl.ds(half * ROWS + row, M, stride=BANDS), :] = strip
        return carry

    lax.fori_loop(0, ROWS, spread, 0, unroll=4)

    for half in range(2):
        factors = [factor_ref[pl.ds(j * BANDS + half, ROWS, stride=2), :] for j in range(POINTS)]
        total = factors[0] + factors[1] + factors[2] + factors[3]
        for j in range(POINTS):
            spot = j * BANDS + half * ROWS
            posn_ref[pl.ds(spot, ROWS), :] = pos_ref[pl.ds(j * BANDS + half, ROWS, stride=2), :]
            weight_ref[pl.ds(spot, ROWS), :] = factors[j] / total

    def regrid(block, carry):
        row = pl.multiple_of(block * 8, 8)
        posn = [posn_ref[pl.ds(j * BANDS + row, 8), :] for j in range(POINTS)]
        weight = [weight_ref[pl.ds(j * BANDS + row, 8), :] for j in range(POINTS)]
        lane = [p & (LANES - 1) for p in posn]
        upper = [p >= LANES for p in posn]
        for m in range(M):
            low = low_ref[pl.ds(m * BANDS + row, 8), :]
            high = high_ref[pl.ds(m * BANDS + row, 8), :]
            out = jnp.zeros((8, LANES), F32)
            for j in range(POINTS):
                a = jnp.take_along_axis(low, lane[j], axis=1, mode="promise_in_bounds")
                b = jnp.take_along_axis(high, lane[j], axis=1, mode="promise_in_bounds")
                out = out + weight[j] * jnp.where(upper[j], b, a)
            field_ref[pl.ds(m * BANDS + row, 8), :] = out
        return carry

    lax.fori_loop(0, BANDS // 8, regrid, 0)

    for half in range(2):
        field_ref[pl.ds(M * BANDS + half * ROWS, ROWS), :] = truth_ref[:, half * LANES : (half + 1) * LANES]
    for m in range(M + 1):
        for half in range(2):
            spot = m * BANDS + half * ROWS
            north_ref[pl.ds((2 * m + half) * 8, 8), :] = field_ref[pl.ds(spot, 8), :]
            south_ref[pl.ds((2 * m + half) * 8, 8), :] = field_ref[pl.ds(spot + ROWS - 8, 8), :]
    for q in range(QUADS + 1):
        for half in range(2):
            if q < QUADS:
                parts = [field_ref[pl.ds((4 * q + i) * BANDS + half * ROWS, ROWS), :] for i in range(4)]
            else:
                parts = [truth_ref[:, half * LANES : (half + 1) * LANES]] * 4
            turned = jnp.transpose(jnp.concatenate(parts, axis=0))
            turned_ref[pl.ds(q * 2 * LANES + half * LANES, LANES), :] = turned
            if half == 0:
                west_ref[pl.ds(q * 8, 8), :] = turned[:8]
            else:
                east_ref[pl.ds(q * 8, 8), :] = turned[LANES - 8 :]


VMEM = pl.BlockSpec(memory_space=pltpu.VMEM)
SMEM = pl.BlockSpec(memory_space=pltpu.SMEM)


def regrid(place, recv, pos, factor, truth):
    tall = struct(((M + 1) * 2 * RANGE, LANES))
    wide = struct(((QUADS + 1) * RANGE, LANES))
    return pl.pallas_call(
        regrid_kernel,
        in_specs=[SMEM, VMEM, VMEM, VMEM, VMEM],
        out_shape=(
            struct(((M + 1) * BANDS, LANES)),
            struct(((QUADS + 1) * 2 * LANES, LANES)),
            struct((POINTS * BANDS, LANES), I32),
            struct((POINTS * BANDS, LANES)),
            tall, tall, wide, wide,
        ),
        scratch_shapes=[pltpu.VMEM((M * BANDS, LANES), F32)] * 2,
        name="regrid",
    )(place, recv, pos, factor, truth)


def steep(diff):
    root = lax.rsqrt(diff * diff + FLOOR)
    value = lax.rsqrt(root)
    return value, (diff * root) * (value * root)


def push_kernel(
    place_ref, tile_ref, field_ref, turned_ref, posn_ref, weight_ref, top_ref, bottom_ref, left_ref, right_ref,
    out_ref, ext, grad, side, turn,
):
    for mh in range(2 * (M + 1)):
        ext[pl.ds(mh * EXT, 8), :] = top_ref[pl.ds(mh * 8, 8), :]
        ext[pl.ds(mh * EXT + 8, ROWS), :] = field_ref[pl.ds(mh * ROWS, ROWS), :]
        ext[pl.ds(mh * EXT + 8 + ROWS, 8), :] = bottom_ref[pl.ds(mh * 8, 8), :]
    for q in range(QUADS + 1):
        side[pl.ds(q * TURN, 8), :] = left_ref[pl.ds(q * 8, 8), :]
        side[pl.ds(q * TURN + 8, 2 * LANES), :] = turned_ref[pl.ds(q * 2 * LANES, 2 * LANES), :]
        side[pl.ds(q * TURN + 8 + 2 * LANES, 8), :] = right_ref[pl.ds(q * 8, 8), :]
    grad[...] = jnp.zeros_like(grad)
    turn[...] = jnp.zeros_like(turn)
    out_ref[...] = jnp.zeros_like(out_ref)
    first_row = tile_ref[0] * ROWS - RANGE

    def latitude(step, carry):
        half = step // 5
        block = step % 5
        base = pl.multiple_of(half * EXT + block * 8, 8)
        rows = row_ids() + (first_row + block * 8)
        for k in range(1, RANGE + 1):
            def diff(m):
                here = base + m * 2 * EXT
                return ext[pl.ds(here, 8), :] - ext[pl.ds(here + k, 8), :]

            total = jnp.zeros((8, LANES), F32)
            slopes = []
            for m in range(M):
                value, slope = steep(diff(m))
                total = total + value
                slopes.append(slope)
            seen, unused = steep(diff(M))
            inside = (rows >= 0) & (rows + k < ROWS * 32)
            push = jnp.where(inside, (1.0 / (k * M)) * (seen - total * (1.0 / M)), 0.0)
            for m in range(M):
                pushed = push * slopes[m]
                here = base + m * 2 * EXT
                grad[pl.ds(here, 8), :] -= pushed
                grad[pl.ds(here + k, 8), :] += pushed
        return carry

    lax.fori_loop(0, 10, latitude, 0)

    def longitude(block, carry):
        base = pl.multiple_of(block * 8, 8)
        for k in range(1, RANGE + 1):
            def diff(q):
                here = base + q * TURN
                return side[pl.ds(here, 8), :] - side[pl.ds(here + k, 8), :]

            total = jnp.zeros((8, LANES), F32)
            slopes = []
            for q in range(QUADS):
                value, slope = steep(diff(q))
                total = total + value
                slopes.append(slope)
            total = total + pltpu.roll(total, 2 * ROWS, 1)
            total = total + pltpu.roll(total, ROWS, 1)
            seen, unused = steep(diff(QUADS))
            push = (1.0 / (k * M)) * (seen - total * (1.0 / M))
            for q in range(QUADS):
                pushed = push * slopes[q]
                here = base + q * TURN
                turn[pl.ds(here, 8), :] -= pushed
                turn[pl.ds(here + k, 8), :] += pushed
        return carry

    lax.fori_loop(0, TURN // 8 - 1, longitude, 0)

    for q in range(QUADS):
        for half in range(2):
            back = jnp.transpose(turn[pl.ds(q * TURN + 8 + half * LANES, LANES), :])
            for i in range(4):
                spot = ((4 * q + i) * 2 + half) * EXT + 8
                grad[pl.ds(spot, ROWS), :] += back[i * ROWS : (i + 1) * ROWS]

    cells = [(lax.broadcasted_iota(I32, (16, LANES), 0) + 16 * i).astype(F32).astype(BF16) for i in range(16)]
    one, zero = jnp.ones((16, LANES), BF16), jnp.zeros((16, LANES), BF16)

    def adjoint(row, carry):
        for half in range(2):
            tile = grad[pl.ds(half * EXT + 8 + row, M, stride=2 * EXT), :]
            parts, hots = [], []
            for j in range(POINTS):
                spot = j * BANDS + half * ROWS + row
                parts.append(tile * weight_ref[pl.ds(spot, 1), :])
                posn = jnp.broadcast_to(posn_ref[pl.ds(spot, 1), :].astype(F32), (16, LANES)).astype(BF16)
                hots.append(jnp.concatenate([jnp.where(c == posn, one, zero) for c in cells], axis=0))
            part = jnp.concatenate(parts, axis=1)
            high = part.astype(BF16)
            low = (part - high.astype(F32)).astype(BF16)
            both = lax.dot_general(
                jnp.concatenate([high, low], axis=0),
                jnp.concatenate(hots, axis=1),
                (((1,), (1,)), ((), ())),
                preferred_element_type=F32,
            )
            both = both[:M] + both[M:]
            for k in range(2):
                strip = both[:, k * LANES : (k + 1) * LANES]
                largest = jnp.maximum(jnp.max(jnp.abs(strip), axis=0, keepdims=True), 1e-36)
                scale = jnp.ceil(jnp.log2(largest) * 256.0)
                code = jnp.round(strip * (jnp.exp2(scale * (-1.0 / 256.0)) * TOP)).astype(I32)
                place = place_ref[k, 2 * row + half]
                spot = (place >> 1) * MESSAGE
                shift = (place & 1) * 16
                out_ref[pl.ds(spot, M), :] |= (code & 0xFFFF) << shift
                out_ref[pl.ds(spot + M, 1), :] |= (scale.astype(I32) & 0xFFFF) << shift
        return carry

    lax.fori_loop(0, ROWS, adjoint, 0)


def push(place, tile, field, turned, posn, weight, top, bottom, left, right):
    return pl.pallas_call(
        push_kernel,
        in_specs=[SMEM, SMEM] + [VMEM] * 8,
        out_shape=struct((DEVICES * MESSAGE, LANES), I32),
        scratch_shapes=[
            pltpu.VMEM((2 * (M + 1) * EXT, LANES), F32),
            pltpu.VMEM((2 * M * EXT, LANES), F32),
            pltpu.VMEM(((QUADS + 1) * TURN, LANES), F32),
            pltpu.VMEM((QUADS * TURN, LANES), F32),
        ],
        name="push",
    )(place, tile, field, turned, posn, weight, top, bottom, left, right)


def collect_kernel(slots_ref, back_ref, out_ref, sums):
    sums[...] = jnp.zeros_like(sums)

    def step(i, carry):
        codes = back_ref[pl.ds(i * MESSAGE, M), :]
        scales = back_ref[pl.ds(i * MESSAGE + M, 1), :]
        for r in range(2):
            code, scale = [((x << 16) if r == 0 else x) >> 16 for x in (codes, scales)]
            scale = jnp.exp2(scale.astype(F32) * (1.0 / 256.0)) * (1.0 / TOP)
            sums[slots_ref[r, i]] += code.astype(F32) * scale
        return carry

    lax.fori_loop(0, DEVICES, step, 0, unroll=4)

    def turn(s, carry):
        out_ref[pl.ds(s, M, stride=BANDS), :] = sums[s]
        return carry

    lax.fori_loop(0, BANDS, turn, 0, unroll=8)


def collect(slots, back):
    return pl.pallas_call(
        collect_kernel,
        in_specs=[SMEM, VMEM],
        out_shape=struct((M * BANDS, LANES)),
        scratch_shapes=[pltpu.VMEM((BANDS, M, LANES), F32)],
        name="collect",
    )(slots, back)


def exchange(x):
    return lax.all_to_all(x, AXES, split_axis=0, concat_axis=0, tiled=True)


def local(predicted_field, parent_band_holder, parent_band_slot, neighbour_positions, unscaled_neighbour_factor, truth_field):
    tiles, faces = lax.axis_size("tile"), lax.axis_size("face")
    bands = jnp.transpose(predicted_field, (1, 0, 2))
    wanted, place = request(parent_band_holder.T, parent_band_slot.T)
    asked = exchange(wanted)
    outgoing, slots = pack(asked, bands)
    recv = exchange(outgoing.reshape(DEVICES, 2, M, LANES)).reshape(2 * DEVICES, M, LANES)
    field, turned, posn, weight, north, south, west, east = regrid(
        place,
        recv,
        neighbour_positions.reshape(POINTS * BANDS, LANES),
        unscaled_neighbour_factor.reshape(POINTS * BANDS, LANES),
        truth_field,
    )
    up = [(i + 1, i) for i in range(tiles - 1)]
    down = [(i, i + 1) for i in range(tiles - 1)]
    bottom = lax.ppermute(north, "tile", up)
    top = lax.ppermute(south, "tile", down)
    right = lax.ppermute(west, "face", [((i + 1) % faces, i) for i in range(faces)])
    left = lax.ppermute(east, "face", [(i, (i + 1) % faces) for i in range(faces)])
    tile = lax.axis_index("tile").astype(I32).reshape(1)
    back = push(place, tile, field, turned, posn, weight, top, bottom, left, right)
    back = exchange(back.reshape(DEVICES, MESSAGE, 1, LANES)).reshape(DEVICES * MESSAGE, LANES)
    return collect(slots, back).reshape(M, BANDS, LANES)


def solution(mesh):
    in_specs = (
        P(None, AXES, None),
        P(AXES, None),
        P(AXES, None),
        P(None, AXES, None),
        P(None, AXES, None),
        P("tile", "face"),
    )
    return jax.shard_map(local, mesh=mesh, in_specs=in_specs, out_specs=P(None, AXES, None), check_vma=False)
```

```python
import jax
import jax.numpy as jnp
from jax import lax
from jax.experimental import pallas as pl
from jax.experimental.pallas import tpu as pltpu
from jax.sharding import PartitionSpec as P

RANGE = 8
FLOOR = 0.01
M = 16
BANDS = 64
LANES = 128
ROWS = 32
EXT = ROWS + 2 * RANGE
DEVICES = 128
POINTS = 4
QUADS = M // 4
TURN = 2 * LANES + 2 * RANGE
MESSAGE = M + 1
TOP = 32700.0
F32 = jnp.float32
I32 = jnp.int32
BF16 = jnp.bfloat16
AXES = ("face", "tile")


def struct(shape, dtype=F32):
    return jax.ShapeDtypeStruct(shape, dtype)


def lane_ids(rows=8):
    return lax.broadcasted_iota(I32, (rows, LANES), 1)


def row_ids(rows=8):
    return lax.broadcasted_iota(I32, (rows, LANES), 0)


def request_kernel(holder_ref, slot_ref, wanted_ref, place_ref):
    owner = lax.broadcasted_iota(I32, (DEVICES, BANDS), 0).astype(F32)
    band = lax.broadcasted_iota(I32, (1, BANDS), 1)
    big = float(1 << 20)
    hots, codes = [], []
    for k in range(2):
        holder = holder_ref[k : k + 1, :].astype(F32)
        code = (band + k * BANDS) * BANDS + slot_ref[k : k + 1, :]
        hots.append(holder == owner)
        codes.append(jnp.broadcast_to(code.astype(F32), (DEVICES, BANDS)))
    low = [jnp.min(jnp.where(h, c, big), axis=1, keepdims=True) for h, c in zip(hots, codes)]
    high = [jnp.max(jnp.where(h, c, -1.0), axis=1, keepdims=True) for h, c in zip(hots, codes)]
    first = jnp.minimum(low[0], low[1])
    last = jnp.maximum(high[0], high[1])
    slots = [
        jnp.where(last >= 0.0, first.astype(I32) & (BANDS - 1), 0),
        jnp.where(last > first, last.astype(I32) & (BANDS - 1), 0),
    ]
    lanes = lane_ids(DEVICES)
    wanted_ref[...] = jnp.where(lanes == 0, slots[0], jnp.where(lanes == 1, slots[1], 0))
    place_ref[...] = jnp.zeros((8, LANES), I32)
    for k in range(2):
        spot = 2.0 * owner + jnp.where(codes[k] == first, 0.0, 1.0)
        spot = jnp.sum(jnp.where(hots[k], spot, 0.0), axis=0, keepdims=True)
        place_ref[k : k + 1, :BANDS] = spot.astype(I32)


def request(holder, slot):
    return pl.pallas_call(
        request_kernel,
        out_shape=(struct((DEVICES, LANES), I32), struct((8, LANES), I32)),
        name="request",
        compiler_params=pltpu.CompilerParams(vmem_limit_bytes=1 << 20),
    )(holder, slot)


def pack_kernel(asked_ref, bands_ref, out_ref, slots_ref, smem, sem):
    table = jnp.transpose(asked_ref[...].astype(F32))[:8].astype(I32)
    slots_ref[...] = table
    copy = pltpu.make_async_copy(slots_ref, smem, sem)
    copy.start()
    copy.wait()

    def step(i, carry):
        for r in range(2):
            out_ref[2 * i + r] = bands_ref[smem[r, i]]
        return carry

    lax.fori_loop(0, DEVICES, step, 0, unroll=8)


def pack(asked, bands):
    return pl.pallas_call(
        pack_kernel,
        out_shape=(struct((2 * DEVICES, M, LANES), BF16), struct((8, LANES), I32)),
        scratch_shapes=[pltpu.SMEM((8, LANES), I32), pltpu.SemaphoreType.DMA],
        name="pack",
        compiler_params=pltpu.CompilerParams(vmem_limit_bytes=4 << 20),
    )(asked, bands)


def regrid_kernel(
    place_ref, recv_ref, pos_ref, factor_ref, truth_ref,
    field_ref, turned_ref, posn_ref, weight_ref, north_ref, south_ref, west_ref, east_ref,
    low_ref, high_ref,
):
    def spread(row, carry):
        for half in range(2):
            for k, tab in enumerate((low_ref, high_ref)):
                strip = recv_ref[place_ref[k, 2 * row + half]].astype(F32)
                tab[pl.ds(half * ROWS + row, M, stride=BANDS), :] = strip
        return carry

    lax.fori_loop(0, ROWS, spread, 0, unroll=4)

    for half in range(2):
        factors = [factor_ref[pl.ds(j * BANDS + half, ROWS, stride=2), :] for j in range(POINTS)]
        total = factors[0] + factors[1] + factors[2] + factors[3]
        for j in range(POINTS):
            spot = j * BANDS + half * ROWS
            posn_ref[pl.ds(spot, ROWS), :] = pos_ref[pl.ds(j * BANDS + half, ROWS, stride=2), :]
            weight_ref[pl.ds(spot, ROWS), :] = factors[j] / total

    def regrid(block, carry):
        row = pl.multiple_of(block * 8, 8)
        posn = [posn_ref[pl.ds(j * BANDS + row, 8), :] for j in range(POINTS)]
        weight = [weight_ref[pl.ds(j * BANDS + row, 8), :] for j in range(POINTS)]
        sums = [jnp.zeros((8, LANES), F32)] * M
        for j in range(POINTS):
            lane, upper = posn[j] & (LANES - 1), posn[j] >= LANES
            for m in range(M):
                a, b = [
                    jnp.take_along_axis(tab[pl.ds(m * BANDS + row, 8), :], lane, axis=1, mode="promise_in_bounds")
                    for tab in (low_ref, high_ref)
                ]
                sums[m] = sums[m] + weight[j] * jnp.where(upper, b, a)
        for m in range(M):
            field_ref[pl.ds(m * BANDS + row, 8), :] = sums[m]
        return carry

    lax.fori_loop(0, BANDS // 8, regrid, 0)

    for half in range(2):
        field_ref[pl.ds(M * BANDS + half * ROWS, ROWS), :] = truth_ref[:, half * LANES : (half + 1) * LANES]
    for m in range(M + 1):
        for half in range(2):
            spot = m * BANDS + half * ROWS
            north_ref[pl.ds((2 * m + half) * 8, 8), :] = field_ref[pl.ds(spot, 8), :]
            south_ref[pl.ds((2 * m + half) * 8, 8), :] = field_ref[pl.ds(spot + ROWS - 8, 8), :]
    for q in range(QUADS + 1):
        for half in range(2):
            if q < QUADS:
                parts = [field_ref[pl.ds((4 * q + i) * BANDS + half * ROWS, ROWS), :] for i in range(4)]
            else:
                parts = [truth_ref[:, half * LANES : (half + 1) * LANES]] * 4
            turned = jnp.transpose(jnp.concatenate(parts, axis=0))
            turned_ref[pl.ds(q * 2 * LANES + half * LANES, LANES), :] = turned
            if half == 0:
                west_ref[pl.ds(q * 8, 8), :] = turned[:8]
            else:
                east_ref[pl.ds(q * 8, 8), :] = turned[LANES - 8 :]


VMEM = pl.BlockSpec(memory_space=pltpu.VMEM)
SMEM = pl.BlockSpec(memory_space=pltpu.SMEM)


def regrid(place, recv, pos, factor, truth):
    tall = struct(((M + 1) * 2 * RANGE, LANES))
    wide = struct(((QUADS + 1) * RANGE, LANES))
    return pl.pallas_call(
        regrid_kernel,
        in_specs=[SMEM, VMEM, VMEM, VMEM, VMEM],
        out_shape=(
            struct(((M + 1) * BANDS, LANES)),
            struct(((QUADS + 1) * 2 * LANES, LANES)),
            struct((POINTS * BANDS, LANES), I32),
            struct((POINTS * BANDS, LANES)),
            tall, tall, wide, wide,
        ),
        scratch_shapes=[pltpu.VMEM((M * BANDS, LANES), F32)] * 2,
        name="regrid",
        compiler_params=pltpu.CompilerParams(vmem_limit_bytes=8 << 20),
    )(place, recv, pos, factor, truth)


def steep(diff):
    root = lax.rsqrt(diff * diff + FLOOR)
    value = lax.rsqrt(root)
    return value, (diff * root) * (value * root)


def push_kernel(
    place_ref, tile_ref, field_ref, turned_ref, posn_ref, weight_ref, top_ref, bottom_ref, left_ref, right_ref,
    out_ref, ext, grad, side, turn, kept_rows, kept_columns,
):
    for mh in range(2 * (M + 1)):
        ext[pl.ds(mh * EXT, 8), :] = top_ref[pl.ds(mh * 8, 8), :]
        ext[pl.ds(mh * EXT + 8, ROWS), :] = field_ref[pl.ds(mh * ROWS, ROWS), :]
        ext[pl.ds(mh * EXT + 8 + ROWS, 8), :] = bottom_ref[pl.ds(mh * 8, 8), :]
    for q in range(QUADS + 1):
        side[pl.ds(q * TURN, 8), :] = left_ref[pl.ds(q * 8, 8), :]
        side[pl.ds(q * TURN + 8, 2 * LANES), :] = turned_ref[pl.ds(q * 2 * LANES, 2 * LANES), :]
        side[pl.ds(q * TURN + 8 + 2 * LANES, 8), :] = right_ref[pl.ds(q * 8, 8), :]
    out_ref[...] = jnp.zeros_like(out_ref)
    first_row = tile_ref[0] * ROWS - RANGE

    def ending(kept, spot, pushed, k):
        moved = pltpu.roll(pushed, k % 8, 0)
        earlier = kept[spot]
        kept[spot] = moved
        return jnp.where(row_ids() >= k, moved, earlier)

    def latitude(step, carry):
        half = step // 5
        block = step % 5
        base = pl.multiple_of(half * EXT + block * 8, 8)
        rows = row_ids() + (first_row + block * 8)
        sums = [jnp.zeros((8, LANES), F32)] * M
        for k in range(1, RANGE + 1):
            def diff(m):
                here = base + m * 2 * EXT
                return ext[pl.ds(here, 8), :] - ext[pl.ds(here + k, 8), :]

            total = jnp.zeros((8, LANES), F32)
            slopes = []
            for m in range(M):
                value, slope = steep(diff(m))
                total = total + value
                slopes.append(slope)
            seen, unused = steep(diff(M))
            inside = (rows >= 0) & (rows + k < ROWS * 32)
            push = jnp.where(inside, (1.0 / (k * M)) * (seen - total * (1.0 / M)), 0.0)
            for m in range(M):
                pushed = push * slopes[m]
                sums[m] = sums[m] - pushed + ending(kept_rows, (k - 1) * M + m, pushed, k)
        for m in range(M):
            grad[pl.ds(base + m * 2 * EXT, 8), :] = sums[m]
        return carry

    lax.fori_loop(0, 10, latitude, 0, unroll=2)

    def longitude(block, carry):
        base = pl.multiple_of(block * 8, 8)
        totals, slopes, sights = [], [], []
        for k in range(1, RANGE + 1):
            def diff(q):
                here = base + q * TURN
                return side[pl.ds(here, 8), :] - side[pl.ds(here + k, 8), :]

            pairs = [steep(diff(q)) for q in range(QUADS)]
            slopes.append([p[1] for p in pairs])
            totals.append((pairs[0][0] + pairs[1][0]) + (pairs[2][0] + pairs[3][0]))
            sights.append(steep(diff(QUADS))[0])
        totals = [t + pltpu.roll(t, 2 * ROWS, 1) for t in totals]
        totals = [t + pltpu.roll(t, ROWS, 1) for t in totals]
        sums = [jnp.zeros((8, LANES), F32)] * QUADS
        for k in range(1, RANGE + 1):
            push = (1.0 / (k * M)) * (sights[k - 1] - totals[k - 1] * (1.0 / M))
            for q in range(QUADS):
                pushed = push * slopes[k - 1][q]
                sums[q] = sums[q] - pushed + ending(kept_columns, (k - 1) * QUADS + q, pushed, k)
        for q in range(QUADS):
            turn[pl.ds(base + q * TURN, 8), :] = sums[q]
        return carry

    lax.fori_loop(0, TURN // 8 - 1, longitude, 0, unroll=3)

    for q in range(QUADS):
        for half in range(2):
            back = jnp.transpose(turn[pl.ds(q * TURN + 8 + half * LANES, LANES), :])
            for i in range(4):
                spot = ((4 * q + i) * 2 + half) * EXT + 8
                grad[pl.ds(spot, ROWS), :] += back[i * ROWS : (i + 1) * ROWS]

    cells = [(lax.broadcasted_iota(I32, (16, LANES), 0) + 16 * i).astype(F32).astype(BF16) for i in range(16)]
    one, zero = jnp.ones((16, LANES), BF16), jnp.zeros((16, LANES), BF16)

    def adjoint(row, carry):
        for half in range(2):
            tile = grad[pl.ds(half * EXT + 8 + row, M, stride=2 * EXT), :]
            parts, hots = [], []
            for j in range(POINTS):
                spot = j * BANDS + half * ROWS + row
                parts.append(tile * weight_ref[pl.ds(spot, 1), :])
                posn = jnp.broadcast_to(posn_ref[pl.ds(spot, 1), :].astype(F32), (16, LANES)).astype(BF16)
                hots.append(jnp.concatenate([jnp.where(c == posn, one, zero) for c in cells], axis=0))
            part = jnp.concatenate(parts, axis=1)
            high = part.astype(BF16)
            low = (part - high.astype(F32)).astype(BF16)
            both = lax.dot_general(
                jnp.concatenate([high, low], axis=0),
                jnp.concatenate(hots, axis=1),
                (((1,), (1,)), ((), ())),
                preferred_element_type=F32,
            )
            both = both[:M] + both[M:]
            for k in range(2):
                strip = both[:, k * LANES : (k + 1) * LANES]
                largest = jnp.maximum(jnp.max(jnp.abs(strip), axis=0, keepdims=True), 1e-36)
                scale = jnp.ceil(jnp.log2(largest) * 256.0)
                code = jnp.round(strip * (jnp.exp2(scale * (-1.0 / 256.0)) * TOP)).astype(I32)
                place = place_ref[k, 2 * row + half]
                spot = (place >> 1) * MESSAGE
                shift = (place & 1) * 16
                out_ref[pl.ds(spot, M), :] |= (code & 0xFFFF) << shift
                out_ref[pl.ds(spot + M, 1), :] |= (scale.astype(I32) & 0xFFFF) << shift
        return carry

    lax.fori_loop(0, ROWS, adjoint, 0, unroll=4)


def push(place, tile, field, turned, posn, weight, top, bottom, left, right):
    return pl.pallas_call(
        push_kernel,
        in_specs=[SMEM, SMEM] + [VMEM] * 8,
        out_shape=struct((DEVICES * MESSAGE, LANES), I32),
        scratch_shapes=[
            pltpu.VMEM((2 * (M + 1) * EXT, LANES), F32),
            pltpu.VMEM((2 * M * EXT, LANES), F32),
            pltpu.VMEM(((QUADS + 1) * TURN, LANES), F32),
            pltpu.VMEM((QUADS * TURN, LANES), F32),
            pltpu.VMEM((RANGE * M, 8, LANES), F32),
            pltpu.VMEM((RANGE * QUADS, 8, LANES), F32),
        ],
        name="push",
        compiler_params=pltpu.CompilerParams(vmem_limit_bytes=12 << 20),
    )(place, tile, field, turned, posn, weight, top, bottom, left, right)


def collect_kernel(slots_ref, back_ref, out_ref, sums):
    sums[...] = jnp.zeros_like(sums)

    def step(i, carry):
        codes = back_ref[pl.ds(i * MESSAGE, M), :]
        scales = back_ref[pl.ds(i * MESSAGE + M, 1), :]
        for r in range(2):
            code, scale = [((x << 16) if r == 0 else x) >> 16 for x in (codes, scales)]
            scale = jnp.exp2(scale.astype(F32) * (1.0 / 256.0)) * (1.0 / TOP)
            sums[slots_ref[r, i]] += code.astype(F32) * scale
        return carry

    lax.fori_loop(0, DEVICES, step, 0, unroll=4)

    def turn(s, carry):
        out_ref[pl.ds(s, M, stride=BANDS), :] = sums[s]
        return carry

    lax.fori_loop(0, BANDS, turn, 0, unroll=8)


def collect(slots, back):
    return pl.pallas_call(
        collect_kernel,
        in_specs=[SMEM, VMEM],
        out_shape=struct((M * BANDS, LANES)),
        scratch_shapes=[pltpu.VMEM((BANDS, M, LANES), F32)],
        name="collect",
        compiler_params=pltpu.CompilerParams(vmem_limit_bytes=5 << 20),
    )(slots, back)


def exchange(x):
    return lax.all_to_all(x, AXES, split_axis=0, concat_axis=0, tiled=True)


def local(predicted_field, parent_band_holder, parent_band_slot, neighbour_positions, unscaled_neighbour_factor, truth_field):
    tiles, faces = lax.axis_size("tile"), lax.axis_size("face")
    bands = jnp.transpose(predicted_field, (1, 0, 2))
    wanted, place = request(parent_band_holder.T, parent_band_slot.T)
    asked = exchange(wanted)
    outgoing, slots = pack(asked, bands)
    recv = exchange(outgoing.reshape(DEVICES, 2, M, LANES)).reshape(2 * DEVICES, M, LANES)
    field, turned, posn, weight, north, south, west, east = regrid(
        place,
        recv,
        neighbour_positions.reshape(POINTS * BANDS, LANES),
        unscaled_neighbour_factor.reshape(POINTS * BANDS, LANES),
        truth_field,
    )
    up = [(i + 1, i) for i in range(tiles - 1)]
    down = [(i, i + 1) for i in range(tiles - 1)]
    bottom = lax.ppermute(north, "tile", up)
    top = lax.ppermute(south, "tile", down)
    right = lax.ppermute(west, "face", [((i + 1) % faces, i) for i in range(faces)])
    left = lax.ppermute(east, "face", [(i, (i + 1) % faces) for i in range(faces)])
    tile = lax.axis_index("tile").astype(I32).reshape(1)
    back = push(place, tile, field, turned, posn, weight, top, bottom, left, right)
    back = exchange(back.reshape(DEVICES, MESSAGE, 1, LANES)).reshape(DEVICES * MESSAGE, LANES)
    return collect(slots, back).reshape(M, BANDS, LANES)


def solution(mesh):
    in_specs = (
        P(None, AXES, None),
        P(AXES, None),
        P(AXES, None),
        P(None, AXES, None),
        P(None, AXES, None),
        P("tile", "face"),
    )
    return jax.shard_map(local, mesh=mesh, in_specs=in_specs, out_specs=P(None, AXES, None), check_vma=False)
```

```python
import jax
import jax.numpy as jnp
from jax import lax
from jax.experimental import pallas as pl
from jax.experimental.pallas import tpu as pltpu
from jax.sharding import PartitionSpec as P

RANGE = 8
FLOOR = 0.01
M = 16
BANDS = 64
LANES = 128
ROWS = 32
EXT = ROWS + 2 * RANGE
DEVICES = 128
POINTS = 4
QUADS = M // 4
MESSAGE = M + 1
TOP = 32700.0
F32 = jnp.float32
I32 = jnp.int32
BF16 = jnp.bfloat16
AXES = ("face", "tile")


def struct(shape, dtype=F32):
    return jax.ShapeDtypeStruct(shape, dtype)


def lane_ids(rows=8):
    return lax.broadcasted_iota(I32, (rows, LANES), 1)


def row_ids(rows=8):
    return lax.broadcasted_iota(I32, (rows, LANES), 0)


def request_kernel(holder_ref, slot_ref, wanted_ref, place_ref):
    owner = lax.broadcasted_iota(I32, (DEVICES, BANDS), 0).astype(F32)
    band = lax.broadcasted_iota(I32, (1, BANDS), 1)
    big = float(1 << 20)
    hots, codes = [], []
    for k in range(2):
        holder = holder_ref[k : k + 1, :].astype(F32)
        code = (band + k * BANDS) * BANDS + slot_ref[k : k + 1, :]
        hots.append(holder == owner)
        codes.append(jnp.broadcast_to(code.astype(F32), (DEVICES, BANDS)))
    low = [jnp.min(jnp.where(h, c, big), axis=1, keepdims=True) for h, c in zip(hots, codes)]
    high = [jnp.max(jnp.where(h, c, -1.0), axis=1, keepdims=True) for h, c in zip(hots, codes)]
    first = jnp.minimum(low[0], low[1])
    last = jnp.maximum(high[0], high[1])
    slots = [
        jnp.where(last >= 0.0, first.astype(I32) & (BANDS - 1), 0),
        jnp.where(last > first, last.astype(I32) & (BANDS - 1), 0),
    ]
    lanes = lane_ids(DEVICES)
    wanted_ref[...] = jnp.where(lanes == 0, slots[0], jnp.where(lanes == 1, slots[1], 0))
    place_ref[...] = jnp.zeros((8, LANES), I32)
    for k in range(2):
        spot = 2.0 * owner + jnp.where(codes[k] == first, 0.0, 1.0)
        spot = jnp.sum(jnp.where(hots[k], spot, 0.0), axis=0, keepdims=True)
        place_ref[k : k + 1, :BANDS] = spot.astype(I32)


def request(holder, slot):
    return pl.pallas_call(
        request_kernel,
        out_shape=(struct((DEVICES, LANES), I32), struct((8, LANES), I32)),
        name="request",
        compiler_params=pltpu.CompilerParams(vmem_limit_bytes=1 << 20),
    )(holder, slot)


def pack_kernel(asked_ref, bands_ref, out_ref, slots_ref, smem, sem):
    table = jnp.transpose(asked_ref[...].astype(F32))[:8].astype(I32)
    slots_ref[...] = table
    copy = pltpu.make_async_copy(slots_ref, smem, sem)
    copy.start()
    copy.wait()

    def step(i, carry):
        for r in range(2):
            out_ref[2 * i + r] = bands_ref[smem[r, i]]
        return carry

    lax.fori_loop(0, DEVICES, step, 0, unroll=8)


def pack(asked, bands):
    return pl.pallas_call(
        pack_kernel,
        out_shape=(struct((2 * DEVICES, M, LANES), BF16), struct((8, LANES), I32)),
        scratch_shapes=[pltpu.SMEM((8, LANES), I32), pltpu.SemaphoreType.DMA],
        name="pack",
        compiler_params=pltpu.CompilerParams(vmem_limit_bytes=4 << 20),
    )(asked, bands)


def prepare_kernel(pos_ref, factor_ref, posn_ref, weight_ref):
    for half in range(2):
        factors = [factor_ref[pl.ds(j * BANDS + half, ROWS, stride=2), :] for j in range(POINTS)]
        total = factors[0] + factors[1] + factors[2] + factors[3]
        for j in range(POINTS):
            spot = j * BANDS + half * ROWS
            posn_ref[pl.ds(spot, ROWS), :] = pos_ref[pl.ds(j * BANDS + half, ROWS, stride=2), :]
            weight_ref[pl.ds(spot, ROWS), :] = factors[j] / total


def prepare(pos, factor):
    return pl.pallas_call(
        prepare_kernel,
        out_shape=(
            struct((POINTS * BANDS, LANES), I32),
            struct((POINTS * BANDS, LANES)),
        ),
        name="prepare",
        cost_estimate=pl.CostEstimate(flops=1 << 20, bytes_accessed=1 << 20, transcendentals=0),
        compiler_params=pltpu.CompilerParams(vmem_limit_bytes=2 << 20),
    )(pos, factor)


def regrid_kernel(
    place_ref, recv_ref, posn_ref, weight_ref, truth_ref,
    field_ref, turned_ref, north_ref, south_ref, west_ref, east_ref,
    low_ref, high_ref,
):
    def spread(row, carry):
        for half in range(2):
            for k, tab in enumerate((low_ref, high_ref)):
                strip = recv_ref[place_ref[k, 2 * row + half]].astype(F32)
                tab[pl.ds(half * ROWS + row, M, stride=BANDS), :] = strip
        return carry

    lax.fori_loop(0, ROWS, spread, 0, unroll=4)

    def regrid(block, carry):
        row = pl.multiple_of(block * 8, 8)
        posn = [posn_ref[pl.ds(j * BANDS + row, 8), :] for j in range(POINTS)]
        weight = [weight_ref[pl.ds(j * BANDS + row, 8), :] for j in range(POINTS)]
        sums = [jnp.zeros((8, LANES), F32)] * M
        for j in range(POINTS):
            lane, upper = posn[j] & (LANES - 1), posn[j] >= LANES
            for m in range(M):
                a, b = [
                    jnp.take_along_axis(tab[pl.ds(m * BANDS + row, 8), :], lane, axis=1, mode="promise_in_bounds")
                    for tab in (low_ref, high_ref)
                ]
                sums[m] = sums[m] + weight[j] * jnp.where(upper, b, a)
        for m in range(M):
            field_ref[pl.ds(m * BANDS + row, 8), :] = sums[m]
        return carry

    lax.fori_loop(0, BANDS // 8, regrid, 0)

    for half in range(2):
        field_ref[pl.ds(M * BANDS + half * ROWS, ROWS), :] = truth_ref[:, half * LANES : (half + 1) * LANES]
    for m in range(M + 1):
        for half in range(2):
            spot = m * BANDS + half * ROWS
            north_ref[pl.ds((2 * m + half) * 8, 8), :] = field_ref[pl.ds(spot, 8), :]
            south_ref[pl.ds((2 * m + half) * 8, 8), :] = field_ref[pl.ds(spot + ROWS - 8, 8), :]
    for q in range(QUADS + 1):
        for half in range(2):
            if q < QUADS:
                parts = [field_ref[pl.ds((4 * q + i) * BANDS + half * ROWS, ROWS), :] for i in range(4)]
            else:
                parts = [truth_ref[:, half * LANES : (half + 1) * LANES]] * 4
            turned = jnp.transpose(jnp.concatenate(parts, axis=0))
            turned_ref[pl.ds(q * 2 * LANES + half * LANES, LANES), :] = turned
            if half == 0:
                west_ref[pl.ds(q * 8, 8), :] = turned[:8]
            else:
                east_ref[pl.ds(q * 8, 8), :] = turned[LANES - 8 :]


VMEM = pl.BlockSpec(memory_space=pltpu.VMEM)
SMEM = pl.BlockSpec(memory_space=pltpu.SMEM)


def regrid(place, recv, posn, weight, truth):
    tall = struct(((M + 1) * 2 * RANGE, LANES))
    wide = struct(((QUADS + 1) * RANGE, LANES))
    return pl.pallas_call(
        regrid_kernel,
        in_specs=[SMEM, VMEM, VMEM, VMEM, VMEM],
        out_shape=(
            struct(((M + 1) * BANDS, LANES)),
            struct(((QUADS + 1) * 2 * LANES, LANES)),
            tall, tall, wide, wide,
        ),
        scratch_shapes=[pltpu.VMEM((M * BANDS, LANES), F32)] * 2,
        name="regrid",
        compiler_params=pltpu.CompilerParams(vmem_limit_bytes=8 << 20),
    )(place, recv, posn, weight, truth)


def steep(diff):
    root = lax.rsqrt(diff * diff + FLOOR)
    value = lax.rsqrt(root)
    return value, (diff * root) * (value * root)


def column_pushes(rows):
    totals, slopes, sights = [], [], []
    for k in range(1, RANGE + 1):
        pairs = [steep(rows(q, 0) - rows(q, k)) for q in range(QUADS)]
        slopes.append([p[1] for p in pairs])
        totals.append((pairs[0][0] + pairs[1][0]) + (pairs[2][0] + pairs[3][0]))
        sights.append(steep(rows(QUADS, 0) - rows(QUADS, k))[0])
    totals = [t + pltpu.roll(t, 2 * ROWS, 1) for t in totals]
    totals = [t + pltpu.roll(t, ROWS, 1) for t in totals]
    pushes = []
    for k in range(1, RANGE + 1):
        push = (1.0 / (k * M)) * (sights[k - 1] - totals[k - 1] * (1.0 / M))
        pushes.append([push * slope for slope in slopes[k - 1]])
    return pushes


def ending(kept, spot, pushed, k):
    moved = pltpu.roll(pushed, k % 8, 0)
    earlier = kept[spot]
    kept[spot] = moved
    return jnp.where(row_ids() >= k, moved, earlier)


def column_sums(kept, rows):
    sums = [jnp.zeros((8, LANES), F32)] * QUADS
    for k, pushes in enumerate(column_pushes(rows), 1):
        for q in range(QUADS):
            sums[q] = sums[q] - pushes[q] + ending(kept, (k - 1) * QUADS + q, pushes[q], k)
    return sums


WIDTH = 2 * LANES
INNER = WIDTH - 2 * RANGE


def inner_kernel(turned_ref, turn_ref, kept_ref):
    kept_ref[...] = jnp.zeros_like(kept_ref)

    def block(b, carry):
        base = pl.multiple_of(b * 8, 8)
        sums = column_sums(kept_ref, lambda q, k: turned_ref[pl.ds(base + (q * WIDTH + k), 8), :])
        for q in range(QUADS):
            turn_ref[pl.ds(base + q * WIDTH, 8), :] = sums[q]
        return carry

    lax.fori_loop(0, INNER // 8, block, 0, unroll=3)


def inner(turned):
    return pl.pallas_call(
        inner_kernel,
        out_shape=(struct((QUADS * WIDTH, LANES)), struct((RANGE * QUADS, 8, LANES))),
        name="inner",
        cost_estimate=pl.CostEstimate(flops=16 << 20, bytes_accessed=12 << 20, transcendentals=2 << 20),
        compiler_params=pltpu.CompilerParams(vmem_limit_bytes=2 << 20),
    )(turned)


def push_kernel(
    place_ref, tile_ref, field_ref, turned_ref, turn_ref, kept_ref, posn_ref, weight_ref,
    top_ref, bottom_ref, left_ref, right_ref,
    out_ref, ext, grad, west, east, kept_columns, kept_rows,
):
    for mh in range(2 * (M + 1)):
        ext[pl.ds(mh * EXT, 8), :] = top_ref[pl.ds(mh * 8, 8), :]
        ext[pl.ds(mh * EXT + 8, ROWS), :] = field_ref[pl.ds(mh * ROWS, ROWS), :]
        ext[pl.ds(mh * EXT + 8 + ROWS, 8), :] = bottom_ref[pl.ds(mh * 8, 8), :]
    for q in range(QUADS + 1):
        west[pl.ds(q * 16, 8), :] = left_ref[pl.ds(q * 8, 8), :]
        west[pl.ds(q * 16 + 8, 8), :] = turned_ref[pl.ds(q * WIDTH, 8), :]
        east[pl.ds(q * 24, 16), :] = turned_ref[pl.ds(q * WIDTH + INNER, 16), :]
        east[pl.ds(q * 24 + 16, 8), :] = right_ref[pl.ds(q * 8, 8), :]
    out_ref[...] = jnp.zeros_like(out_ref)
    first_row = tile_ref[0] * ROWS - RANGE

    def latitude(step, carry):
        half = step // 5
        block = step % 5
        base = pl.multiple_of(half * EXT + block * 8, 8)
        rows = row_ids() + (first_row + block * 8)
        sums = [jnp.zeros((8, LANES), F32)] * M
        for k in range(1, RANGE + 1):
            def diff(m):
                here = base + m * 2 * EXT
                return ext[pl.ds(here, 8), :] - ext[pl.ds(here + k, 8), :]

            total = jnp.zeros((8, LANES), F32)
            slopes = []
            for m in range(M):
                value, slope = steep(diff(m))
                total = total + value
                slopes.append(slope)
            seen, unused = steep(diff(M))
            inside = (rows >= 0) & (rows + k < ROWS * 32)
            push = jnp.where(inside, (1.0 / (k * M)) * (seen - total * (1.0 / M)), 0.0)
            for m in range(M):
                pushed = push * slopes[m]
                sums[m] = sums[m] - pushed + ending(kept_rows, (k - 1) * M + m, pushed, k)
        for m in range(M):
            grad[pl.ds(base + m * 2 * EXT, 8), :] = sums[m]
        return carry

    lax.fori_loop(0, 10, latitude, 0, unroll=2)

    added = [jnp.zeros((8, LANES), F32)] * QUADS
    for k, pushes in enumerate(column_pushes(lambda q, k: west[pl.ds(q * 16 + k, 8), :]), 1):
        for q in range(QUADS):
            added[q] = added[q] + jnp.where(row_ids() < k, pltpu.roll(pushes[q], k % 8, 0), 0.0)
    kept_columns[...] = kept_ref[...]
    near = column_sums(kept_columns, lambda q, k: east[pl.ds(q * 24 + k, 8), :])
    last = column_sums(kept_columns, lambda q, k: east[pl.ds(q * 24 + 8 + k, 8), :])

    for q in range(QUADS):
        first = turn_ref[pl.ds(q * WIDTH, 8), :] + added[q]
        halves = [
            jnp.concatenate([first, turn_ref[pl.ds(q * WIDTH + 8, LANES - 8), :]], axis=0),
            jnp.concatenate([turn_ref[pl.ds(q * WIDTH + LANES, INNER - LANES), :], near[q], last[q]], axis=0),
        ]
        for half in range(2):
            back = jnp.transpose(halves[half])
            for i in range(4):
                spot = ((4 * q + i) * 2 + half) * EXT + 8
                grad[pl.ds(spot, ROWS), :] += back[i * ROWS : (i + 1) * ROWS]

    cells = [(lax.broadcasted_iota(I32, (16, LANES), 0) + 16 * i).astype(F32).astype(BF16) for i in range(16)]
    one, zero = jnp.ones((16, LANES), BF16), jnp.zeros((16, LANES), BF16)

    def adjoint(row, carry):
        for half in range(2):
            tile = grad[pl.ds(half * EXT + 8 + row, M, stride=2 * EXT), :]
            parts, hots = [], []
            for j in range(POINTS):
                spot = j * BANDS + half * ROWS + row
                parts.append(tile * weight_ref[pl.ds(spot, 1), :])
                posn = jnp.broadcast_to(posn_ref[pl.ds(spot, 1), :].astype(F32), (16, LANES)).astype(BF16)
                hots.append(jnp.concatenate([jnp.where(c == posn, one, zero) for c in cells], axis=0))
            part = jnp.concatenate(parts, axis=1)
            high = part.astype(BF16)
            low = (part - high.astype(F32)).astype(BF16)
            both = lax.dot_general(
                jnp.concatenate([high, low], axis=0),
                jnp.concatenate(hots, axis=1),
                (((1,), (1,)), ((), ())),
                preferred_element_type=F32,
            )
            both = both[:M] + both[M:]
            for k in range(2):
                strip = both[:, k * LANES : (k + 1) * LANES]
                largest = jnp.maximum(jnp.max(jnp.abs(strip), axis=0, keepdims=True), 1e-36)
                scale = jnp.ceil(jnp.log2(largest) * 256.0)
                code = jnp.round(strip * (jnp.exp2(scale * (-1.0 / 256.0)) * TOP)).astype(I32)
                place = place_ref[k, 2 * row + half]
                spot = (place >> 1) * MESSAGE
                shift = (place & 1) * 16
                out_ref[pl.ds(spot, M), :] |= (code & 0xFFFF) << shift
                out_ref[pl.ds(spot + M, 1), :] |= (scale.astype(I32) & 0xFFFF) << shift
        return carry

    lax.fori_loop(0, ROWS, adjoint, 0, unroll=4)


def push(place, tile, *arrays):
    return pl.pallas_call(
        push_kernel,
        in_specs=[SMEM, SMEM] + [VMEM] * len(arrays),
        out_shape=struct((DEVICES * MESSAGE, LANES), I32),
        scratch_shapes=[
            pltpu.VMEM((2 * (M + 1) * EXT, LANES), F32),
            pltpu.VMEM((2 * M * EXT, LANES), F32),
            pltpu.VMEM(((QUADS + 1) * 16, LANES), F32),
            pltpu.VMEM(((QUADS + 1) * 24, LANES), F32),
            pltpu.VMEM((RANGE * QUADS, 8, LANES), F32),
            pltpu.VMEM((RANGE * M, 8, LANES), F32),
        ],
        name="push",
        compiler_params=pltpu.CompilerParams(vmem_limit_bytes=6 << 20),
    )(place, tile, *arrays)


def collect_kernel(slots_ref, back_ref, out_ref, sums):
    sums[...] = jnp.zeros_like(sums)

    def step(i, carry):
        codes = back_ref[pl.ds(i * MESSAGE, M), :]
        scales = back_ref[pl.ds(i * MESSAGE + M, 1), :]
        for r in range(2):
            code, scale = [((x << 16) if r == 0 else x) >> 16 for x in (codes, scales)]
            scale = jnp.exp2(scale.astype(F32) * (1.0 / 256.0)) * (1.0 / TOP)
            sums[slots_ref[r, i]] += code.astype(F32) * scale
        return carry

    lax.fori_loop(0, DEVICES, step, 0, unroll=4)

    def turn(s, carry):
        out_ref[pl.ds(s, M, stride=BANDS), :] = sums[s]
        return carry

    lax.fori_loop(0, BANDS, turn, 0, unroll=8)


def collect(slots, back):
    return pl.pallas_call(
        collect_kernel,
        in_specs=[SMEM, VMEM],
        out_shape=struct((M * BANDS, LANES)),
        scratch_shapes=[pltpu.VMEM((BANDS, M, LANES), F32)],
        name="collect",
        compiler_params=pltpu.CompilerParams(vmem_limit_bytes=5 << 20),
    )(slots, back)


def exchange(x):
    return lax.all_to_all(x, AXES, split_axis=0, concat_axis=0, tiled=True)


def local(predicted_field, parent_band_holder, parent_band_slot, neighbour_positions, unscaled_neighbour_factor, truth_field):
    tiles, faces = lax.axis_size("tile"), lax.axis_size("face")
    bands = jnp.transpose(predicted_field, (1, 0, 2))
    posn, weight = prepare(
        neighbour_positions.reshape(POINTS * BANDS, LANES),
        unscaled_neighbour_factor.reshape(POINTS * BANDS, LANES),
    )
    wanted, place = request(parent_band_holder.T, parent_band_slot.T)
    asked = exchange(wanted)
    outgoing, slots = pack(asked, bands)
    recv = exchange(outgoing.reshape(DEVICES, 2, M, LANES)).reshape(2 * DEVICES, M, LANES)
    field, turned, north, south, west, east = regrid(place, recv, posn, weight, truth_field)
    up = [(i + 1, i) for i in range(tiles - 1)]
    down = [(i, i + 1) for i in range(tiles - 1)]
    bottom = lax.ppermute(north, "tile", up)
    top = lax.ppermute(south, "tile", down)
    right = lax.ppermute(west, "face", [((i + 1) % faces, i) for i in range(faces)])
    left = lax.ppermute(east, "face", [(i, (i + 1) % faces) for i in range(faces)])
    tile = lax.axis_index("tile").astype(I32).reshape(1)
    turn, kept = inner(turned)
    back = push(place, tile, field, turned, turn, kept, posn, weight, top, bottom, left, right)
    back = exchange(back.reshape(DEVICES, MESSAGE, 1, LANES)).reshape(DEVICES * MESSAGE, LANES)
    return collect(slots, back).reshape(M, BANDS, LANES)


def solution(mesh):
    in_specs = (
        P(None, AXES, None),
        P(AXES, None),
        P(AXES, None),
        P(None, AXES, None),
        P(None, AXES, None),
        P("tile", "face"),
    )
    return jax.shard_map(local, mesh=mesh, in_specs=in_specs, out_specs=P(None, AXES, None), check_vma=False)
```

```python
import jax
import jax.numpy as jnp
from jax import lax
from jax.experimental import pallas as pl
from jax.experimental.pallas import tpu as pltpu
from jax.sharding import PartitionSpec as P

RANGE = 8
FLOOR = 0.01
M = 16
BANDS = 64
LANES = 128
ROWS = 32
EXT = ROWS + 2 * RANGE
DEVICES = 128
POINTS = 4
QUADS = M // 4
MESSAGE = M + 1
TOP = 32700.0
F32 = jnp.float32
I32 = jnp.int32
BF16 = jnp.bfloat16
AXES = ("face", "tile")


def struct(shape, dtype=F32):
    return jax.ShapeDtypeStruct(shape, dtype)


def lane_ids(rows=8):
    return lax.broadcasted_iota(I32, (rows, LANES), 1)


def row_ids(rows=8):
    return lax.broadcasted_iota(I32, (rows, LANES), 0)


def request_kernel(holder_hbm, slot_hbm, wanted_ref, place_ref, holder_ref, slot_ref, sems):
    copies = [
        pltpu.make_async_copy(holder_hbm, holder_ref, sems.at[0]),
        pltpu.make_async_copy(slot_hbm, slot_ref, sems.at[1]),
    ]
    for copy in copies:
        copy.start()
    for copy in copies:
        copy.wait()
    owner = lax.broadcasted_iota(I32, (DEVICES, BANDS), 0).astype(F32)
    band = lax.broadcasted_iota(I32, (1, BANDS), 1)
    big = float(1 << 20)
    hots, codes = [], []
    for k in range(2):
        holder = holder_ref[k : k + 1, :].astype(F32)
        code = (band + k * BANDS) * BANDS + slot_ref[k : k + 1, :]
        hots.append(holder == owner)
        codes.append(jnp.broadcast_to(code.astype(F32), (DEVICES, BANDS)))
    low = [jnp.min(jnp.where(h, c, big), axis=1, keepdims=True) for h, c in zip(hots, codes)]
    high = [jnp.max(jnp.where(h, c, -1.0), axis=1, keepdims=True) for h, c in zip(hots, codes)]
    first = jnp.minimum(low[0], low[1])
    last = jnp.maximum(high[0], high[1])
    slots = [
        jnp.where(last >= 0.0, first.astype(I32) & (BANDS - 1), 0),
        jnp.where(last > first, last.astype(I32) & (BANDS - 1), 0),
    ]
    lanes = lane_ids(DEVICES)
    wanted_ref[...] = jnp.where(lanes == 0, slots[0], jnp.where(lanes == 1, slots[1], 0))
    place_ref[...] = jnp.zeros((8, LANES), I32)
    for k in range(2):
        spot = 2.0 * owner + jnp.where(codes[k] == first, 0.0, 1.0)
        spot = jnp.sum(jnp.where(hots[k], spot, 0.0), axis=0, keepdims=True)
        place_ref[k : k + 1, :BANDS] = spot.astype(I32)


def request(holder, slot):
    return pl.pallas_call(
        request_kernel,
        in_specs=[pl.BlockSpec(memory_space=pl.ANY)] * 2,
        out_shape=(struct((DEVICES, LANES), I32), struct((8, LANES), I32)),
        scratch_shapes=[pltpu.VMEM((2, BANDS), I32)] * 2 + [pltpu.SemaphoreType.DMA((2,))],
        name="request",
    )(holder, slot)


def pack_kernel(asked_ref, bands_ref, out_ref, slots_ref, smem, sem):
    table = jnp.transpose(asked_ref[...].astype(F32))[:8].astype(I32)
    slots_ref[...] = table
    copy = pltpu.make_async_copy(slots_ref, smem, sem)
    copy.start()
    copy.wait()

    def step(i, carry):
        for r in range(2):
            out_ref[2 * i + r] = bands_ref[smem[r, i]]
        return carry

    lax.fori_loop(0, DEVICES, step, 0, unroll=8)


def pack(asked, bands):
    return pl.pallas_call(
        pack_kernel,
        out_shape=(struct((2 * DEVICES, M, LANES), BF16), struct((8, LANES), I32)),
        scratch_shapes=[pltpu.SMEM((8, LANES), I32), pltpu.SemaphoreType.DMA],
        name="pack",
        compiler_params=pltpu.CompilerParams(vmem_limit_bytes=4 << 20),
    )(asked, bands)


def prepare_kernel(pos_ref, factor_ref, posn_ref, weight_ref):
    for half in range(2):
        factors = [factor_ref[pl.ds(j * BANDS + half, ROWS, stride=2), :] for j in range(POINTS)]
        total = factors[0] + factors[1] + factors[2] + factors[3]
        for j in range(POINTS):
            spot = j * BANDS + half * ROWS
            posn_ref[pl.ds(spot, ROWS), :] = pos_ref[pl.ds(j * BANDS + half, ROWS, stride=2), :]
            weight_ref[pl.ds(spot, ROWS), :] = factors[j] / total


def prepare(pos, factor):
    return pl.pallas_call(
        prepare_kernel,
        out_shape=(
            struct((POINTS * BANDS, LANES), I32),
            struct((POINTS * BANDS, LANES)),
        ),
        name="prepare",
        cost_estimate=pl.CostEstimate(flops=1 << 20, bytes_accessed=1 << 20, transcendentals=0),
        compiler_params=pltpu.CompilerParams(vmem_limit_bytes=2 << 20),
    )(pos, factor)


def regrid_kernel(
    place_ref, recv_ref, posn_ref, weight_ref, truth_ref,
    field_ref, turned_ref, north_ref, south_ref, west_ref, east_ref,
    low_ref, high_ref,
):
    def spread(row, carry):
        for half in range(2):
            for k, tab in enumerate((low_ref, high_ref)):
                strip = recv_ref[place_ref[k, 2 * row + half]].astype(F32)
                tab[pl.ds(half * ROWS + row, M, stride=BANDS), :] = strip
        return carry

    lax.fori_loop(0, ROWS, spread, 0, unroll=8)

    def regrid(block, carry):
        row = pl.multiple_of(block * 8, 8)
        posn = [posn_ref[pl.ds(j * BANDS + row, 8), :] for j in range(POINTS)]
        weight = [weight_ref[pl.ds(j * BANDS + row, 8), :] for j in range(POINTS)]
        sums = [jnp.zeros((8, LANES), F32)] * M
        for j in range(POINTS):
            lane, upper = posn[j] & (LANES - 1), posn[j] >= LANES
            for m in range(M):
                a, b = [
                    jnp.take_along_axis(tab[pl.ds(m * BANDS + row, 8), :], lane, axis=1, mode="promise_in_bounds")
                    for tab in (low_ref, high_ref)
                ]
                sums[m] = sums[m] + weight[j] * jnp.where(upper, b, a)
        for m in range(M):
            field_ref[pl.ds(m * BANDS + row, 8), :] = sums[m]
        return carry

    lax.fori_loop(0, BANDS // 8, regrid, 0)

    for half in range(2):
        field_ref[pl.ds(M * BANDS + half * ROWS, ROWS), :] = truth_ref[:, half * LANES : (half + 1) * LANES]
    for m in range(M + 1):
        for half in range(2):
            spot = m * BANDS + half * ROWS
            north_ref[pl.ds((2 * m + half) * 8, 8), :] = field_ref[pl.ds(spot, 8), :]
            south_ref[pl.ds((2 * m + half) * 8, 8), :] = field_ref[pl.ds(spot + ROWS - 8, 8), :]
    for q in range(QUADS + 1):
        for half in range(2):
            if q < QUADS:
                parts = [field_ref[pl.ds((4 * q + i) * BANDS + half * ROWS, ROWS), :] for i in range(4)]
            else:
                parts = [truth_ref[:, half * LANES : (half + 1) * LANES]] * 4
            turned = jnp.transpose(jnp.concatenate(parts, axis=0))
            turned_ref[pl.ds(q * 2 * LANES + half * LANES, LANES), :] = turned
            if half == 0:
                west_ref[pl.ds(q * 8, 8), :] = turned[:8]
            else:
                east_ref[pl.ds(q * 8, 8), :] = turned[LANES - 8 :]


VMEM = pl.BlockSpec(memory_space=pltpu.VMEM)
SMEM = pl.BlockSpec(memory_space=pltpu.SMEM)


def regrid(place, recv, posn, weight, truth):
    tall = struct(((M + 1) * 2 * RANGE, LANES))
    wide = struct(((QUADS + 1) * RANGE, LANES))
    return pl.pallas_call(
        regrid_kernel,
        in_specs=[SMEM, VMEM, VMEM, VMEM, VMEM],
        out_shape=(
            struct(((M + 1) * BANDS, LANES)),
            struct(((QUADS + 1) * 2 * LANES, LANES)),
            tall, tall, wide, wide,
        ),
        scratch_shapes=[pltpu.VMEM((M * BANDS, LANES), F32)] * 2,
        name="regrid",
        compiler_params=pltpu.CompilerParams(vmem_limit_bytes=8 << 20),
    )(place, recv, posn, weight, truth)


def steep(diff):
    root = lax.rsqrt(diff * diff + FLOOR)
    value = lax.rsqrt(root)
    return value, (diff * root) * (value * root)


def column_pushes(rows):
    totals, slopes, sights = [], [], []
    for k in range(1, RANGE + 1):
        pairs = [steep(rows(q, 0) - rows(q, k)) for q in range(QUADS)]
        slopes.append([p[1] for p in pairs])
        totals.append((pairs[0][0] + pairs[1][0]) + (pairs[2][0] + pairs[3][0]))
        sights.append(steep(rows(QUADS, 0) - rows(QUADS, k))[0])
    totals = [t + pltpu.roll(t, 2 * ROWS, 1) for t in totals]
    totals = [t + pltpu.roll(t, ROWS, 1) for t in totals]
    pushes = []
    for k in range(1, RANGE + 1):
        push = (1.0 / (k * M)) * (sights[k - 1] - totals[k - 1] * (1.0 / M))
        pushes.append([push * slope for slope in slopes[k - 1]])
    return pushes


def ending(kept, spot, pushed, k):
    moved = pltpu.roll(pushed, k % 8, 0)
    earlier = kept[spot]
    kept[spot] = moved
    return jnp.where(row_ids() >= k, moved, earlier)


def column_sums(kept, rows):
    sums = [jnp.zeros((8, LANES), F32)] * QUADS
    for k, pushes in enumerate(column_pushes(rows), 1):
        for q in range(QUADS):
            sums[q] = sums[q] - pushes[q] + ending(kept, (k - 1) * QUADS + q, pushes[q], k)
    return sums


WIDTH = 2 * LANES
INNER = WIDTH - 2 * RANGE


def inner_kernel(turned_ref, turn_ref, kept_ref):
    kept_ref[...] = jnp.zeros_like(kept_ref)

    def block(b, carry):
        base = pl.multiple_of(b * 8, 8)
        sums = column_sums(kept_ref, lambda q, k: turned_ref[pl.ds(base + (q * WIDTH + k), 8), :])
        for q in range(QUADS):
            turn_ref[pl.ds(base + q * WIDTH, 8), :] = sums[q]
        return carry

    lax.fori_loop(0, INNER // 8, block, 0, unroll=3)


def inner(turned):
    return pl.pallas_call(
        inner_kernel,
        out_shape=(struct((QUADS * WIDTH, LANES)), struct((RANGE * QUADS, 8, LANES))),
        name="inner",
        cost_estimate=pl.CostEstimate(flops=16 << 20, bytes_accessed=12 << 20, transcendentals=2 << 20),
        compiler_params=pltpu.CompilerParams(vmem_limit_bytes=2 << 20),
    )(turned)


def push_kernel(
    place_ref, tile_ref, field_ref, turned_ref, turn_ref, kept_ref, posn_ref, weight_ref,
    top_ref, bottom_ref, left_ref, right_ref,
    out_ref, ext, grad, west, east, kept_columns, kept_rows,
):
    for mh in range(2 * (M + 1)):
        ext[pl.ds(mh * EXT, 8), :] = top_ref[pl.ds(mh * 8, 8), :]
        ext[pl.ds(mh * EXT + 8, ROWS), :] = field_ref[pl.ds(mh * ROWS, ROWS), :]
        ext[pl.ds(mh * EXT + 8 + ROWS, 8), :] = bottom_ref[pl.ds(mh * 8, 8), :]
    for q in range(QUADS + 1):
        west[pl.ds(q * 16, 8), :] = left_ref[pl.ds(q * 8, 8), :]
        west[pl.ds(q * 16 + 8, 8), :] = turned_ref[pl.ds(q * WIDTH, 8), :]
        east[pl.ds(q * 24, 16), :] = turned_ref[pl.ds(q * WIDTH + INNER, 16), :]
        east[pl.ds(q * 24 + 16, 8), :] = right_ref[pl.ds(q * 8, 8), :]
    out_ref[...] = jnp.zeros_like(out_ref)
    first_row = tile_ref[0] * ROWS - RANGE

    def latitude(step, carry):
        half = step // 5
        block = step % 5
        base = pl.multiple_of(half * EXT + block * 8, 8)
        rows = row_ids() + (first_row + block * 8)
        sums = [jnp.zeros((8, LANES), F32)] * M
        for k in range(1, RANGE + 1):
            def diff(m):
                here = base + m * 2 * EXT
                return ext[pl.ds(here, 8), :] - ext[pl.ds(here + k, 8), :]

            total = jnp.zeros((8, LANES), F32)
            slopes = []
            for m in range(M):
                value, slope = steep(diff(m))
                total = total + value
                slopes.append(slope)
            seen, unused = steep(diff(M))
            inside = (rows >= 0) & (rows + k < ROWS * 32)
            push = jnp.where(inside, (1.0 / (k * M)) * (seen - total * (1.0 / M)), 0.0)
            for m in range(M):
                pushed = push * slopes[m]
                sums[m] = sums[m] - pushed + ending(kept_rows, (k - 1) * M + m, pushed, k)
        for m in range(M):
            grad[pl.ds(base + m * 2 * EXT, 8), :] = sums[m]
        return carry

    lax.fori_loop(0, 10, latitude, 0, unroll=2)

    added = [jnp.zeros((8, LANES), F32)] * QUADS
    for k, pushes in enumerate(column_pushes(lambda q, k: west[pl.ds(q * 16 + k, 8), :]), 1):
        for q in range(QUADS):
            added[q] = added[q] + jnp.where(row_ids() < k, pltpu.roll(pushes[q], k % 8, 0), 0.0)
    kept_columns[...] = kept_ref[...]
    near = column_sums(kept_columns, lambda q, k: east[pl.ds(q * 24 + k, 8), :])
    last = column_sums(kept_columns, lambda q, k: east[pl.ds(q * 24 + 8 + k, 8), :])

    for q in range(QUADS):
        first = turn_ref[pl.ds(q * WIDTH, 8), :] + added[q]
        halves = [
            jnp.concatenate([first, turn_ref[pl.ds(q * WIDTH + 8, LANES - 8), :]], axis=0),
            jnp.concatenate([turn_ref[pl.ds(q * WIDTH + LANES, INNER - LANES), :], near[q], last[q]], axis=0),
        ]
        for half in range(2):
            back = jnp.transpose(halves[half])
            for i in range(4):
                spot = ((4 * q + i) * 2 + half) * EXT + 8
                grad[pl.ds(spot, ROWS), :] += back[i * ROWS : (i + 1) * ROWS]

    cells = [(lax.broadcasted_iota(I32, (16, LANES), 0) + 16 * i).astype(F32).astype(BF16) for i in range(16)]
    one, zero = jnp.ones((16, LANES), BF16), jnp.zeros((16, LANES), BF16)

    def adjoint(row, carry):
        for half in range(2):
            tile = grad[pl.ds(half * EXT + 8 + row, M, stride=2 * EXT), :]
            parts, hots = [], []
            for j in range(POINTS):
                spot = j * BANDS + half * ROWS + row
                parts.append(tile * weight_ref[pl.ds(spot, 1), :])
                posn = jnp.broadcast_to(posn_ref[pl.ds(spot, 1), :].astype(F32), (16, LANES)).astype(BF16)
                hots.append(jnp.concatenate([jnp.where(c == posn, one, zero) for c in cells], axis=0))
            part = jnp.concatenate(parts, axis=1)
            high = part.astype(BF16)
            low = (part - high.astype(F32)).astype(BF16)
            both = lax.dot_general(
                jnp.concatenate([high, low], axis=0),
                jnp.concatenate(hots, axis=1),
                (((1,), (1,)), ((), ())),
                preferred_element_type=F32,
            )
            both = both[:M] + both[M:]
            for k in range(2):
                strip = both[:, k * LANES : (k + 1) * LANES]
                largest = jnp.maximum(jnp.max(jnp.abs(strip), axis=0, keepdims=True), 1e-36)
                scale = jnp.ceil(jnp.log2(largest) * 256.0)
                code = jnp.round(strip * (jnp.exp2(scale * (-1.0 / 256.0)) * TOP)).astype(I32)
                place = place_ref[k, 2 * row + half]
                spot = (place >> 1) * MESSAGE
                shift = (place & 1) * 16
                out_ref[pl.ds(spot, M), :] |= (code & 0xFFFF) << shift
                out_ref[pl.ds(spot + M, 1), :] |= (scale.astype(I32) & 0xFFFF) << shift
        return carry

    lax.fori_loop(0, ROWS, adjoint, 0, unroll=4)


def push(place, tile, *arrays):
    return pl.pallas_call(
        push_kernel,
        in_specs=[SMEM, SMEM] + [VMEM] * len(arrays),
        out_shape=struct((DEVICES * MESSAGE, LANES), I32),
        scratch_shapes=[
            pltpu.VMEM((2 * (M + 1) * EXT, LANES), F32),
            pltpu.VMEM((2 * M * EXT, LANES), F32),
            pltpu.VMEM(((QUADS + 1) * 16, LANES), F32),
            pltpu.VMEM(((QUADS + 1) * 24, LANES), F32),
            pltpu.VMEM((RANGE * QUADS, 8, LANES), F32),
            pltpu.VMEM((RANGE * M, 8, LANES), F32),
        ],
        name="push",
        compiler_params=pltpu.CompilerParams(vmem_limit_bytes=6 << 20),
    )(place, tile, *arrays)


def collect_kernel(slots_ref, back_ref, out_ref, *sums):
    for part in sums:
        part[...] = jnp.zeros_like(part)

    def step(i, carry):
        codes = back_ref[pl.ds(i * MESSAGE, M), :]
        scales = back_ref[pl.ds(i * MESSAGE + M, 1), :]
        for r in range(2):
            code, scale = [((x << 16) if r == 0 else x) >> 16 for x in (codes, scales)]
            scale = jnp.exp2(scale.astype(F32) * (1.0 / 256.0)) * (1.0 / TOP)
            sums[r][slots_ref[r, i]] += code.astype(F32) * scale
        return carry

    lax.fori_loop(0, DEVICES, step, 0, unroll=8)

    def turn(s, carry):
        out_ref[pl.ds(s, M, stride=BANDS), :] = sums[0][s] + sums[1][s]
        return carry

    lax.fori_loop(0, BANDS, turn, 0, unroll=8)


def collect(slots, back):
    return pl.pallas_call(
        collect_kernel,
        in_specs=[SMEM, VMEM],
        out_shape=struct((M * BANDS, LANES)),
        scratch_shapes=[pltpu.VMEM((BANDS, M, LANES), F32)] * 2,
        name="collect",
        compiler_params=pltpu.CompilerParams(vmem_limit_bytes=5 << 20),
    )(slots, back)


def exchange(x):
    return lax.all_to_all(x, AXES, split_axis=0, concat_axis=0, tiled=True)


def local(predicted_field, parent_band_holder, parent_band_slot, neighbour_positions, unscaled_neighbour_factor, truth_field):
    tiles, faces = lax.axis_size("tile"), lax.axis_size("face")
    bands = jnp.transpose(predicted_field, (1, 0, 2))
    posn, weight = prepare(
        neighbour_positions.reshape(POINTS * BANDS, LANES),
        unscaled_neighbour_factor.reshape(POINTS * BANDS, LANES),
    )
    wanted, place = request(parent_band_holder.T, parent_band_slot.T)
    asked, posn, weight = lax.optimization_barrier((exchange(wanted), posn, weight))
    outgoing, slots = pack(asked, bands)
    recv = exchange(outgoing.reshape(DEVICES, 2, M, LANES)).reshape(2 * DEVICES, M, LANES)
    field, turned, north, south, west, east = regrid(place, recv, posn, weight, truth_field)
    up = [(i + 1, i) for i in range(tiles - 1)]
    down = [(i, i + 1) for i in range(tiles - 1)]
    bottom = lax.ppermute(north, "tile", up)
    top = lax.ppermute(south, "tile", down)
    right = lax.ppermute(west, "face", [((i + 1) % faces, i) for i in range(faces)])
    left = lax.ppermute(east, "face", [(i, (i + 1) % faces) for i in range(faces)])
    tile = lax.axis_index("tile").astype(I32).reshape(1)
    turn, kept = inner(turned)
    back = push(place, tile, field, turned, turn, kept, posn, weight, top, bottom, left, right)
    back = exchange(back.reshape(DEVICES, MESSAGE, 1, LANES)).reshape(DEVICES * MESSAGE, LANES)
    return collect(slots, back).reshape(M, BANDS, LANES)


def solution(mesh):
    in_specs = (
        P(None, AXES, None),
        P(AXES, None),
        P(AXES, None),
        P(None, AXES, None),
        P(None, AXES, None),
        P("tile", "face"),
    )
    return jax.shard_map(local, mesh=mesh, in_specs=in_specs, out_specs=P(None, AXES, None), check_vma=False)
```

```python
import jax
import jax.numpy as jnp
from jax import lax
from jax.experimental import pallas as pl
from jax.experimental.pallas import tpu as pltpu
from jax.sharding import PartitionSpec as P

RANGE = 8
FLOOR = 0.01
M = 16
BANDS = 64
LANES = 128
ROWS = 32
EXT = ROWS + 2 * RANGE
DEVICES = 128
POINTS = 4
QUADS = M // 4
MESSAGE = M + 1
TOP = 32700.0
F32 = jnp.float32
I32 = jnp.int32
BF16 = jnp.bfloat16
AXES = ("face", "tile")


def struct(shape, dtype=F32):
    return jax.ShapeDtypeStruct(shape, dtype)


def lane_ids(rows=8):
    return lax.broadcasted_iota(I32, (rows, LANES), 1)


def row_ids(rows=8):
    return lax.broadcasted_iota(I32, (rows, LANES), 0)


def request_kernel(holder_hbm, slot_hbm, wanted_ref, place_ref, holder_ref, slot_ref, sems):
    copies = [
        pltpu.make_async_copy(holder_hbm, holder_ref, sems.at[0]),
        pltpu.make_async_copy(slot_hbm, slot_ref, sems.at[1]),
    ]
    for copy in copies:
        copy.start()
    for copy in copies:
        copy.wait()
    owner = lax.broadcasted_iota(I32, (DEVICES, BANDS), 0).astype(F32)
    band = lax.broadcasted_iota(I32, (1, BANDS), 1)
    big = float(1 << 20)
    hots, codes = [], []
    for k in range(2):
        holder = holder_ref[k : k + 1, :].astype(F32)
        code = (band + k * BANDS) * BANDS + slot_ref[k : k + 1, :]
        hots.append(holder == owner)
        codes.append(jnp.broadcast_to(code.astype(F32), (DEVICES, BANDS)))
    low = [jnp.min(jnp.where(h, c, big), axis=1, keepdims=True) for h, c in zip(hots, codes)]
    high = [jnp.max(jnp.where(h, c, -1.0), axis=1, keepdims=True) for h, c in zip(hots, codes)]
    first = jnp.minimum(low[0], low[1])
    last = jnp.maximum(high[0], high[1])
    slots = [
        jnp.where(last >= 0.0, first.astype(I32) & (BANDS - 1), 0),
        jnp.where(last > first, last.astype(I32) & (BANDS - 1), 0),
    ]
    lanes = lane_ids(DEVICES)
    wanted_ref[...] = jnp.where(lanes == 0, slots[0], jnp.where(lanes == 1, slots[1], 0))
    place_ref[...] = jnp.zeros((8, LANES), I32)
    for k in range(2):
        spot = 2.0 * owner + jnp.where(codes[k] == first, 0.0, 1.0)
        spot = jnp.sum(jnp.where(hots[k], spot, 0.0), axis=0, keepdims=True)
        place_ref[k : k + 1, :BANDS] = spot.astype(I32)


def request(holder, slot):
    return pl.pallas_call(
        request_kernel,
        in_specs=[pl.BlockSpec(memory_space=pl.ANY)] * 2,
        out_shape=(struct((DEVICES, LANES), I32), struct((8, LANES), I32)),
        scratch_shapes=[pltpu.VMEM((2, BANDS), I32)] * 2 + [pltpu.SemaphoreType.DMA((2,))],
        name="request",
    )(holder, slot)


def pack_kernel(asked_ref, bands_ref, out_ref, slots_ref, smem, sem):
    table = jnp.transpose(asked_ref[...].astype(F32))[:8].astype(I32)
    slots_ref[...] = table
    copy = pltpu.make_async_copy(slots_ref, smem, sem)
    copy.start()
    copy.wait()

    def step(i, carry):
        for r in range(2):
            out_ref[2 * i + r] = bands_ref[smem[r, i]]
        return carry

    lax.fori_loop(0, DEVICES, step, 0, unroll=8)


def pack(asked, bands):
    return pl.pallas_call(
        pack_kernel,
        out_shape=(struct((2 * DEVICES, M, LANES), BF16), struct((8, LANES), I32)),
        scratch_shapes=[pltpu.SMEM((8, LANES), I32), pltpu.SemaphoreType.DMA],
        name="pack",
        compiler_params=pltpu.CompilerParams(vmem_limit_bytes=4 << 20),
    )(asked, bands)


def prepare_kernel(pos_ref, factor_ref, posn_ref, weight_ref):
    for half in range(2):
        factors = [factor_ref[pl.ds(j * BANDS + half, ROWS, stride=2), :] for j in range(POINTS)]
        total = factors[0] + factors[1] + factors[2] + factors[3]
        for j in range(POINTS):
            spot = j * BANDS + half * ROWS
            posn_ref[pl.ds(spot, ROWS), :] = pos_ref[pl.ds(j * BANDS + half, ROWS, stride=2), :]
            weight_ref[pl.ds(spot, ROWS), :] = factors[j] / total


def prepare(pos, factor):
    return pl.pallas_call(
        prepare_kernel,
        out_shape=(
            struct((POINTS * BANDS, LANES), I32),
            struct((POINTS * BANDS, LANES)),
        ),
        name="prepare",
        cost_estimate=pl.CostEstimate(flops=1 << 20, bytes_accessed=1 << 20, transcendentals=0),
        compiler_params=pltpu.CompilerParams(vmem_limit_bytes=2 << 20),
    )(pos, factor)


def regrid_kernel(
    place_ref, tile_ref, face_ref, recv_ref, posn_ref, weight_ref, truth_ref,
    field_ref, turned_ref, tall0_ref, tall1_ref, wide0_ref, wide1_ref,
    low_ref, high_ref,
):
    def spread(row, carry):
        for half in range(2):
            for k, tab in enumerate((low_ref, high_ref)):
                strip = recv_ref[place_ref[k, 2 * row + half]].astype(F32)
                tab[pl.ds(half * ROWS + row, M, stride=BANDS), :] = strip
        return carry

    lax.fori_loop(0, ROWS, spread, 0, unroll=8)

    def regrid(block, carry):
        row = pl.multiple_of(block * 8, 8)
        posn = [posn_ref[pl.ds(j * BANDS + row, 8), :] for j in range(POINTS)]
        weight = [weight_ref[pl.ds(j * BANDS + row, 8), :] for j in range(POINTS)]
        sums = [jnp.zeros((8, LANES), F32)] * M
        for j in range(POINTS):
            lane, upper = posn[j] & (LANES - 1), posn[j] >= LANES
            for m in range(M):
                a, b = [
                    jnp.take_along_axis(tab[pl.ds(m * BANDS + row, 8), :], lane, axis=1, mode="promise_in_bounds")
                    for tab in (low_ref, high_ref)
                ]
                sums[m] = sums[m] + weight[j] * jnp.where(upper, b, a)
        for m in range(M):
            field_ref[pl.ds(m * BANDS + row, 8), :] = sums[m]
        return carry

    lax.fori_loop(0, BANDS // 8, regrid, 0)

    for half in range(2):
        field_ref[pl.ds(M * BANDS + half * ROWS, ROWS), :] = truth_ref[:, half * LANES : (half + 1) * LANES]
    odd = tile_ref[0] & 1
    for m in range(M + 1):
        for half in range(2):
            spot = m * BANDS + half * ROWS
            for message, edge in ((tall0_ref, 1 - odd), (tall1_ref, odd)):
                rows = pl.ds(pl.multiple_of(spot + edge * (ROWS - 8), 8), 8)
                message[pl.ds((2 * m + half) * 8, 8), :] = field_ref[rows, :]
    for q in range(QUADS + 1):
        for half in range(2):
            if q < QUADS:
                parts = [field_ref[pl.ds((4 * q + i) * BANDS + half * ROWS, ROWS), :] for i in range(4)]
            else:
                parts = [truth_ref[:, half * LANES : (half + 1) * LANES]] * 4
            turned = jnp.transpose(jnp.concatenate(parts, axis=0))
            turned_ref[pl.ds(q * 2 * LANES + half * LANES, LANES), :] = turned
    odd = face_ref[0] & 1
    for q in range(QUADS + 1):
        for message, edge in ((wide0_ref, 1 - odd), (wide1_ref, odd)):
            columns = pl.ds(pl.multiple_of(q * 2 * LANES + edge * (2 * LANES - 8), 8), 8)
            message[pl.ds(q * 8, 8), :] = turned_ref[columns, :]


VMEM = pl.BlockSpec(memory_space=pltpu.VMEM)
SMEM = pl.BlockSpec(memory_space=pltpu.SMEM)


def regrid(place, tile, face, recv, posn, weight, truth):
    tall = struct(((M + 1) * 2 * RANGE, LANES))
    wide = struct(((QUADS + 1) * RANGE, LANES))
    return pl.pallas_call(
        regrid_kernel,
        in_specs=[SMEM] * 3 + [VMEM] * 4,
        out_shape=(
            struct(((M + 1) * BANDS, LANES)),
            struct(((QUADS + 1) * 2 * LANES, LANES)),
            tall, tall, wide, wide,
        ),
        scratch_shapes=[pltpu.VMEM((M * BANDS, LANES), F32)] * 2,
        name="regrid",
        compiler_params=pltpu.CompilerParams(vmem_limit_bytes=8 << 20),
    )(place, tile, face, recv, posn, weight, truth)


def steep(diff):
    root = lax.rsqrt(diff * diff + FLOOR)
    value = lax.rsqrt(root)
    return value, (diff * root) * (value * root)


def column_pushes(rows):
    totals, slopes, sights = [], [], []
    for k in range(1, RANGE + 1):
        pairs = [steep(rows(q, 0) - rows(q, k)) for q in range(QUADS)]
        slopes.append([p[1] for p in pairs])
        totals.append((pairs[0][0] + pairs[1][0]) + (pairs[2][0] + pairs[3][0]))
        sights.append(steep(rows(QUADS, 0) - rows(QUADS, k))[0])
    totals = [t + pltpu.roll(t, 2 * ROWS, 1) for t in totals]
    totals = [t + pltpu.roll(t, ROWS, 1) for t in totals]
    pushes = []
    for k in range(1, RANGE + 1):
        push = (1.0 / (k * M)) * (sights[k - 1] - totals[k - 1] * (1.0 / M))
        pushes.append([push * slope for slope in slopes[k - 1]])
    return pushes


def ending(kept, spot, pushed, k):
    moved = pltpu.roll(pushed, k % 8, 0)
    earlier = kept[spot]
    kept[spot] = moved
    return jnp.where(row_ids() >= k, moved, earlier)


def column_sums(kept, rows):
    sums = [jnp.zeros((8, LANES), F32)] * QUADS
    for k, pushes in enumerate(column_pushes(rows), 1):
        for q in range(QUADS):
            sums[q] = sums[q] - pushes[q] + ending(kept, (k - 1) * QUADS + q, pushes[q], k)
    return sums


WIDTH = 2 * LANES
INNER = WIDTH - 2 * RANGE


def inner_kernel(turned_ref, turn_ref, kept_ref):
    kept_ref[...] = jnp.zeros_like(kept_ref)

    def block(b, carry):
        base = pl.multiple_of(b * 8, 8)
        sums = column_sums(kept_ref, lambda q, k: turned_ref[pl.ds(base + (q * WIDTH + k), 8), :])
        for q in range(QUADS):
            turn_ref[pl.ds(base + q * WIDTH, 8), :] = sums[q]
        return carry

    lax.fori_loop(0, INNER // 8, block, 0, unroll=3)


def inner(turned):
    return pl.pallas_call(
        inner_kernel,
        out_shape=(struct((QUADS * WIDTH, LANES)), struct((RANGE * QUADS, 8, LANES))),
        name="inner",
        cost_estimate=pl.CostEstimate(flops=16 << 20, bytes_accessed=12 << 20, transcendentals=2 << 20),
        compiler_params=pltpu.CompilerParams(vmem_limit_bytes=2 << 20),
    )(turned)


def push_kernel(
    place_ref, tile_ref, face_ref, field_ref, turned_ref, turn_ref, kept_ref, posn_ref, weight_ref,
    tall0_ref, tall1_ref, wide0_ref, wide1_ref,
    out_ref, ext, grad, west, east, kept_columns, kept_rows,
):
    odd = tile_ref[0] & 1
    for mh in range(2 * (M + 1)):
        for message, below in ((tall0_ref, 1 - odd), (tall1_ref, odd)):
            rows = pl.ds(pl.multiple_of(mh * EXT + below * (ROWS + 8), 8), 8)
            ext[rows, :] = message[pl.ds(mh * 8, 8), :]
        ext[pl.ds(mh * EXT + 8, ROWS), :] = field_ref[pl.ds(mh * ROWS, ROWS), :]
    even = jnp.full((8, LANES), face_ref[0] & 1, I32) == 0
    for q in range(QUADS + 1):
        ones, twos = wide0_ref[pl.ds(q * 8, 8), :], wide1_ref[pl.ds(q * 8, 8), :]
        west[pl.ds(q * 16, 8), :] = jnp.where(even, twos, ones)
        west[pl.ds(q * 16 + 8, 8), :] = turned_ref[pl.ds(q * WIDTH, 8), :]
        east[pl.ds(q * 24, 16), :] = turned_ref[pl.ds(q * WIDTH + INNER, 16), :]
        east[pl.ds(q * 24 + 16, 8), :] = jnp.where(even, ones, twos)
    out_ref[...] = jnp.zeros_like(out_ref)
    first_row = tile_ref[0] * ROWS - RANGE

    def latitude(step, carry):
        half = step // 5
        block = step % 5
        base = pl.multiple_of(half * EXT + block * 8, 8)
        rows = row_ids() + (first_row + block * 8)
        sums = [jnp.zeros((8, LANES), F32)] * M
        for k in range(1, RANGE + 1):
            def diff(m):
                here = base + m * 2 * EXT
                return ext[pl.ds(here, 8), :] - ext[pl.ds(here + k, 8), :]

            total = jnp.zeros((8, LANES), F32)
            slopes = []
            for m in range(M):
                value, slope = steep(diff(m))
                total = total + value
                slopes.append(slope)
            seen, unused = steep(diff(M))
            inside = (rows >= 0) & (rows + k < ROWS * 32)
            push = jnp.where(inside, (1.0 / (k * M)) * (seen - total * (1.0 / M)), 0.0)
            for m in range(M):
                pushed = push * slopes[m]
                sums[m] = sums[m] - pushed + ending(kept_rows, (k - 1) * M + m, pushed, k)
        for m in range(M):
            grad[pl.ds(base + m * 2 * EXT, 8), :] = sums[m]
        return carry

    lax.fori_loop(0, 10, latitude, 0, unroll=2)

    added = [jnp.zeros((8, LANES), F32)] * QUADS
    for k, pushes in enumerate(column_pushes(lambda q, k: west[pl.ds(q * 16 + k, 8), :]), 1):
        for q in range(QUADS):
            added[q] = added[q] + jnp.where(row_ids() < k, pltpu.roll(pushes[q], k % 8, 0), 0.0)
    kept_columns[...] = kept_ref[...]
    near = column_sums(kept_columns, lambda q, k: east[pl.ds(q * 24 + k, 8), :])
    last = column_sums(kept_columns, lambda q, k: east[pl.ds(q * 24 + 8 + k, 8), :])

    for q in range(QUADS):
        first = turn_ref[pl.ds(q * WIDTH, 8), :] + added[q]
        halves = [
            jnp.concatenate([first, turn_ref[pl.ds(q * WIDTH + 8, LANES - 8), :]], axis=0),
            jnp.concatenate([turn_ref[pl.ds(q * WIDTH + LANES, INNER - LANES), :], near[q], last[q]], axis=0),
        ]
        for half in range(2):
            back = jnp.transpose(halves[half])
            for i in range(4):
                spot = ((4 * q + i) * 2 + half) * EXT + 8
                grad[pl.ds(spot, ROWS), :] += back[i * ROWS : (i + 1) * ROWS]

    cells = [(lax.broadcasted_iota(I32, (16, LANES), 0) + 16 * i).astype(F32).astype(BF16) for i in range(16)]
    one, zero = jnp.ones((16, LANES), BF16), jnp.zeros((16, LANES), BF16)

    def adjoint(row, carry):
        for half in range(2):
            tile = grad[pl.ds(half * EXT + 8 + row, M, stride=2 * EXT), :]
            parts, hots = [], []
            for j in range(POINTS):
                spot = j * BANDS + half * ROWS + row
                parts.append(tile * weight_ref[pl.ds(spot, 1), :])
                posn = jnp.broadcast_to(posn_ref[pl.ds(spot, 1), :].astype(F32), (16, LANES)).astype(BF16)
                hots.append(jnp.concatenate([jnp.where(c == posn, one, zero) for c in cells], axis=0))
            part = jnp.concatenate(parts, axis=1)
            high = part.astype(BF16)
            low = (part - high.astype(F32)).astype(BF16)
            both = lax.dot_general(
                jnp.concatenate([high, low], axis=0),
                jnp.concatenate(hots, axis=1),
                (((1,), (1,)), ((), ())),
                preferred_element_type=F32,
            )
            both = both[:M] + both[M:]
            for k in range(2):
                strip = both[:, k * LANES : (k + 1) * LANES]
                largest = jnp.maximum(jnp.max(jnp.abs(strip), axis=0, keepdims=True), 1e-36)
                scale = jnp.ceil(jnp.log2(largest) * 256.0)
                code = jnp.round(strip * (jnp.exp2(scale * (-1.0 / 256.0)) * TOP)).astype(I32)
                place = place_ref[k, 2 * row + half]
                spot = (place >> 1) * MESSAGE
                shift = (place & 1) * 16
                out_ref[pl.ds(spot, M), :] |= (code & 0xFFFF) << shift
                out_ref[pl.ds(spot + M, 1), :] |= (scale.astype(I32) & 0xFFFF) << shift
        return carry

    lax.fori_loop(0, ROWS, adjoint, 0, unroll=4)


def push(place, tile, face, *arrays):
    return pl.pallas_call(
        push_kernel,
        in_specs=[SMEM] * 3 + [VMEM] * len(arrays),
        out_shape=struct((DEVICES * MESSAGE, LANES), I32),
        scratch_shapes=[
            pltpu.VMEM((2 * (M + 1) * EXT, LANES), F32),
            pltpu.VMEM((2 * M * EXT, LANES), F32),
            pltpu.VMEM(((QUADS + 1) * 16, LANES), F32),
            pltpu.VMEM(((QUADS + 1) * 24, LANES), F32),
            pltpu.VMEM((RANGE * QUADS, 8, LANES), F32),
            pltpu.VMEM((RANGE * M, 8, LANES), F32),
        ],
        name="push",
        compiler_params=pltpu.CompilerParams(vmem_limit_bytes=6 << 20),
    )(place, tile, face, *arrays)


def collect_kernel(slots_ref, back_ref, out_ref, *sums):
    for part in sums:
        part[...] = jnp.zeros_like(part)

    def step(i, carry):
        codes = back_ref[pl.ds(i * MESSAGE, M), :]
        scales = back_ref[pl.ds(i * MESSAGE + M, 1), :]
        for r in range(2):
            code, scale = [((x << 16) if r == 0 else x) >> 16 for x in (codes, scales)]
            scale = jnp.exp2(scale.astype(F32) * (1.0 / 256.0)) * (1.0 / TOP)
            sums[r][slots_ref[r, i]] += code.astype(F32) * scale
        return carry

    lax.fori_loop(0, DEVICES, step, 0, unroll=8)

    def turn(s, carry):
        out_ref[pl.ds(s, M, stride=BANDS), :] = sums[0][s] + sums[1][s]
        return carry

    lax.fori_loop(0, BANDS, turn, 0, unroll=8)


def collect(slots, back):
    return pl.pallas_call(
        collect_kernel,
        in_specs=[SMEM, VMEM],
        out_shape=struct((M * BANDS, LANES)),
        scratch_shapes=[pltpu.VMEM((BANDS, M, LANES), F32)] * 2,
        name="collect",
        compiler_params=pltpu.CompilerParams(vmem_limit_bytes=5 << 20),
    )(slots, back)


def exchange(x):
    return lax.all_to_all(x, AXES, split_axis=0, concat_axis=0, tiled=True)


def local(predicted_field, parent_band_holder, parent_band_slot, neighbour_positions, unscaled_neighbour_factor, truth_field):
    tiles, faces = lax.axis_size("tile"), lax.axis_size("face")
    bands = jnp.transpose(predicted_field, (1, 0, 2))
    posn, weight = prepare(
        neighbour_positions.reshape(POINTS * BANDS, LANES),
        unscaled_neighbour_factor.reshape(POINTS * BANDS, LANES),
    )
    wanted, place = request(parent_band_holder.T, parent_band_slot.T)
    tile = lax.axis_index("tile").astype(I32).reshape(1)
    face = lax.axis_index("face").astype(I32).reshape(1)
    asked, posn, weight, tile, face = lax.optimization_barrier((exchange(wanted), posn, weight, tile, face))
    outgoing, slots = pack(asked, bands)
    recv = exchange(outgoing.reshape(DEVICES, 2, M, LANES)).reshape(2 * DEVICES, M, LANES)
    field, turned, *messages = regrid(place, tile, face, recv, posn, weight, truth_field)
    rounds = [
        ("tile", [(i, i + 1) for i in range(0, tiles - 1, 2)]),
        ("tile", [(i, i + 1) for i in range(1, tiles - 1, 2)]),
        ("face", [(i, i + 1) for i in range(0, faces, 2)]),
        ("face", [(i, (i + 1) % faces) for i in range(1, faces, 2)]),
    ]
    messages = [lax.ppermute(m, axis, pairs + [(j, i) for i, j in pairs]) for m, (axis, pairs) in zip(messages, rounds)]
    turn, kept = inner(turned)
    back = push(place, tile, face, field, turned, turn, kept, posn, weight, *messages)
    back = exchange(back.reshape(DEVICES, MESSAGE, 1, LANES)).reshape(DEVICES * MESSAGE, LANES)
    return collect(slots, back).reshape(M, BANDS, LANES)


def solution(mesh):
    in_specs = (
        P(None, AXES, None),
        P(AXES, None),
        P(AXES, None),
        P(None, AXES, None),
        P(None, AXES, None),
        P("tile", "face"),
    )
    return jax.shard_map(local, mesh=mesh, in_specs=in_specs, out_specs=P(None, AXES, None), check_vma=False)
```

```python
import jax
import jax.numpy as jnp
from jax import lax
from jax.experimental import pallas as pl
from jax.experimental.pallas import tpu as pltpu
from jax.sharding import PartitionSpec as P

RANGE = 8
FLOOR = 0.01
M = 16
BANDS = 64
LANES = 128
ROWS = 32
EXT = ROWS + 2 * RANGE
DEVICES = 128
POINTS = 4
TABLE = BANDS + 1
GRAD = 2 * EXT + 1
QUADS = M // 4
MESSAGE = M + 1
TOP = 32700.0
F32 = jnp.float32
I32 = jnp.int32
BF16 = jnp.bfloat16
AXES = ("face", "tile")


def struct(shape, dtype=F32):
    return jax.ShapeDtypeStruct(shape, dtype)


def lane_ids(rows=8):
    return lax.broadcasted_iota(I32, (rows, LANES), 1)


def row_ids(rows=8):
    return lax.broadcasted_iota(I32, (rows, LANES), 0)


def request_kernel(holder_hbm, slot_hbm, wanted_ref, place_ref, holder_ref, slot_ref, sems):
    copies = [
        pltpu.make_async_copy(holder_hbm, holder_ref, sems.at[0]),
        pltpu.make_async_copy(slot_hbm, slot_ref, sems.at[1]),
    ]
    for copy in copies:
        copy.start()
    for copy in copies:
        copy.wait()
    owner = lax.broadcasted_iota(I32, (DEVICES, BANDS), 0).astype(F32)
    band = lax.broadcasted_iota(I32, (1, BANDS), 1)
    big = float(1 << 20)
    hots, codes = [], []
    for k in range(2):
        holder = holder_ref[k : k + 1, :].astype(F32)
        code = (band + k * BANDS) * BANDS + slot_ref[k : k + 1, :]
        hots.append(holder == owner)
        codes.append(jnp.broadcast_to(code.astype(F32), (DEVICES, BANDS)))
    low = [jnp.min(jnp.where(h, c, big), axis=1, keepdims=True) for h, c in zip(hots, codes)]
    high = [jnp.max(jnp.where(h, c, -1.0), axis=1, keepdims=True) for h, c in zip(hots, codes)]
    first = jnp.minimum(low[0], low[1])
    last = jnp.maximum(high[0], high[1])
    slots = [
        jnp.where(last >= 0.0, first.astype(I32) & (BANDS - 1), 0),
        jnp.where(last > first, last.astype(I32) & (BANDS - 1), 0),
    ]
    lanes = lane_ids(DEVICES)
    wanted_ref[...] = jnp.where(lanes == 0, slots[0], jnp.where(lanes == 1, slots[1], 0))
    place_ref[...] = jnp.zeros((8, LANES), I32)
    for k in range(2):
        spot = 2.0 * owner + jnp.where(codes[k] == first, 0.0, 1.0)
        spot = jnp.sum(jnp.where(hots[k], spot, 0.0), axis=0, keepdims=True)
        place_ref[k : k + 1, :BANDS] = spot.astype(I32)


def request(holder, slot):
    return pl.pallas_call(
        request_kernel,
        in_specs=[pl.BlockSpec(memory_space=pl.ANY)] * 2,
        out_shape=(struct((DEVICES, LANES), I32), struct((8, LANES), I32)),
        scratch_shapes=[pltpu.VMEM((2, BANDS), I32)] * 2 + [pltpu.SemaphoreType.DMA((2,))],
        name="request",
    )(holder, slot)


def pack_kernel(asked_ref, bands_ref, out_ref, slots_ref, smem, sem):
    table = jnp.transpose(asked_ref[...].astype(F32))[:8].astype(I32)
    slots_ref[...] = table
    copy = pltpu.make_async_copy(slots_ref, smem, sem)
    copy.start()
    copy.wait()

    def step(i, carry):
        for r in range(2):
            out_ref[2 * i + r] = bands_ref[smem[r, i]]
        return carry

    lax.fori_loop(0, DEVICES, step, 0, unroll=8)


def pack(asked, bands):
    return pl.pallas_call(
        pack_kernel,
        out_shape=(struct((2 * DEVICES, M, LANES), BF16), struct((8, LANES), I32)),
        scratch_shapes=[pltpu.SMEM((8, LANES), I32), pltpu.SemaphoreType.DMA],
        name="pack",
        compiler_params=pltpu.CompilerParams(vmem_limit_bytes=4 << 20),
    )(asked, bands)


def prepare_kernel(pos_ref, factor_ref, posn_ref, weight_ref):
    for half in range(2):
        factors = [factor_ref[pl.ds(j * BANDS + half, ROWS, stride=2), :] for j in range(POINTS)]
        total = factors[0] + factors[1] + factors[2] + factors[3]
        for j in range(POINTS):
            spot = j * BANDS + half * ROWS
            posn_ref[pl.ds(spot, ROWS), :] = pos_ref[pl.ds(j * BANDS + half, ROWS, stride=2), :]
            weight_ref[pl.ds(spot, ROWS), :] = factors[j] / total


def prepare(pos, factor):
    return pl.pallas_call(
        prepare_kernel,
        out_shape=(
            struct((POINTS * BANDS, LANES), I32),
            struct((POINTS * BANDS, LANES)),
        ),
        name="prepare",
        cost_estimate=pl.CostEstimate(flops=1 << 20, bytes_accessed=1 << 20, transcendentals=0),
        compiler_params=pltpu.CompilerParams(vmem_limit_bytes=2 << 20),
    )(pos, factor)


def regrid_kernel(
    place_ref, tile_ref, face_ref, recv_ref, posn_ref, weight_ref, truth_ref,
    field_ref, turned_ref, tall0_ref, tall1_ref, wide0_ref, wide1_ref,
    low_ref, high_ref,
):
    def spread(row, carry):
        for half in range(2):
            for k, tab in enumerate((low_ref, high_ref)):
                strip = recv_ref[place_ref[k, 2 * row + half]].astype(F32)
                tab[pl.ds(half * ROWS + row, M, stride=TABLE), :] = strip
        return carry

    lax.fori_loop(0, ROWS, spread, 0, unroll=8)

    def regrid(block, carry):
        row = pl.multiple_of(block * 8, 8)
        posn = [posn_ref[pl.ds(j * BANDS + row, 8), :] for j in range(POINTS)]
        weight = [weight_ref[pl.ds(j * BANDS + row, 8), :] for j in range(POINTS)]
        sums = [jnp.zeros((8, LANES), F32)] * M
        for j in range(POINTS):
            lane, upper = posn[j] & (LANES - 1), posn[j] >= LANES
            for m in range(M):
                a, b = [
                    jnp.take_along_axis(tab[pl.ds(m * TABLE + row, 8), :], lane, axis=1, mode="promise_in_bounds")
                    for tab in (low_ref, high_ref)
                ]
                sums[m] = sums[m] + weight[j] * jnp.where(upper, b, a)
        for m in range(M):
            field_ref[pl.ds(m * BANDS + row, 8), :] = sums[m]
        return carry

    lax.fori_loop(0, BANDS // 8, regrid, 0)

    for half in range(2):
        field_ref[pl.ds(M * BANDS + half * ROWS, ROWS), :] = truth_ref[:, half * LANES : (half + 1) * LANES]
    odd = tile_ref[0] & 1
    for m in range(M + 1):
        for half in range(2):
            spot = m * BANDS + half * ROWS
            for message, edge in ((tall0_ref, 1 - odd), (tall1_ref, odd)):
                rows = pl.ds(pl.multiple_of(spot + edge * (ROWS - 8), 8), 8)
                message[pl.ds((2 * m + half) * 8, 8), :] = field_ref[rows, :]
    for q in range(QUADS + 1):
        for half in range(2):
            if q < QUADS:
                parts = [field_ref[pl.ds((4 * q + i) * BANDS + half * ROWS, ROWS), :] for i in range(4)]
            else:
                parts = [truth_ref[:, half * LANES : (half + 1) * LANES]] * 4
            turned = jnp.transpose(jnp.concatenate(parts, axis=0))
            turned_ref[pl.ds(q * 2 * LANES + half * LANES, LANES), :] = turned
    odd = face_ref[0] & 1
    for q in range(QUADS + 1):
        for message, edge in ((wide0_ref, 1 - odd), (wide1_ref, odd)):
            columns = pl.ds(pl.multiple_of(q * 2 * LANES + edge * (2 * LANES - 8), 8), 8)
            message[pl.ds(q * 8, 8), :] = turned_ref[columns, :]


VMEM = pl.BlockSpec(memory_space=pltpu.VMEM)
SMEM = pl.BlockSpec(memory_space=pltpu.SMEM)


def regrid(place, tile, face, recv, posn, weight, truth):
    tall = struct(((M + 1) * 2 * RANGE, LANES))
    wide = struct(((QUADS + 1) * RANGE, LANES))
    return pl.pallas_call(
        regrid_kernel,
        in_specs=[SMEM] * 3 + [VMEM] * 4,
        out_shape=(
            struct(((M + 1) * BANDS, LANES)),
            struct(((QUADS + 1) * 2 * LANES, LANES)),
            tall, tall, wide, wide,
        ),
        scratch_shapes=[pltpu.VMEM((M * TABLE, LANES), F32)] * 2,
        name="regrid",
        compiler_params=pltpu.CompilerParams(vmem_limit_bytes=8 << 20),
    )(place, tile, face, recv, posn, weight, truth)


def steep(diff):
    root = lax.rsqrt(diff * diff + FLOOR)
    value = lax.rsqrt(root)
    return value, (diff * root) * (value * root)


def column_pushes(rows):
    totals, slopes, sights = [], [], []
    for k in range(1, RANGE + 1):
        pairs = [steep(rows(q, 0) - rows(q, k)) for q in range(QUADS)]
        slopes.append([p[1] for p in pairs])
        totals.append((pairs[0][0] + pairs[1][0]) + (pairs[2][0] + pairs[3][0]))
        sights.append(steep(rows(QUADS, 0) - rows(QUADS, k))[0])
    totals = [t + pltpu.roll(t, 2 * ROWS, 1) for t in totals]
    totals = [t + pltpu.roll(t, ROWS, 1) for t in totals]
    pushes = []
    for k in range(1, RANGE + 1):
        push = (1.0 / (k * M)) * (sights[k - 1] - totals[k - 1] * (1.0 / M))
        pushes.append([push * slope for slope in slopes[k - 1]])
    return pushes


def ending(kept, spot, pushed, k):
    moved = pltpu.roll(pushed, k % 8, 0)
    earlier = kept[spot]
    kept[spot] = moved
    return jnp.where(row_ids() >= k, moved, earlier)


def column_sums(kept, rows):
    sums = [jnp.zeros((8, LANES), F32)] * QUADS
    for k, pushes in enumerate(column_pushes(rows), 1):
        for q in range(QUADS):
            sums[q] = sums[q] - pushes[q] + ending(kept, (k - 1) * QUADS + q, pushes[q], k)
    return sums


WIDTH = 2 * LANES
INNER = WIDTH - 2 * RANGE


def inner_kernel(turned_ref, turn_ref, kept_ref):
    kept_ref[...] = jnp.zeros_like(kept_ref)

    def block(b, carry):
        base = pl.multiple_of(b * 8, 8)
        sums = column_sums(kept_ref, lambda q, k: turned_ref[pl.ds(base + (q * WIDTH + k), 8), :])
        for q in range(QUADS):
            turn_ref[pl.ds(base + q * WIDTH, 8), :] = sums[q]
        return carry

    lax.fori_loop(0, INNER // 8, block, 0, unroll=3)


def inner(turned):
    return pl.pallas_call(
        inner_kernel,
        out_shape=(struct((QUADS * WIDTH, LANES)), struct((RANGE * QUADS, 8, LANES))),
        name="inner",
        cost_estimate=pl.CostEstimate(flops=16 << 20, bytes_accessed=12 << 20, transcendentals=2 << 20),
        compiler_params=pltpu.CompilerParams(vmem_limit_bytes=2 << 20),
    )(turned)


def push_kernel(
    place_ref, tile_ref, face_ref, field_ref, turned_ref, turn_ref, kept_ref, posn_ref, weight_ref,
    tall0_ref, tall1_ref, wide0_ref, wide1_ref,
    out_ref, ext, grad, west, east, kept_columns, kept_rows,
):
    odd = tile_ref[0] & 1
    for mh in range(2 * (M + 1)):
        for message, below in ((tall0_ref, 1 - odd), (tall1_ref, odd)):
            rows = pl.ds(pl.multiple_of(mh * EXT + below * (ROWS + 8), 8), 8)
            ext[rows, :] = message[pl.ds(mh * 8, 8), :]
        ext[pl.ds(mh * EXT + 8, ROWS), :] = field_ref[pl.ds(mh * ROWS, ROWS), :]
    even = jnp.full((8, LANES), face_ref[0] & 1, I32) == 0
    for q in range(QUADS + 1):
        ones, twos = wide0_ref[pl.ds(q * 8, 8), :], wide1_ref[pl.ds(q * 8, 8), :]
        west[pl.ds(q * 16, 8), :] = jnp.where(even, twos, ones)
        west[pl.ds(q * 16 + 8, 8), :] = turned_ref[pl.ds(q * WIDTH, 8), :]
        east[pl.ds(q * 24, 16), :] = turned_ref[pl.ds(q * WIDTH + INNER, 16), :]
        east[pl.ds(q * 24 + 16, 8), :] = jnp.where(even, ones, twos)
    out_ref[...] = jnp.zeros_like(out_ref)
    first_row = tile_ref[0] * ROWS - RANGE

    def latitude(step, carry):
        half = step // 5
        block = step % 5
        base = pl.multiple_of(half * EXT + block * 8, 8)
        rows = row_ids() + (first_row + block * 8)
        sums = [jnp.zeros((8, LANES), F32)] * M
        for k in range(1, RANGE + 1):
            def diff(m):
                here = base + m * 2 * EXT
                return ext[pl.ds(here, 8), :] - ext[pl.ds(here + k, 8), :]

            total = jnp.zeros((8, LANES), F32)
            slopes = []
            for m in range(M):
                value, slope = steep(diff(m))
                total = total + value
                slopes.append(slope)
            seen, unused = steep(diff(M))
            inside = (rows >= 0) & (rows + k < ROWS * 32)
            push = jnp.where(inside, (1.0 / (k * M)) * (seen - total * (1.0 / M)), 0.0)
            for m in range(M):
                pushed = push * slopes[m]
                sums[m] = sums[m] - pushed + ending(kept_rows, (k - 1) * M + m, pushed, k)
        for m in range(M):
            grad[pl.ds(base + m * GRAD, 8), :] = sums[m]
        return carry

    lax.fori_loop(0, 10, latitude, 0, unroll=2)

    added = [jnp.zeros((8, LANES), F32)] * QUADS
    for k, pushes in enumerate(column_pushes(lambda q, k: west[pl.ds(q * 16 + k, 8), :]), 1):
        for q in range(QUADS):
            added[q] = added[q] + jnp.where(row_ids() < k, pltpu.roll(pushes[q], k % 8, 0), 0.0)
    kept_columns[...] = kept_ref[...]
    near = column_sums(kept_columns, lambda q, k: east[pl.ds(q * 24 + k, 8), :])
    last = column_sums(kept_columns, lambda q, k: east[pl.ds(q * 24 + 8 + k, 8), :])

    for q in range(QUADS):
        first = turn_ref[pl.ds(q * WIDTH, 8), :] + added[q]
        halves = [
            jnp.concatenate([first, turn_ref[pl.ds(q * WIDTH + 8, LANES - 8), :]], axis=0),
            jnp.concatenate([turn_ref[pl.ds(q * WIDTH + LANES, INNER - LANES), :], near[q], last[q]], axis=0),
        ]
        for half in range(2):
            back = jnp.transpose(halves[half])
            for i in range(4):
                spot = (4 * q + i) * GRAD + half * EXT + 8
                grad[pl.ds(spot, ROWS), :] += back[i * ROWS : (i + 1) * ROWS]

    cells = [(lax.broadcasted_iota(I32, (16, LANES), 0) + 16 * i).astype(F32).astype(BF16) for i in range(16)]
    one, zero = jnp.ones((16, LANES), BF16), jnp.zeros((16, LANES), BF16)

    def adjoint(row, carry):
        for half in range(2):
            tile = grad[pl.ds(half * EXT + 8 + row, M, stride=GRAD), :]
            parts, hots = [], []
            for j in range(POINTS):
                spot = j * BANDS + half * ROWS + row
                parts.append(tile * weight_ref[pl.ds(spot, 1), :])
                posn = jnp.broadcast_to(posn_ref[pl.ds(spot, 1), :].astype(F32), (16, LANES)).astype(BF16)
                hots.append(jnp.concatenate([jnp.where(c == posn, one, zero) for c in cells], axis=0))
            part = jnp.concatenate(parts, axis=1)
            high = part.astype(BF16)
            low = (part - high.astype(F32)).astype(BF16)
            both = lax.dot_general(
                jnp.concatenate([high, low], axis=0),
                jnp.concatenate(hots, axis=1),
                (((1,), (1,)), ((), ())),
                preferred_element_type=F32,
            )
            both = both[:M] + both[M:]
            for k in range(2):
                strip = both[:, k * LANES : (k + 1) * LANES]
                largest = jnp.maximum(jnp.max(jnp.abs(strip), axis=0, keepdims=True), 1e-36)
                scale = jnp.ceil(jnp.log2(largest) * 256.0)
                code = jnp.round(strip * (jnp.exp2(scale * (-1.0 / 256.0)) * TOP)).astype(I32)
                place = place_ref[k, 2 * row + half]
                spot = (place >> 1) * MESSAGE
                shift = (place & 1) * 16
                out_ref[pl.ds(spot, M), :] |= (code & 0xFFFF) << shift
                out_ref[pl.ds(spot + M, 1), :] |= (scale.astype(I32) & 0xFFFF) << shift
        return carry

    lax.fori_loop(0, ROWS, adjoint, 0, unroll=4)


def push(place, tile, face, *arrays):
    return pl.pallas_call(
        push_kernel,
        in_specs=[SMEM] * 3 + [VMEM] * len(arrays),
        out_shape=struct((DEVICES * MESSAGE, LANES), I32),
        scratch_shapes=[
            pltpu.VMEM((2 * (M + 1) * EXT, LANES), F32),
            pltpu.VMEM((M * GRAD, LANES), F32),
            pltpu.VMEM(((QUADS + 1) * 16, LANES), F32),
            pltpu.VMEM(((QUADS + 1) * 24, LANES), F32),
            pltpu.VMEM((RANGE * QUADS, 8, LANES), F32),
            pltpu.VMEM((RANGE * M, 8, LANES), F32),
        ],
        name="push",
        compiler_params=pltpu.CompilerParams(vmem_limit_bytes=6 << 20),
    )(place, tile, face, *arrays)


def collect_kernel(slots_ref, back_ref, out_ref, *sums):
    for part in sums:
        part[...] = jnp.zeros_like(part)

    def step(i, carry):
        codes = back_ref[pl.ds(i * MESSAGE, M), :]
        scales = back_ref[pl.ds(i * MESSAGE + M, 1), :]
        for r in range(2):
            code, scale = [((x << 16) if r == 0 else x) >> 16 for x in (codes, scales)]
            scale = jnp.exp2(scale.astype(F32) * (1.0 / 256.0)) * (1.0 / TOP)
            sums[r][pl.ds(slots_ref[r, i] * MESSAGE, M), :] += code.astype(F32) * scale
        return carry

    lax.fori_loop(0, DEVICES, step, 0, unroll=8)

    def turn(block, carry):
        for m in range(M):
            where = pl.ds(block * 8 * MESSAGE + m, 8, stride=MESSAGE)
            out_ref[pl.ds(pl.multiple_of(m * BANDS + block * 8, 8), 8), :] = sums[0][where, :] + sums[1][where, :]
        return carry

    lax.fori_loop(0, BANDS // 8, turn, 0)


def collect(slots, back):
    return pl.pallas_call(
        collect_kernel,
        in_specs=[SMEM, VMEM],
        out_shape=struct((M * BANDS, LANES)),
        scratch_shapes=[pltpu.VMEM((BANDS * MESSAGE, LANES), F32)] * 2,
        name="collect",
        compiler_params=pltpu.CompilerParams(vmem_limit_bytes=5 << 20),
    )(slots, back)


def exchange(x):
    return lax.all_to_all(x, AXES, split_axis=0, concat_axis=0, tiled=True)


def local(predicted_field, parent_band_holder, parent_band_slot, neighbour_positions, unscaled_neighbour_factor, truth_field):
    tiles, faces = lax.axis_size("tile"), lax.axis_size("face")
    bands = jnp.transpose(predicted_field, (1, 0, 2))
    posn, weight = prepare(
        neighbour_positions.reshape(POINTS * BANDS, LANES),
        unscaled_neighbour_factor.reshape(POINTS * BANDS, LANES),
    )
    wanted, place = request(parent_band_holder.T, parent_band_slot.T)
    tile = lax.axis_index("tile").astype(I32).reshape(1)
    face = lax.axis_index("face").astype(I32).reshape(1)
    asked, posn, weight, tile, face = lax.optimization_barrier((exchange(wanted), posn, weight, tile, face))
    outgoing, slots = pack(asked, bands)
    recv = exchange(outgoing.reshape(DEVICES, 2, M, LANES)).reshape(2 * DEVICES, M, LANES)
    field, turned, *messages = regrid(place, tile, face, recv, posn, weight, truth_field)
    rounds = [
        ("tile", [(i, i + 1) for i in range(0, tiles - 1, 2)]),
        ("tile", [(i, i + 1) for i in range(1, tiles - 1, 2)]),
        ("face", [(i, i + 1) for i in range(0, faces, 2)]),
        ("face", [(i, (i + 1) % faces) for i in range(1, faces, 2)]),
    ]
    messages = [lax.ppermute(m, axis, pairs + [(j, i) for i, j in pairs]) for m, (axis, pairs) in zip(messages, rounds)]
    turn, kept = inner(turned)
    back = push(place, tile, face, field, turned, turn, kept, posn, weight, *messages)
    back = exchange(back.reshape(DEVICES, MESSAGE, 1, LANES)).reshape(DEVICES * MESSAGE, LANES)
    return collect(slots, back).reshape(M, BANDS, LANES)


def solution(mesh):
    in_specs = (
        P(None, AXES, None),
        P(AXES, None),
        P(AXES, None),
        P(None, AXES, None),
        P(None, AXES, None),
        P("tile", "face"),
    )
    return jax.shard_map(local, mesh=mesh, in_specs=in_specs, out_specs=P(None, AXES, None), check_vma=False)
```

```python
import jax
import jax.numpy as jnp
from jax import lax
from jax.experimental import pallas as pl
from jax.experimental.pallas import tpu as pltpu
from jax.sharding import PartitionSpec as P

RANGE = 8
FLOOR = 0.01
M = 16
BANDS = 64
LANES = 128
ROWS = 32
EXT = ROWS + 2 * RANGE
DEVICES = 128
POINTS = 4
TABLE = BANDS + 1
GRAD = 2 * EXT + 1
QUADS = M // 4
MESSAGE = M + 1
TOP = 32700.0
F32 = jnp.float32
I32 = jnp.int32
BF16 = jnp.bfloat16
AXES = ("face", "tile")


def struct(shape, dtype=F32):
    return jax.ShapeDtypeStruct(shape, dtype)


def lane_ids(rows=8):
    return lax.broadcasted_iota(I32, (rows, LANES), 1)


def row_ids(rows=8):
    return lax.broadcasted_iota(I32, (rows, LANES), 0)


def request_kernel(holder_hbm, slot_hbm, wanted_ref, place_ref, holder_ref, slot_ref, sems):
    copies = [
        pltpu.make_async_copy(holder_hbm, holder_ref, sems.at[0]),
        pltpu.make_async_copy(slot_hbm, slot_ref, sems.at[1]),
    ]
    for copy in copies:
        copy.start()
    for copy in copies:
        copy.wait()
    owner = lax.broadcasted_iota(I32, (DEVICES, BANDS), 0).astype(F32)
    band = lax.broadcasted_iota(I32, (1, BANDS), 1)
    big = float(1 << 20)
    hots, codes = [], []
    for k in range(2):
        holder = holder_ref[k : k + 1, :].astype(F32)
        code = (band + k * BANDS) * BANDS + slot_ref[k : k + 1, :]
        hots.append(holder == owner)
        codes.append(jnp.broadcast_to(code.astype(F32), (DEVICES, BANDS)))
    low = [jnp.min(jnp.where(h, c, big), axis=1, keepdims=True) for h, c in zip(hots, codes)]
    high = [jnp.max(jnp.where(h, c, -1.0), axis=1, keepdims=True) for h, c in zip(hots, codes)]
    first = jnp.minimum(low[0], low[1])
    last = jnp.maximum(high[0], high[1])
    slots = [
        jnp.where(last >= 0.0, first.astype(I32) & (BANDS - 1), 0),
        jnp.where(last > first, last.astype(I32) & (BANDS - 1), 0),
    ]
    lanes = lane_ids(DEVICES)
    wanted_ref[...] = jnp.where(lanes == 0, slots[0], jnp.where(lanes == 1, slots[1], 0))
    place_ref[...] = jnp.zeros((8, LANES), I32)
    for k in range(2):
        spot = 2.0 * owner + jnp.where(codes[k] == first, 0.0, 1.0)
        spot = jnp.sum(jnp.where(hots[k], spot, 0.0), axis=0, keepdims=True)
        place_ref[k : k + 1, :BANDS] = spot.astype(I32)


def request(holder, slot):
    return pl.pallas_call(
        request_kernel,
        in_specs=[pl.BlockSpec(memory_space=pl.ANY)] * 2,
        out_shape=(struct((DEVICES, LANES), I32), struct((8, LANES), I32)),
        scratch_shapes=[pltpu.VMEM((2, BANDS), I32)] * 2 + [pltpu.SemaphoreType.DMA((2,))],
        name="request",
    )(holder, slot)


def pack_kernel(asked_ref, bands_ref, out_ref, slots_ref, smem, sem):
    table = jnp.transpose(asked_ref[...].astype(F32))[:8].astype(I32)
    slots_ref[...] = table
    copy = pltpu.make_async_copy(slots_ref, smem, sem)
    copy.start()
    copy.wait()

    def step(i, carry):
        for r in range(2):
            out_ref[2 * i + r] = bands_ref[smem[r, i]]
        return carry

    lax.fori_loop(0, DEVICES, step, 0, unroll=8)


def pack(asked, bands):
    return pl.pallas_call(
        pack_kernel,
        out_shape=(struct((2 * DEVICES, M, LANES), BF16), struct((8, LANES), I32)),
        scratch_shapes=[pltpu.SMEM((8, LANES), I32), pltpu.SemaphoreType.DMA],
        name="pack",
        compiler_params=pltpu.CompilerParams(vmem_limit_bytes=4 << 20),
    )(asked, bands)


def regrid_kernel(
    place_ref, tile_ref, face_ref, recv_ref, pos_ref, factor_ref, truth_ref,
    field_ref, turned_ref, posn_ref, weight_ref, tall0_ref, tall1_ref, wide0_ref, wide1_ref,
    low_ref, high_ref,
):
    def spread(row, carry):
        for half in range(2):
            for k, tab in enumerate((low_ref, high_ref)):
                strip = recv_ref[place_ref[k, 2 * row + half]].astype(F32)
                tab[pl.ds(half * ROWS + row, M, stride=TABLE), :] = strip
        return carry

    lax.fori_loop(0, ROWS, spread, 0, unroll=8)

    for half in range(2):
        factors = [factor_ref[pl.ds(j * BANDS + half, ROWS, stride=2), :] for j in range(POINTS)]
        total = factors[0] + factors[1] + factors[2] + factors[3]
        for j in range(POINTS):
            spot = j * BANDS + half * ROWS
            posn_ref[pl.ds(spot, ROWS), :] = pos_ref[pl.ds(j * BANDS + half, ROWS, stride=2), :]
            weight_ref[pl.ds(spot, ROWS), :] = factors[j] / total

    def regrid(block, carry):
        row = pl.multiple_of(block * 8, 8)
        posn = [posn_ref[pl.ds(j * BANDS + row, 8), :] for j in range(POINTS)]
        weight = [weight_ref[pl.ds(j * BANDS + row, 8), :] for j in range(POINTS)]
        sums = [jnp.zeros((8, LANES), F32)] * M
        for j in range(POINTS):
            lane, upper = posn[j] & (LANES - 1), posn[j] >= LANES
            for m in range(M):
                a, b = [
                    jnp.take_along_axis(tab[pl.ds(m * TABLE + row, 8), :], lane, axis=1, mode="promise_in_bounds")
                    for tab in (low_ref, high_ref)
                ]
                sums[m] = sums[m] + weight[j] * jnp.where(upper, b, a)
        for m in range(M):
            field_ref[pl.ds(m * BANDS + row, 8), :] = sums[m]
        return carry

    lax.fori_loop(0, BANDS // 8, regrid, 0)

    for half in range(2):
        field_ref[pl.ds(M * BANDS + half * ROWS, ROWS), :] = truth_ref[:, half * LANES : (half + 1) * LANES]
    odd = tile_ref[0] & 1
    for m in range(M + 1):
        for half in range(2):
            spot = m * BANDS + half * ROWS
            for message, edge in ((tall0_ref, 1 - odd), (tall1_ref, odd)):
                rows = pl.ds(pl.multiple_of(spot + edge * (ROWS - 8), 8), 8)
                message[pl.ds((2 * m + half) * 8, 8), :] = field_ref[rows, :]
    for q in range(QUADS + 1):
        for half in range(2):
            if q < QUADS:
                parts = [field_ref[pl.ds((4 * q + i) * BANDS + half * ROWS, ROWS), :] for i in range(4)]
            else:
                parts = [truth_ref[:, half * LANES : (half + 1) * LANES]] * 4
            turned = jnp.transpose(jnp.concatenate(parts, axis=0))
            turned_ref[pl.ds(q * 2 * LANES + half * LANES, LANES), :] = turned
    odd = face_ref[0] & 1
    for q in range(QUADS + 1):
        for message, edge in ((wide0_ref, 1 - odd), (wide1_ref, odd)):
            columns = pl.ds(pl.multiple_of(q * 2 * LANES + edge * (2 * LANES - 8), 8), 8)
            message[pl.ds(q * 8, 8), :] = turned_ref[columns, :]


VMEM = pl.BlockSpec(memory_space=pltpu.VMEM)
SMEM = pl.BlockSpec(memory_space=pltpu.SMEM)


def regrid(place, tile, face, recv, pos, factor, truth):
    tall = struct(((M + 1) * 2 * RANGE, LANES))
    wide = struct(((QUADS + 1) * RANGE, LANES))
    return pl.pallas_call(
        regrid_kernel,
        in_specs=[SMEM] * 3 + [VMEM] * 4,
        out_shape=(
            struct(((M + 1) * BANDS, LANES)),
            struct(((QUADS + 1) * 2 * LANES, LANES)),
            struct((POINTS * BANDS, LANES), I32),
            struct((POINTS * BANDS, LANES)),
            tall, tall, wide, wide,
        ),
        scratch_shapes=[pltpu.VMEM((M * TABLE, LANES), F32)] * 2,
        name="regrid",
        compiler_params=pltpu.CompilerParams(vmem_limit_bytes=8 << 20),
    )(place, tile, face, recv, pos, factor, truth)


def steep(diff):
    root = lax.rsqrt(diff * diff + FLOOR)
    value = lax.rsqrt(root)
    return value, (diff * root) * (value * root)


def column_pushes(rows):
    totals, slopes, sights = [], [], []
    for k in range(1, RANGE + 1):
        pairs = [steep(rows(q, 0) - rows(q, k)) for q in range(QUADS)]
        slopes.append([p[1] for p in pairs])
        totals.append((pairs[0][0] + pairs[1][0]) + (pairs[2][0] + pairs[3][0]))
        sights.append(steep(rows(QUADS, 0) - rows(QUADS, k))[0])
    totals = [t + pltpu.roll(t, 2 * ROWS, 1) for t in totals]
    totals = [t + pltpu.roll(t, ROWS, 1) for t in totals]
    pushes = []
    for k in range(1, RANGE + 1):
        push = (1.0 / (k * M)) * (sights[k - 1] - totals[k - 1] * (1.0 / M))
        pushes.append([push * slope for slope in slopes[k - 1]])
    return pushes


def ending(kept, spot, pushed, k):
    moved = pltpu.roll(pushed, k % 8, 0)
    earlier = kept[spot]
    kept[spot] = moved
    return jnp.where(row_ids() >= k, moved, earlier)


def column_sums(kept, rows):
    sums = [jnp.zeros((8, LANES), F32)] * QUADS
    for k, pushes in enumerate(column_pushes(rows), 1):
        for q in range(QUADS):
            sums[q] = sums[q] - pushes[q] + ending(kept, (k - 1) * QUADS + q, pushes[q], k)
    return sums


WIDTH = 2 * LANES
INNER = WIDTH - 2 * RANGE


def inner_kernel(turned_ref, turn_ref, kept_ref):
    kept_ref[...] = jnp.zeros_like(kept_ref)

    def block(b, carry):
        base = pl.multiple_of(b * 8, 8)
        sums = column_sums(kept_ref, lambda q, k: turned_ref[pl.ds(base + (q * WIDTH + k), 8), :])
        for q in range(QUADS):
            turn_ref[pl.ds(base + q * WIDTH, 8), :] = sums[q]
        return carry

    lax.fori_loop(0, INNER // 8, block, 0, unroll=3)


def inner(turned):
    return pl.pallas_call(
        inner_kernel,
        out_shape=(struct((QUADS * WIDTH, LANES)), struct((RANGE * QUADS, 8, LANES))),
        name="inner",
        cost_estimate=pl.CostEstimate(flops=16 << 20, bytes_accessed=12 << 20, transcendentals=2 << 20),
        compiler_params=pltpu.CompilerParams(vmem_limit_bytes=2 << 20),
    )(turned)


def push_kernel(
    place_ref, tile_ref, face_ref, field_ref, turned_ref, turn_ref, kept_ref, posn_ref, weight_ref,
    tall0_ref, tall1_ref, wide0_ref, wide1_ref,
    out_ref, ext, grad, west, east, kept_columns, kept_rows,
):
    odd = tile_ref[0] & 1
    for mh in range(2 * (M + 1)):
        for message, below in ((tall0_ref, 1 - odd), (tall1_ref, odd)):
            rows = pl.ds(pl.multiple_of(mh * EXT + below * (ROWS + 8), 8), 8)
            ext[rows, :] = message[pl.ds(mh * 8, 8), :]
        ext[pl.ds(mh * EXT + 8, ROWS), :] = field_ref[pl.ds(mh * ROWS, ROWS), :]
    even = jnp.full((8, LANES), face_ref[0] & 1, I32) == 0
    for q in range(QUADS + 1):
        ones, twos = wide0_ref[pl.ds(q * 8, 8), :], wide1_ref[pl.ds(q * 8, 8), :]
        west[pl.ds(q * 16, 8), :] = jnp.where(even, twos, ones)
        west[pl.ds(q * 16 + 8, 8), :] = turned_ref[pl.ds(q * WIDTH, 8), :]
        east[pl.ds(q * 24, 16), :] = turned_ref[pl.ds(q * WIDTH + INNER, 16), :]
        east[pl.ds(q * 24 + 16, 8), :] = jnp.where(even, ones, twos)
    out_ref[...] = jnp.zeros_like(out_ref)
    first_row = tile_ref[0] * ROWS - RANGE

    def latitude(step, carry):
        half = step // 5
        block = step % 5
        base = pl.multiple_of(half * EXT + block * 8, 8)
        rows = row_ids() + (first_row + block * 8)
        sums = [jnp.zeros((8, LANES), F32)] * M
        for k in range(1, RANGE + 1):
            def diff(m):
                here = base + m * 2 * EXT
                return ext[pl.ds(here, 8), :] - ext[pl.ds(here + k, 8), :]

            total = jnp.zeros((8, LANES), F32)
            slopes = []
            for m in range(M):
                value, slope = steep(diff(m))
                total = total + value
                slopes.append(slope)
            seen, unused = steep(diff(M))
            inside = (rows >= 0) & (rows + k < ROWS * 32)
            push = jnp.where(inside, (1.0 / (k * M)) * (seen - total * (1.0 / M)), 0.0)
            for m in range(M):
                pushed = push * slopes[m]
                sums[m] = sums[m] - pushed + ending(kept_rows, (k - 1) * M + m, pushed, k)
        for m in range(M):
            grad[pl.ds(base + m * GRAD, 8), :] = sums[m]
        return carry

    lax.fori_loop(0, 10, latitude, 0, unroll=2)

    added = [jnp.zeros((8, LANES), F32)] * QUADS
    for k, pushes in enumerate(column_pushes(lambda q, k: west[pl.ds(q * 16 + k, 8), :]), 1):
        for q in range(QUADS):
            added[q] = added[q] + jnp.where(row_ids() < k, pltpu.roll(pushes[q], k % 8, 0), 0.0)
    kept_columns[...] = kept_ref[...]
    near = column_sums(kept_columns, lambda q, k: east[pl.ds(q * 24 + k, 8), :])
    last = column_sums(kept_columns, lambda q, k: east[pl.ds(q * 24 + 8 + k, 8), :])

    for q in range(QUADS):
        first = turn_ref[pl.ds(q * WIDTH, 8), :] + added[q]
        halves = [
            jnp.concatenate([first, turn_ref[pl.ds(q * WIDTH + 8, LANES - 8), :]], axis=0),
            jnp.concatenate([turn_ref[pl.ds(q * WIDTH + LANES, INNER - LANES), :], near[q], last[q]], axis=0),
        ]
        for half in range(2):
            back = jnp.transpose(halves[half])
            for i in range(4):
                spot = (4 * q + i) * GRAD + half * EXT + 8
                grad[pl.ds(spot, ROWS), :] += back[i * ROWS : (i + 1) * ROWS]

    cells = [(lax.broadcasted_iota(I32, (16, LANES), 0) + 16 * i).astype(F32).astype(BF16) for i in range(16)]
    one, zero = jnp.ones((16, LANES), BF16), jnp.zeros((16, LANES), BF16)

    def adjoint(row, carry):
        for half in range(2):
            tile = grad[pl.ds(half * EXT + 8 + row, M, stride=GRAD), :]
            parts, hots = [], []
            for j in range(POINTS):
                spot = j * BANDS + half * ROWS + row
                parts.append(tile * weight_ref[pl.ds(spot, 1), :])
                posn = jnp.broadcast_to(posn_ref[pl.ds(spot, 1), :].astype(F32), (16, LANES)).astype(BF16)
                hots.append(jnp.concatenate([jnp.where(c == posn, one, zero) for c in cells], axis=0))
            part = jnp.concatenate(parts, axis=1)
            high = part.astype(BF16)
            low = (part - high.astype(F32)).astype(BF16)
            both = lax.dot_general(
                jnp.concatenate([high, low], axis=0),
                jnp.concatenate(hots, axis=1),
                (((1,), (1,)), ((), ())),
                preferred_element_type=F32,
            )
            both = both[:M] + both[M:]
            for k in range(2):
                strip = both[:, k * LANES : (k + 1) * LANES]
                largest = jnp.maximum(jnp.max(jnp.abs(strip), axis=0, keepdims=True), 1e-36)
                scale = jnp.ceil(jnp.log2(largest) * 256.0)
                code = jnp.round(strip * (jnp.exp2(scale * (-1.0 / 256.0)) * TOP)).astype(I32)
                place = place_ref[k, 2 * row + half]
                spot = (place >> 1) * MESSAGE
                shift = (place & 1) * 16
                out_ref[pl.ds(spot, M), :] |= (code & 0xFFFF) << shift
                out_ref[pl.ds(spot + M, 1), :] |= (scale.astype(I32) & 0xFFFF) << shift
        return carry

    lax.fori_loop(0, ROWS, adjoint, 0, unroll=4)


def push(place, tile, face, *arrays):
    return pl.pallas_call(
        push_kernel,
        in_specs=[SMEM] * 3 + [VMEM] * len(arrays),
        out_shape=struct((DEVICES * MESSAGE, LANES), I32),
        scratch_shapes=[
            pltpu.VMEM((2 * (M + 1) * EXT, LANES), F32),
            pltpu.VMEM((M * GRAD, LANES), F32),
            pltpu.VMEM(((QUADS + 1) * 16, LANES), F32),
            pltpu.VMEM(((QUADS + 1) * 24, LANES), F32),
            pltpu.VMEM((RANGE * QUADS, 8, LANES), F32),
            pltpu.VMEM((RANGE * M, 8, LANES), F32),
        ],
        name="push",
        compiler_params=pltpu.CompilerParams(vmem_limit_bytes=6 << 20),
    )(place, tile, face, *arrays)


def collect_kernel(slots_ref, back_ref, out_ref, *sums):
    for part in sums:
        part[...] = jnp.zeros_like(part)

    def step(i, carry):
        codes = back_ref[pl.ds(i * MESSAGE, M), :]
        scales = back_ref[pl.ds(i * MESSAGE + M, 1), :]
        for r in range(2):
            code, scale = [((x << 16) if r == 0 else x) >> 16 for x in (codes, scales)]
            scale = jnp.exp2(scale.astype(F32) * (1.0 / 256.0)) * (1.0 / TOP)
            sums[r][pl.ds(slots_ref[r, i] * MESSAGE, M), :] += code.astype(F32) * scale
        return carry

    lax.fori_loop(0, DEVICES, step, 0, unroll=8)

    def turn(block, carry):
        for m in range(M):
            where = pl.ds(block * 8 * MESSAGE + m, 8, stride=MESSAGE)
            out_ref[pl.ds(pl.multiple_of(m * BANDS + block * 8, 8), 8), :] = sums[0][where, :] + sums[1][where, :]
        return carry

    lax.fori_loop(0, BANDS // 8, turn, 0)


def collect(slots, back):
    return pl.pallas_call(
        collect_kernel,
        in_specs=[SMEM, VMEM],
        out_shape=struct((M * BANDS, LANES)),
        scratch_shapes=[pltpu.VMEM((BANDS * MESSAGE, LANES), F32)] * 2,
        name="collect",
        compiler_params=pltpu.CompilerParams(vmem_limit_bytes=5 << 20),
    )(slots, back)


def exchange(x):
    return lax.all_to_all(x, AXES, split_axis=0, concat_axis=0, tiled=True)


def local(predicted_field, parent_band_holder, parent_band_slot, neighbour_positions, unscaled_neighbour_factor, truth_field):
    tiles, faces = lax.axis_size("tile"), lax.axis_size("face")
    bands = jnp.transpose(predicted_field, (1, 0, 2))
    wanted, place = request(parent_band_holder.T, parent_band_slot.T)
    tile = lax.axis_index("tile").astype(I32).reshape(1)
    face = lax.axis_index("face").astype(I32).reshape(1)
    asked, tile, face = lax.optimization_barrier((exchange(wanted), tile, face))
    outgoing, slots = pack(asked, bands)
    recv = exchange(outgoing.reshape(DEVICES, 2, M, LANES)).reshape(2 * DEVICES, M, LANES)
    field, turned, posn, weight, *messages = regrid(
        place,
        tile,
        face,
        recv,
        neighbour_positions.reshape(POINTS * BANDS, LANES),
        unscaled_neighbour_factor.reshape(POINTS * BANDS, LANES),
        truth_field,
    )
    rounds = [
        ("tile", [(i, i + 1) for i in range(0, tiles - 1, 2)]),
        ("tile", [(i, i + 1) for i in range(1, tiles - 1, 2)]),
        ("face", [(i, i + 1) for i in range(0, faces, 2)]),
        ("face", [(i, (i + 1) % faces) for i in range(1, faces, 2)]),
    ]
    messages = [lax.ppermute(m, axis, pairs + [(j, i) for i, j in pairs]) for m, (axis, pairs) in zip(messages, rounds)]
    turn, kept = inner(turned)
    back = push(place, tile, face, field, turned, turn, kept, posn, weight, *messages)
    back = exchange(back.reshape(DEVICES, MESSAGE, 1, LANES)).reshape(DEVICES * MESSAGE, LANES)
    return collect(slots, back).reshape(M, BANDS, LANES)


def solution(mesh):
    in_specs = (
        P(None, AXES, None),
        P(AXES, None),
        P(AXES, None),
        P(None, AXES, None),
        P(None, AXES, None),
        P("tile", "face"),
    )
    return jax.shard_map(local, mesh=mesh, in_specs=in_specs, out_specs=P(None, AXES, None), check_vma=False)
```

```python
import jax
import jax.numpy as jnp
from jax import lax
from jax.experimental import pallas as pl
from jax.experimental.pallas import tpu as pltpu
from jax.sharding import PartitionSpec as P

RANGE = 8
FLOOR = 0.01
M = 16
BANDS = 64
LANES = 128
ROWS = 32
EXT = ROWS + 2 * RANGE
DEVICES = 128
POINTS = 4
TABLE = BANDS + 1
GRAD = 2 * EXT + 1
QUADS = M // 4
MESSAGE = M + 1
TOP = 32700.0
F32 = jnp.float32
I32 = jnp.int32
BF16 = jnp.bfloat16
AXES = ("face", "tile")


def struct(shape, dtype=F32):
    return jax.ShapeDtypeStruct(shape, dtype)


def lane_ids(rows=8):
    return lax.broadcasted_iota(I32, (rows, LANES), 1)


def row_ids(rows=8):
    return lax.broadcasted_iota(I32, (rows, LANES), 0)


def request_kernel(holder_hbm, slot_hbm, wanted_ref, place_ref, holder_ref, slot_ref, sems):
    copies = [
        pltpu.make_async_copy(holder_hbm, holder_ref, sems.at[0]),
        pltpu.make_async_copy(slot_hbm, slot_ref, sems.at[1]),
    ]
    for copy in copies:
        copy.start()
    for copy in copies:
        copy.wait()
    owner = lax.broadcasted_iota(I32, (DEVICES, BANDS), 0).astype(F32)
    band = lax.broadcasted_iota(I32, (1, BANDS), 1)
    big = float(1 << 20)
    hots, codes = [], []
    for k in range(2):
        holder = holder_ref[k : k + 1, :].astype(F32)
        code = (band + k * BANDS) * BANDS + slot_ref[k : k + 1, :]
        hots.append(holder == owner)
        codes.append(jnp.broadcast_to(code.astype(F32), (DEVICES, BANDS)))
    low = [jnp.min(jnp.where(h, c, big), axis=1, keepdims=True) for h, c in zip(hots, codes)]
    high = [jnp.max(jnp.where(h, c, -1.0), axis=1, keepdims=True) for h, c in zip(hots, codes)]
    first = jnp.minimum(low[0], low[1])
    last = jnp.maximum(high[0], high[1])
    slots = [
        jnp.where(last >= 0.0, first.astype(I32) & (BANDS - 1), 0),
        jnp.where(last > first, last.astype(I32) & (BANDS - 1), 0),
    ]
    lanes = lane_ids(DEVICES)
    wanted_ref[...] = jnp.where(lanes == 0, slots[0], jnp.where(lanes == 1, slots[1], 0))
    place_ref[...] = jnp.zeros((8, LANES), I32)
    for k in range(2):
        spot = 2.0 * owner + jnp.where(codes[k] == first, 0.0, 1.0)
        spot = jnp.sum(jnp.where(hots[k], spot, 0.0), axis=0, keepdims=True)
        place_ref[k : k + 1, :BANDS] = spot.astype(I32)


def request(holder, slot):
    return pl.pallas_call(
        request_kernel,
        in_specs=[pl.BlockSpec(memory_space=pl.ANY)] * 2,
        out_shape=(struct((DEVICES, LANES), I32), struct((8, LANES), I32)),
        scratch_shapes=[pltpu.VMEM((2, BANDS), I32)] * 2 + [pltpu.SemaphoreType.DMA((2,))],
        name="request",
    )(holder, slot)


def pack_kernel(asked_ref, bands_ref, out_ref, slots_ref, smem, sem):
    table = jnp.transpose(asked_ref[...].astype(F32))[:8].astype(I32)
    slots_ref[...] = table
    copy = pltpu.make_async_copy(slots_ref, smem, sem)
    copy.start()
    copy.wait()

    def step(i, carry):
        for r in range(2):
            out_ref[2 * i + r] = bands_ref[smem[r, i]]
        return carry

    lax.fori_loop(0, DEVICES, step, 0, unroll=8)


def pack(asked, bands):
    return pl.pallas_call(
        pack_kernel,
        out_shape=(struct((2 * DEVICES, M, LANES), BF16), struct((8, LANES), I32)),
        scratch_shapes=[pltpu.SMEM((8, LANES), I32), pltpu.SemaphoreType.DMA],
        name="pack",
        compiler_params=pltpu.CompilerParams(vmem_limit_bytes=4 << 20),
    )(asked, bands)


def prepare_kernel(pos_ref, factor_ref, posn_ref, weight_ref):
    for half in range(2):
        factors = [factor_ref[pl.ds(j * BANDS + half, ROWS, stride=2), :] for j in range(POINTS)]
        total = factors[0] + factors[1] + factors[2] + factors[3]
        for j in range(POINTS):
            spot = j * BANDS + half * ROWS
            posn_ref[pl.ds(spot, ROWS), :] = pos_ref[pl.ds(j * BANDS + half, ROWS, stride=2), :]
            weight_ref[pl.ds(spot, ROWS), :] = factors[j] / total


def prepare(pos, factor):
    return pl.pallas_call(
        prepare_kernel,
        out_shape=(
            struct((POINTS * BANDS, LANES), I32),
            struct((POINTS * BANDS, LANES)),
        ),
        name="prepare",
        cost_estimate=pl.CostEstimate(flops=1 << 20, bytes_accessed=1 << 20, transcendentals=0),
        compiler_params=pltpu.CompilerParams(vmem_limit_bytes=2 << 20),
    )(pos, factor)


def regrid_kernel(
    place_ref, tile_ref, face_ref, recv_ref, posn_ref, weight_ref, truth_ref,
    field_ref, turned_ref, tall0_ref, tall1_ref, wide0_ref, wide1_ref,
    low_ref, high_ref,
):
    def spread(row, carry):
        for half in range(2):
            for k, tab in enumerate((low_ref, high_ref)):
                strip = recv_ref[place_ref[k, 2 * row + half]].astype(F32)
                tab[pl.ds(half * ROWS + row, M, stride=TABLE), :] = strip
        return carry

    lax.fori_loop(0, ROWS, spread, 0, unroll=8)

    def regrid(block, carry):
        row = pl.multiple_of(block * 8, 8)
        posn = [posn_ref[pl.ds(j * BANDS + row, 8), :] for j in range(POINTS)]
        weight = [weight_ref[pl.ds(j * BANDS + row, 8), :] for j in range(POINTS)]
        sums = [jnp.zeros((8, LANES), F32)] * M
        for j in range(POINTS):
            lane, upper = posn[j] & (LANES - 1), posn[j] >= LANES
            for m in range(M):
                a, b = [
                    jnp.take_along_axis(tab[pl.ds(m * TABLE + row, 8), :], lane, axis=1, mode="promise_in_bounds")
                    for tab in (low_ref, high_ref)
                ]
                sums[m] = sums[m] + weight[j] * jnp.where(upper, b, a)
        for m in range(M):
            field_ref[pl.ds(m * BANDS + row, 8), :] = sums[m]
        return carry

    lax.fori_loop(0, BANDS // 8, regrid, 0)

    for half in range(2):
        field_ref[pl.ds(M * BANDS + half * ROWS, ROWS), :] = truth_ref[:, half * LANES : (half + 1) * LANES]
    odd = 1 - (tile_ref[0] & 1)
    for m in range(M + 1):
        for half in range(2):
            spot = m * BANDS + half * ROWS
            for message, edge in ((tall0_ref, 1 - odd), (tall1_ref, odd)):
                rows = pl.ds(pl.multiple_of(spot + edge * (ROWS - 8), 8), 8)
                message[pl.ds((2 * m + half) * 8, 8), :] = field_ref[rows, :]
    for q in range(QUADS + 1):
        for half in range(2):
            if q < QUADS:
                parts = [field_ref[pl.ds((4 * q + i) * BANDS + half * ROWS, ROWS), :] for i in range(4)]
            else:
                parts = [truth_ref[:, half * LANES : (half + 1) * LANES]] * 4
            turned = jnp.transpose(jnp.concatenate(parts, axis=0))
            turned_ref[pl.ds(q * 2 * LANES + half * LANES, LANES), :] = turned
    odd = 1 - (face_ref[0] & 1)
    for q in range(QUADS + 1):
        for message, edge in ((wide0_ref, 1 - odd), (wide1_ref, odd)):
            columns = pl.ds(pl.multiple_of(q * 2 * LANES + edge * (2 * LANES - 8), 8), 8)
            message[pl.ds(q * 8, 8), :] = turned_ref[columns, :]


VMEM = pl.BlockSpec(memory_space=pltpu.VMEM)
SMEM = pl.BlockSpec(memory_space=pltpu.SMEM)


def regrid(place, tile, face, recv, posn, weight, truth):
    tall = struct(((M + 1) * 2 * RANGE, LANES))
    wide = struct(((QUADS + 1) * RANGE, LANES))
    return pl.pallas_call(
        regrid_kernel,
        in_specs=[SMEM] * 3 + [VMEM] * 4,
        out_shape=(
            struct(((M + 1) * BANDS, LANES)),
            struct(((QUADS + 1) * 2 * LANES, LANES)),
            tall, tall, wide, wide,
        ),
        scratch_shapes=[pltpu.VMEM((M * TABLE, LANES), F32)] * 2,
        name="regrid",
        compiler_params=pltpu.CompilerParams(vmem_limit_bytes=8 << 20),
    )(place, tile, face, recv, posn, weight, truth)


def steep(diff):
    root = lax.rsqrt(diff * diff + FLOOR)
    value = lax.rsqrt(root)
    return value, (diff * root) * (value * root)


def column_pushes(rows):
    totals, slopes, sights = [], [], []
    for k in range(1, RANGE + 1):
        pairs = [steep(rows(q, 0) - rows(q, k)) for q in range(QUADS)]
        slopes.append([p[1] for p in pairs])
        totals.append((pairs[0][0] + pairs[1][0]) + (pairs[2][0] + pairs[3][0]))
        sights.append(steep(rows(QUADS, 0) - rows(QUADS, k))[0])
    totals = [t + pltpu.roll(t, 2 * ROWS, 1) for t in totals]
    totals = [t + pltpu.roll(t, ROWS, 1) for t in totals]
    pushes = []
    for k in range(1, RANGE + 1):
        push = (1.0 / (k * M)) * (sights[k - 1] - totals[k - 1] * (1.0 / M))
        pushes.append([push * slope for slope in slopes[k - 1]])
    return pushes


def ending(kept, spot, pushed, k):
    moved = pltpu.roll(pushed, k % 8, 0)
    earlier = kept[spot]
    kept[spot] = moved
    return jnp.where(row_ids() >= k, moved, earlier)


def column_sums(kept, rows):
    sums = [jnp.zeros((8, LANES), F32)] * QUADS
    for k, pushes in enumerate(column_pushes(rows), 1):
        for q in range(QUADS):
            sums[q] = sums[q] - pushes[q] + ending(kept, (k - 1) * QUADS + q, pushes[q], k)
    return sums


WIDTH = 2 * LANES
INNER = WIDTH - 2 * RANGE


def inner_kernel(turned_ref, turn_ref, kept_ref):
    kept_ref[...] = jnp.zeros_like(kept_ref)

    def block(b, carry):
        base = pl.multiple_of(b * 8, 8)
        sums = column_sums(kept_ref, lambda q, k: turned_ref[pl.ds(base + (q * WIDTH + k), 8), :])
        for q in range(QUADS):
            turn_ref[pl.ds(base + q * WIDTH, 8), :] = sums[q]
        return carry

    lax.fori_loop(0, INNER // 8, block, 0, unroll=3)


def inner(turned):
    return pl.pallas_call(
        inner_kernel,
        out_shape=(struct((QUADS * WIDTH, LANES)), struct((RANGE * QUADS, 8, LANES))),
        name="inner",
        cost_estimate=pl.CostEstimate(flops=16 << 20, bytes_accessed=12 << 20, transcendentals=2 << 20),
        compiler_params=pltpu.CompilerParams(vmem_limit_bytes=2 << 20),
    )(turned)


def push_kernel(
    place_ref, tile_ref, face_ref, field_ref, turned_ref, turn_ref, kept_ref, posn_ref, weight_ref,
    tall0_ref, tall1_ref, wide0_ref, wide1_ref,
    out_ref, ext, grad, west, east, kept_columns, kept_rows,
):
    odd = 1 - (tile_ref[0] & 1)
    for mh in range(2 * (M + 1)):
        for message, below in ((tall0_ref, 1 - odd), (tall1_ref, odd)):
            rows = pl.ds(pl.multiple_of(mh * EXT + below * (ROWS + 8), 8), 8)
            ext[rows, :] = message[pl.ds(mh * 8, 8), :]
        ext[pl.ds(mh * EXT + 8, ROWS), :] = field_ref[pl.ds(mh * ROWS, ROWS), :]
    even = jnp.full((8, LANES), face_ref[0] & 1, I32) == 1
    for q in range(QUADS + 1):
        ones, twos = wide0_ref[pl.ds(q * 8, 8), :], wide1_ref[pl.ds(q * 8, 8), :]
        west[pl.ds(q * 16, 8), :] = jnp.where(even, twos, ones)
        west[pl.ds(q * 16 + 8, 8), :] = turned_ref[pl.ds(q * WIDTH, 8), :]
        east[pl.ds(q * 24, 16), :] = turned_ref[pl.ds(q * WIDTH + INNER, 16), :]
        east[pl.ds(q * 24 + 16, 8), :] = jnp.where(even, ones, twos)
    out_ref[...] = jnp.zeros_like(out_ref)
    first_row = tile_ref[0] * ROWS - RANGE

    def latitude(step, carry):
        half = step // 5
        block = step % 5
        base = pl.multiple_of(half * EXT + block * 8, 8)
        rows = row_ids() + (first_row + block * 8)
        sums = [jnp.zeros((8, LANES), F32)] * M
        for k in range(1, RANGE + 1):
            def diff(m):
                here = base + m * 2 * EXT
                return ext[pl.ds(here, 8), :] - ext[pl.ds(here + k, 8), :]

            total = jnp.zeros((8, LANES), F32)
            slopes = []
            for m in range(M):
                value, slope = steep(diff(m))
                total = total + value
                slopes.append(slope)
            seen, unused = steep(diff(M))
            inside = (rows >= 0) & (rows + k < ROWS * 32)
            push = jnp.where(inside, (1.0 / (k * M)) * (seen - total * (1.0 / M)), 0.0)
            for m in range(M):
                pushed = push * slopes[m]
                sums[m] = sums[m] - pushed + ending(kept_rows, (k - 1) * M + m, pushed, k)
        for m in range(M):
            grad[pl.ds(base + m * GRAD, 8), :] = sums[m]
        return carry

    lax.fori_loop(0, 10, latitude, 0, unroll=2)

    added = [jnp.zeros((8, LANES), F32)] * QUADS
    for k, pushes in enumerate(column_pushes(lambda q, k: west[pl.ds(q * 16 + k, 8), :]), 1):
        for q in range(QUADS):
            added[q] = added[q] + jnp.where(row_ids() < k, pltpu.roll(pushes[q], k % 8, 0), 0.0)
    kept_columns[...] = kept_ref[...]
    near = column_sums(kept_columns, lambda q, k: east[pl.ds(q * 24 + k, 8), :])
    last = column_sums(kept_columns, lambda q, k: east[pl.ds(q * 24 + 8 + k, 8), :])

    for q in range(QUADS):
        first = turn_ref[pl.ds(q * WIDTH, 8), :] + added[q]
        halves = [
            jnp.concatenate([first, turn_ref[pl.ds(q * WIDTH + 8, LANES - 8), :]], axis=0),
            jnp.concatenate([turn_ref[pl.ds(q * WIDTH + LANES, INNER - LANES), :], near[q], last[q]], axis=0),
        ]
        for half in range(2):
            back = jnp.transpose(halves[half])
            for i in range(4):
                spot = (4 * q + i) * GRAD + half * EXT + 8
                grad[pl.ds(spot, ROWS), :] += back[i * ROWS : (i + 1) * ROWS]

    cells = [(lax.broadcasted_iota(I32, (16, LANES), 0) + 16 * i).astype(F32).astype(BF16) for i in range(16)]
    one, zero = jnp.ones((16, LANES), BF16), jnp.zeros((16, LANES), BF16)

    def adjoint(row, carry):
        for half in range(2):
            tile = grad[pl.ds(half * EXT + 8 + row, M, stride=GRAD), :]
            parts, hots = [], []
            for j in range(POINTS):
                spot = j * BANDS + half * ROWS + row
                parts.append(tile * weight_ref[pl.ds(spot, 1), :])
                posn = jnp.broadcast_to(posn_ref[pl.ds(spot, 1), :].astype(F32), (16, LANES)).astype(BF16)
                hots.append(jnp.concatenate([jnp.where(c == posn, one, zero) for c in cells], axis=0))
            part = jnp.concatenate(parts, axis=1)
            high = part.astype(BF16)
            low = (part - high.astype(F32)).astype(BF16)
            both = lax.dot_general(
                jnp.concatenate([high, low], axis=0),
                jnp.concatenate(hots, axis=1),
                (((1,), (1,)), ((), ())),
                preferred_element_type=F32,
            )
            both = both[:M] + both[M:]
            for k in range(2):
                strip = both[:, k * LANES : (k + 1) * LANES]
                largest = jnp.maximum(jnp.max(jnp.abs(strip), axis=0, keepdims=True), 1e-36)
                scale = jnp.ceil(jnp.log2(largest) * 256.0)
                code = jnp.round(strip * (jnp.exp2(scale * (-1.0 / 256.0)) * TOP)).astype(I32)
                place = place_ref[k, 2 * row + half]
                spot = (place >> 1) * MESSAGE
                shift = (place & 1) * 16
                out_ref[pl.ds(spot, M), :] |= (code & 0xFFFF) << shift
                out_ref[pl.ds(spot + M, 1), :] |= (scale.astype(I32) & 0xFFFF) << shift
        return carry

    lax.fori_loop(0, ROWS, adjoint, 0, unroll=4)


def push(place, tile, face, *arrays):
    return pl.pallas_call(
        push_kernel,
        in_specs=[SMEM] * 3 + [VMEM] * len(arrays),
        out_shape=struct((DEVICES * MESSAGE, LANES), I32),
        scratch_shapes=[
            pltpu.VMEM((2 * (M + 1) * EXT, LANES), F32),
            pltpu.VMEM((M * GRAD, LANES), F32),
            pltpu.VMEM(((QUADS + 1) * 16, LANES), F32),
            pltpu.VMEM(((QUADS + 1) * 24, LANES), F32),
            pltpu.VMEM((RANGE * QUADS, 8, LANES), F32),
            pltpu.VMEM((RANGE * M, 8, LANES), F32),
        ],
        name="push",
        compiler_params=pltpu.CompilerParams(vmem_limit_bytes=6 << 20),
    )(place, tile, face, *arrays)


def collect_kernel(slots_ref, back_ref, out_ref, *sums):
    for part in sums:
        part[...] = jnp.zeros_like(part)

    def step(i, carry):
        codes = back_ref[pl.ds(i * MESSAGE, M), :]
        scales = back_ref[pl.ds(i * MESSAGE + M, 1), :]
        for r in range(2):
            code, scale = [((x << 16) if r == 0 else x) >> 16 for x in (codes, scales)]
            scale = jnp.exp2(scale.astype(F32) * (1.0 / 256.0)) * (1.0 / TOP)
            sums[r][pl.ds(slots_ref[r, i] * MESSAGE, M), :] += code.astype(F32) * scale
        return carry

    lax.fori_loop(0, DEVICES, step, 0, unroll=8)

    def turn(block, carry):
        for m in range(M):
            where = pl.ds(block * 8 * MESSAGE + m, 8, stride=MESSAGE)
            out_ref[pl.ds(pl.multiple_of(m * BANDS + block * 8, 8), 8), :] = sums[0][where, :] + sums[1][where, :]
        return carry

    lax.fori_loop(0, BANDS // 8, turn, 0)


def collect(slots, back):
    return pl.pallas_call(
        collect_kernel,
        in_specs=[SMEM, VMEM],
        out_shape=struct((M * BANDS, LANES)),
        scratch_shapes=[pltpu.VMEM((BANDS * MESSAGE, LANES), F32)] * 2,
        name="collect",
        compiler_params=pltpu.CompilerParams(vmem_limit_bytes=5 << 20),
    )(slots, back)


def exchange(x):
    return lax.all_to_all(x, AXES, split_axis=0, concat_axis=0, tiled=True)


def local(predicted_field, parent_band_holder, parent_band_slot, neighbour_positions, unscaled_neighbour_factor, truth_field):
    tiles, faces = lax.axis_size("tile"), lax.axis_size("face")
    bands = jnp.transpose(predicted_field, (1, 0, 2))
    posn, weight = prepare(
        neighbour_positions.reshape(POINTS * BANDS, LANES),
        unscaled_neighbour_factor.reshape(POINTS * BANDS, LANES),
    )
    wanted, place = request(parent_band_holder.T, parent_band_slot.T)
    tile = lax.axis_index("tile").astype(I32).reshape(1)
    face = lax.axis_index("face").astype(I32).reshape(1)
    asked, posn, weight, tile, face = lax.optimization_barrier((exchange(wanted), posn, weight, tile, face))
    outgoing, slots = pack(asked, bands)
    recv = exchange(outgoing.reshape(DEVICES, 2, M, LANES)).reshape(2 * DEVICES, M, LANES)
    field, turned, *messages = regrid(place, tile, face, recv, posn, weight, truth_field)
    rounds = [
        ("tile", [(i, i + 1) for i in range(1, tiles - 1, 2)]),
        ("tile", [(i, i + 1) for i in range(0, tiles - 1, 2)]),
        ("face", [(i, (i + 1) % faces) for i in range(1, faces, 2)]),
        ("face", [(i, i + 1) for i in range(0, faces, 2)]),
    ]
    messages = [lax.ppermute(m, axis, pairs + [(j, i) for i, j in pairs]) for m, (axis, pairs) in zip(messages, rounds)]
    turn, kept = inner(turned)
    back = push(place, tile, face, field, turned, turn, kept, posn, weight, *messages)
    back = exchange(back.reshape(DEVICES, MESSAGE, 1, LANES)).reshape(DEVICES * MESSAGE, LANES)
    return collect(slots, back).reshape(M, BANDS, LANES)


def solution(mesh):
    in_specs = (
        P(None, AXES, None),
        P(AXES, None),
        P(AXES, None),
        P(None, AXES, None),
        P(None, AXES, None),
        P("tile", "face"),
    )
    return jax.shard_map(local, mesh=mesh, in_specs=in_specs, out_specs=P(None, AXES, None), check_vma=False)
```

```python
import jax
import jax.numpy as jnp
from jax import lax
from jax.experimental import pallas as pl
from jax.experimental.pallas import tpu as pltpu
from jax.sharding import PartitionSpec as P

RANGE = 8
FLOOR = 0.01
M = 16
BANDS = 64
LANES = 128
ROWS = 32
EXT = ROWS + 2 * RANGE
DEVICES = 128
POINTS = 4
TABLE = BANDS + 1
GRAD = 2 * EXT + 1
QUADS = M // 4
MESSAGE = M + 1
TOP = 32700.0
F32 = jnp.float32
I32 = jnp.int32
BF16 = jnp.bfloat16
AXES = ("face", "tile")


def struct(shape, dtype=F32):
    return jax.ShapeDtypeStruct(shape, dtype)


def lane_ids(rows=8):
    return lax.broadcasted_iota(I32, (rows, LANES), 1)


def row_ids(rows=8):
    return lax.broadcasted_iota(I32, (rows, LANES), 0)


def request_kernel(holder_hbm, slot_hbm, wanted_ref, place_ref, holder_ref, slot_ref, sems):
    copies = [
        pltpu.make_async_copy(holder_hbm, holder_ref, sems.at[0]),
        pltpu.make_async_copy(slot_hbm, slot_ref, sems.at[1]),
    ]
    for copy in copies:
        copy.start()
    for copy in copies:
        copy.wait()
    owner = lax.broadcasted_iota(I32, (DEVICES, BANDS), 0).astype(F32)
    band = lax.broadcasted_iota(I32, (1, BANDS), 1)
    big = float(1 << 20)
    hots, codes = [], []
    for k in range(2):
        holder = holder_ref[k : k + 1, :].astype(F32)
        code = (band + k * BANDS) * BANDS + slot_ref[k : k + 1, :]
        hots.append(holder == owner)
        codes.append(jnp.broadcast_to(code.astype(F32), (DEVICES, BANDS)))
    low = [jnp.min(jnp.where(h, c, big), axis=1, keepdims=True) for h, c in zip(hots, codes)]
    high = [jnp.max(jnp.where(h, c, -1.0), axis=1, keepdims=True) for h, c in zip(hots, codes)]
    first = jnp.minimum(low[0], low[1])
    last = jnp.maximum(high[0], high[1])
    slots = [
        jnp.where(last >= 0.0, first.astype(I32) & (BANDS - 1), 0),
        jnp.where(last > first, last.astype(I32) & (BANDS - 1), 0),
    ]
    lanes = lane_ids(DEVICES)
    wanted_ref[...] = jnp.where(lanes == 0, slots[0], jnp.where(lanes == 1, slots[1], 0))
    place_ref[...] = jnp.zeros((8, LANES), I32)
    for k in range(2):
        spot = 2.0 * owner + jnp.where(codes[k] == first, 0.0, 1.0)
        spot = jnp.sum(jnp.where(hots[k], spot, 0.0), axis=0, keepdims=True)
        place_ref[k : k + 1, :BANDS] = spot.astype(I32)


def request(holder, slot):
    return pl.pallas_call(
        request_kernel,
        in_specs=[pl.BlockSpec(memory_space=pl.ANY)] * 2,
        out_shape=(struct((DEVICES, LANES), I32), struct((8, LANES), I32)),
        scratch_shapes=[pltpu.VMEM((2, BANDS), I32)] * 2 + [pltpu.SemaphoreType.DMA((2,))],
        name="request",
    )(holder, slot)


def pack_kernel(asked_ref, bands_ref, out_ref, slots_ref, smem, sem):
    table = jnp.transpose(asked_ref[...].astype(F32))[:8].astype(I32)
    slots_ref[...] = table
    copy = pltpu.make_async_copy(slots_ref, smem, sem)
    copy.start()
    copy.wait()

    def step(i, carry):
        for r in range(2):
            out_ref[2 * i + r] = bands_ref[smem[r, i]]
        return carry

    lax.fori_loop(0, DEVICES, step, 0, unroll=8)


def pack(asked, bands):
    return pl.pallas_call(
        pack_kernel,
        out_shape=(struct((2 * DEVICES, M, LANES), BF16), struct((8, LANES), I32)),
        scratch_shapes=[pltpu.SMEM((8, LANES), I32), pltpu.SemaphoreType.DMA],
        name="pack",
        compiler_params=pltpu.CompilerParams(vmem_limit_bytes=4 << 20),
    )(asked, bands)


def prepare_kernel(pos_ref, factor_ref, posn_ref, weight_ref):
    for half in range(2):
        factors = [factor_ref[pl.ds(j * BANDS + half, ROWS, stride=2), :] for j in range(POINTS)]
        total = factors[0] + factors[1] + factors[2] + factors[3]
        for j in range(POINTS):
            spot = j * BANDS + half * ROWS
            posn_ref[pl.ds(spot, ROWS), :] = pos_ref[pl.ds(j * BANDS + half, ROWS, stride=2), :]
            weight_ref[pl.ds(spot, ROWS), :] = factors[j] / total


def prepare(pos, factor):
    return pl.pallas_call(
        prepare_kernel,
        out_shape=(
            struct((POINTS * BANDS, LANES), I32),
            struct((POINTS * BANDS, LANES)),
        ),
        name="prepare",
        cost_estimate=pl.CostEstimate(flops=1 << 20, bytes_accessed=1 << 20, transcendentals=0),
        compiler_params=pltpu.CompilerParams(vmem_limit_bytes=2 << 20),
    )(pos, factor)


def regrid_kernel(
    place_ref, tile_ref, face_ref, recv_ref, posn_ref, weight_ref, truth_ref,
    field_ref, turned_ref, tall0_ref, tall1_ref, wide0_ref, wide1_ref,
    low_ref, high_ref,
):
    def spread(row, carry):
        for half in range(2):
            for k, tab in enumerate((low_ref, high_ref)):
                strip = recv_ref[place_ref[k, 2 * row + half]].astype(F32)
                tab[pl.ds(half * ROWS + row, M, stride=TABLE), :] = strip
        return carry

    lax.fori_loop(0, ROWS, spread, 0, unroll=8)

    def regrid(block, carry):
        row = pl.multiple_of(block * 8, 8)
        posn = [posn_ref[pl.ds(j * BANDS + row, 8), :] for j in range(POINTS)]
        weight = [weight_ref[pl.ds(j * BANDS + row, 8), :] for j in range(POINTS)]
        sums = [jnp.zeros((8, LANES), F32)] * M
        for j in range(POINTS):
            lane, upper = posn[j] & (LANES - 1), posn[j] >= LANES
            for m in range(M):
                a, b = [
                    jnp.take_along_axis(tab[pl.ds(m * TABLE + row, 8), :], lane, axis=1, mode="promise_in_bounds")
                    for tab in (low_ref, high_ref)
                ]
                sums[m] = sums[m] + weight[j] * jnp.where(upper, b, a)
        for m in range(M):
            field_ref[pl.ds(m * BANDS + row, 8), :] = sums[m]
        return carry

    lax.fori_loop(0, BANDS // 8, regrid, 0)

    for half in range(2):
        field_ref[pl.ds(M * BANDS + half * ROWS, ROWS), :] = truth_ref[:, half * LANES : (half + 1) * LANES]
    odd = tile_ref[0] & 1
    for m in range(M + 1):
        for half in range(2):
            spot = m * BANDS + half * ROWS
            for message, edge in ((tall0_ref, 1 - odd), (tall1_ref, odd)):
                rows = pl.ds(pl.multiple_of(spot + edge * (ROWS - 8), 8), 8)
                message[pl.ds((2 * m + half) * 8, 8), :] = field_ref[rows, :]
    for q in range(QUADS + 1):
        for half in range(2):
            if q < QUADS:
                parts = [field_ref[pl.ds((4 * q + i) * BANDS + half * ROWS, ROWS), :] for i in range(4)]
            else:
                parts = [truth_ref[:, half * LANES : (half + 1) * LANES]] * 4
            turned = jnp.transpose(jnp.concatenate(parts, axis=0))
            turned_ref[pl.ds(q * 2 * LANES + half * LANES, LANES), :] = turned
    odd = face_ref[0] & 1
    for q in range(QUADS + 1):
        for message, edge in ((wide0_ref, 1 - odd), (wide1_ref, odd)):
            columns = pl.ds(pl.multiple_of(q * 2 * LANES + edge * (2 * LANES - 8), 8), 8)
            message[pl.ds(q * 8, 8), :] = turned_ref[columns, :]


VMEM = pl.BlockSpec(memory_space=pltpu.VMEM)
SMEM = pl.BlockSpec(memory_space=pltpu.SMEM)


def regrid(place, tile, face, recv, posn, weight, truth):
    tall = struct(((M + 1) * 2 * RANGE, LANES))
    wide = struct(((QUADS + 1) * RANGE, LANES))
    return pl.pallas_call(
        regrid_kernel,
        in_specs=[SMEM] * 3 + [VMEM] * 4,
        out_shape=(
            struct(((M + 1) * BANDS, LANES)),
            struct(((QUADS + 1) * 2 * LANES, LANES)),
            tall, tall, wide, wide,
        ),
        scratch_shapes=[pltpu.VMEM((M * TABLE, LANES), F32)] * 2,
        name="regrid",
        compiler_params=pltpu.CompilerParams(vmem_limit_bytes=8 << 20),
    )(place, tile, face, recv, posn, weight, truth)


def steep(diff):
    root = lax.rsqrt(diff * diff + FLOOR)
    value = lax.rsqrt(root)
    return value, (diff * root) * (value * root)


def column_pushes(rows):
    totals, slopes, sights = [], [], []
    for k in range(1, RANGE + 1):
        pairs = [steep(rows(q, 0) - rows(q, k)) for q in range(QUADS)]
        slopes.append([p[1] for p in pairs])
        totals.append((pairs[0][0] + pairs[1][0]) + (pairs[2][0] + pairs[3][0]))
        sights.append(steep(rows(QUADS, 0) - rows(QUADS, k))[0])
    totals = [t + pltpu.roll(t, 2 * ROWS, 1) for t in totals]
    totals = [t + pltpu.roll(t, ROWS, 1) for t in totals]
    pushes = []
    for k in range(1, RANGE + 1):
        push = (1.0 / (k * M)) * (sights[k - 1] - totals[k - 1] * (1.0 / M))
        pushes.append([push * slope for slope in slopes[k - 1]])
    return pushes


def ending(kept, spot, pushed, k):
    moved = pltpu.roll(pushed, k % 8, 0)
    earlier = kept[spot]
    kept[spot] = moved
    return jnp.where(row_ids() >= k, moved, earlier)


def column_sums(kept, rows):
    sums = [jnp.zeros((8, LANES), F32)] * QUADS
    for k, pushes in enumerate(column_pushes(rows), 1):
        for q in range(QUADS):
            sums[q] = sums[q] - pushes[q] + ending(kept, (k - 1) * QUADS + q, pushes[q], k)
    return sums


WIDTH = 2 * LANES
INNER = WIDTH - 2 * RANGE


def inner_kernel(turned_ref, turn_ref, kept_ref):
    kept_ref[...] = jnp.zeros_like(kept_ref)

    def block(b, carry):
        base = pl.multiple_of(b * 8, 8)
        sums = column_sums(kept_ref, lambda q, k: turned_ref[pl.ds(base + (q * WIDTH + k), 8), :])
        for q in range(QUADS):
            turn_ref[pl.ds(base + q * WIDTH, 8), :] = sums[q]
        return carry

    lax.fori_loop(0, INNER // 8, block, 0, unroll=3)


def inner(turned):
    return pl.pallas_call(
        inner_kernel,
        out_shape=(struct((QUADS * WIDTH, LANES)), struct((RANGE * QUADS, 8, LANES))),
        name="inner",
        cost_estimate=pl.CostEstimate(flops=16 << 20, bytes_accessed=12 << 20, transcendentals=2 << 20),
        compiler_params=pltpu.CompilerParams(vmem_limit_bytes=2 << 20),
    )(turned)


def push_kernel(
    place_ref, tile_ref, face_ref, field_ref, turned_ref, turn_ref, kept_ref, posn_ref, weight_ref,
    tall0_ref, tall1_ref, wide0_ref, wide1_ref,
    out_ref, ext, grad, west, east, kept_columns, kept_rows,
):
    odd = tile_ref[0] & 1
    for mh in range(2 * (M + 1)):
        for message, below in ((tall0_ref, 1 - odd), (tall1_ref, odd)):
            rows = pl.ds(pl.multiple_of(mh * EXT + below * (ROWS + 8), 8), 8)
            ext[rows, :] = message[pl.ds(mh * 8, 8), :]
        ext[pl.ds(mh * EXT + 8, ROWS), :] = field_ref[pl.ds(mh * ROWS, ROWS), :]
    even = jnp.full((8, LANES), face_ref[0] & 1, I32) == 0
    for q in range(QUADS + 1):
        ones, twos = wide0_ref[pl.ds(q * 8, 8), :], wide1_ref[pl.ds(q * 8, 8), :]
        west[pl.ds(q * 16, 8), :] = jnp.where(even, twos, ones)
        west[pl.ds(q * 16 + 8, 8), :] = turned_ref[pl.ds(q * WIDTH, 8), :]
        east[pl.ds(q * 24, 16), :] = turned_ref[pl.ds(q * WIDTH + INNER, 16), :]
        east[pl.ds(q * 24 + 16, 8), :] = jnp.where(even, ones, twos)
    out_ref[...] = jnp.zeros_like(out_ref)
    first_row = tile_ref[0] * ROWS - RANGE

    def latitude(step, carry):
        half = step // 5
        block = step % 5
        base = pl.multiple_of(half * EXT + block * 8, 8)
        rows = row_ids() + (first_row + block * 8)
        sums = [jnp.zeros((8, LANES), F32)] * M
        for k in range(1, RANGE + 1):
            def diff(m):
                here = base + m * 2 * EXT
                return ext[pl.ds(here, 8), :] - ext[pl.ds(here + k, 8), :]

            total = jnp.zeros((8, LANES), F32)
            slopes = []
            for m in range(M):
                value, slope = steep(diff(m))
                total = total + value
                slopes.append(slope)
            seen, unused = steep(diff(M))
            inside = (rows >= 0) & (rows + k < ROWS * 32)
            push = jnp.where(inside, (1.0 / (k * M)) * (seen - total * (1.0 / M)), 0.0)
            for m in range(M):
                pushed = push * slopes[m]
                sums[m] = sums[m] - pushed + ending(kept_rows, (k - 1) * M + m, pushed, k)
        for m in range(M):
            grad[pl.ds(base + m * GRAD, 8), :] = sums[m]
        return carry

    lax.fori_loop(0, 10, latitude, 0, unroll=2)

    added = [jnp.zeros((8, LANES), F32)] * QUADS
    for k, pushes in enumerate(column_pushes(lambda q, k: west[pl.ds(q * 16 + k, 8), :]), 1):
        for q in range(QUADS):
            added[q] = added[q] + jnp.where(row_ids() < k, pltpu.roll(pushes[q], k % 8, 0), 0.0)
    kept_columns[...] = kept_ref[...]
    near = column_sums(kept_columns, lambda q, k: east[pl.ds(q * 24 + k, 8), :])
    last = column_sums(kept_columns, lambda q, k: east[pl.ds(q * 24 + 8 + k, 8), :])

    for q in range(QUADS):
        first = turn_ref[pl.ds(q * WIDTH, 8), :] + added[q]
        halves = [
            jnp.concatenate([first, turn_ref[pl.ds(q * WIDTH + 8, LANES - 8), :]], axis=0),
            jnp.concatenate([turn_ref[pl.ds(q * WIDTH + LANES, INNER - LANES), :], near[q], last[q]], axis=0),
        ]
        for half in range(2):
            back = jnp.transpose(halves[half])
            for i in range(4):
                spot = (4 * q + i) * GRAD + half * EXT + 8
                grad[pl.ds(spot, ROWS), :] += back[i * ROWS : (i + 1) * ROWS]

    cells = [(lax.broadcasted_iota(I32, (16, LANES), 0) + 16 * i).astype(F32).astype(BF16) for i in range(16)]
    one, zero = jnp.ones((16, LANES), BF16), jnp.zeros((16, LANES), BF16)

    def adjoint(row, carry):
        for half in range(2):
            tile = grad[pl.ds(half * EXT + 8 + row, M, stride=GRAD), :]
            parts, hots = [], []
            for j in range(POINTS):
                spot = j * BANDS + half * ROWS + row
                parts.append(tile * weight_ref[pl.ds(spot, 1), :])
                posn = jnp.broadcast_to(posn_ref[pl.ds(spot, 1), :].astype(F32), (16, LANES)).astype(BF16)
                hots.append(jnp.concatenate([jnp.where(c == posn, one, zero) for c in cells], axis=0))
            part = jnp.concatenate(parts, axis=1)
            high = part.astype(BF16)
            low = (part - high.astype(F32)).astype(BF16)
            both = lax.dot_general(
                jnp.concatenate([high, low], axis=0),
                jnp.concatenate(hots, axis=1),
                (((1,), (1,)), ((), ())),
                preferred_element_type=F32,
            )
            both = both[:M] + both[M:]
            for k in range(2):
                strip = both[:, k * LANES : (k + 1) * LANES]
                largest = jnp.maximum(jnp.max(jnp.abs(strip), axis=0, keepdims=True), 1e-36)
                scale = jnp.ceil(jnp.log2(largest) * 256.0)
                code = jnp.round(strip * (jnp.exp2(scale * (-1.0 / 256.0)) * TOP)).astype(I32)
                place = place_ref[k, 2 * row + half]
                spot = (place >> 1) * MESSAGE
                shift = (place & 1) * 16
                out_ref[pl.ds(spot, M), :] |= (code & 0xFFFF) << shift
                out_ref[pl.ds(spot + M, 1), :] |= (scale.astype(I32) & 0xFFFF) << shift
        return carry

    lax.fori_loop(0, ROWS, adjoint, 0, unroll=8)


def push(place, tile, face, *arrays):
    return pl.pallas_call(
        push_kernel,
        in_specs=[SMEM] * 3 + [VMEM] * len(arrays),
        out_shape=struct((DEVICES * MESSAGE, LANES), I32),
        scratch_shapes=[
            pltpu.VMEM((2 * (M + 1) * EXT, LANES), F32),
            pltpu.VMEM((M * GRAD, LANES), F32),
            pltpu.VMEM(((QUADS + 1) * 16, LANES), F32),
            pltpu.VMEM(((QUADS + 1) * 24, LANES), F32),
            pltpu.VMEM((RANGE * QUADS, 8, LANES), F32),
            pltpu.VMEM((RANGE * M, 8, LANES), F32),
        ],
        name="push",
        compiler_params=pltpu.CompilerParams(vmem_limit_bytes=6 << 20),
    )(place, tile, face, *arrays)


def collect_kernel(slots_ref, back_ref, out_ref, *sums):
    for part in sums:
        part[...] = jnp.zeros_like(part)

    def step(i, carry):
        codes = back_ref[pl.ds(i * MESSAGE, M), :]
        scales = back_ref[pl.ds(i * MESSAGE + M, 1), :]
        for r in range(2):
            code, scale = [((x << 16) if r == 0 else x) >> 16 for x in (codes, scales)]
            scale = jnp.exp2(scale.astype(F32) * (1.0 / 256.0)) * (1.0 / TOP)
            sums[r][pl.ds(slots_ref[r, i] * MESSAGE, M), :] += code.astype(F32) * scale
        return carry

    lax.fori_loop(0, DEVICES, step, 0, unroll=8)

    def turn(block, carry):
        for m in range(M):
            where = pl.ds(block * 8 * MESSAGE + m, 8, stride=MESSAGE)
            out_ref[pl.ds(pl.multiple_of(m * BANDS + block * 8, 8), 8), :] = sums[0][where, :] + sums[1][where, :]
        return carry

    lax.fori_loop(0, BANDS // 8, turn, 0)


def collect(slots, back):
    return pl.pallas_call(
        collect_kernel,
        in_specs=[SMEM, VMEM],
        out_shape=struct((M * BANDS, LANES)),
        scratch_shapes=[pltpu.VMEM((BANDS * MESSAGE, LANES), F32)] * 2,
        name="collect",
        compiler_params=pltpu.CompilerParams(vmem_limit_bytes=5 << 20),
    )(slots, back)


def exchange(x):
    return lax.all_to_all(x, AXES, split_axis=0, concat_axis=0, tiled=True)


def local(predicted_field, parent_band_holder, parent_band_slot, neighbour_positions, unscaled_neighbour_factor, truth_field):
    tiles, faces = lax.axis_size("tile"), lax.axis_size("face")
    bands = jnp.transpose(predicted_field, (1, 0, 2))
    posn, weight = prepare(
        neighbour_positions.reshape(POINTS * BANDS, LANES),
        unscaled_neighbour_factor.reshape(POINTS * BANDS, LANES),
    )
    wanted, place = request(parent_band_holder.T, parent_band_slot.T)
    tile = lax.axis_index("tile").astype(I32).reshape(1)
    face = lax.axis_index("face").astype(I32).reshape(1)
    asked, posn, weight, tile, face = lax.optimization_barrier((exchange(wanted), posn, weight, tile, face))
    outgoing, slots = pack(asked, bands)
    recv = exchange(outgoing.reshape(DEVICES, 2, M, LANES)).reshape(2 * DEVICES, M, LANES)
    field, turned, *messages = regrid(place, tile, face, recv, posn, weight, truth_field)
    rounds = [
        ("tile", [(i, i + 1) for i in range(0, tiles - 1, 2)]),
        ("tile", [(i, i + 1) for i in range(1, tiles - 1, 2)]),
        ("face", [(i, i + 1) for i in range(0, faces, 2)]),
        ("face", [(i, (i + 1) % faces) for i in range(1, faces, 2)]),
    ]
    messages = [lax.ppermute(m, axis, pairs + [(j, i) for i, j in pairs]) for m, (axis, pairs) in zip(messages, rounds)]
    turn, kept = inner(turned)
    back = push(place, tile, face, field, turned, turn, kept, posn, weight, *messages)
    back = exchange(back.reshape(DEVICES, MESSAGE, 1, LANES)).reshape(DEVICES * MESSAGE, LANES)
    return collect(slots, back).reshape(M, BANDS, LANES)


def solution(mesh):
    in_specs = (
        P(None, AXES, None),
        P(AXES, None),
        P(AXES, None),
        P(None, AXES, None),
        P(None, AXES, None),
        P("tile", "face"),
    )
    return jax.shard_map(local, mesh=mesh, in_specs=in_specs, out_specs=P(None, AXES, None), check_vma=False)
```
